32 devices in a mesh: dp: 16 (over z, x, core), mp: 2 (over y).
Axes of the slice: x: 2, y: 2, z: 4, core: 2. Of those that a mesh axis runs over, the one named last changes fastest.
Arguments:
- tokens_in: bfloat16 [32768, 1024], P(('dp', 'mp')), may hold values from -6 to 6
- timesteps: int32 [16], P('dp'), may hold values from 0 to 4999
- segment_ids: int32 [16, 2048], P('dp'), may hold values from 0 to 7, never falling along the last dimension, each value on 1 to 512 neighbouring positions
- padding: int32 [16, 2048], P('dp'), may hold values 0 or 1
- qkv_weight: bfloat16 [3, 1024, 1024], P(None, None, 'mp'), may hold values from -0.1875 to 0.1875
- head_bias: float32 [2, 1024], P(None, 'mp'), may hold values from -1.5 to 1.5
- out_weight: bfloat16 [1024, 1024], P('mp'), may hold values from -0.75 to 0.75
- up_weight: bfloat16 [1024, 4096], P(None, 'mp'), may hold values from -0.1875 to 0.1875
- up_bias: float32 [4096], P('mp'), may hold values from -1.5 to 1.5
- down_weight: bfloat16 [4096, 1024], P('mp'), may hold values from -0.09375 to 0.09375
- vectors: float32 [6, 1024], replicated, may hold values from -1.5 to 1.5, as said below
- cotangent: bfloat16 [32768, 1024], P(('dp', 'mp')), may hold values from -6 to 6
Outputs:
- output: bfloat16 [32768, 1024], P(('dp', 'mp'))
- grad_input: bfloat16 [32768, 1024], P(('dp', 'mp'))
- grad_qkv: float32 [3, 1024, 1024], P(None, 'dp', 'mp')
- grad_head_bias: float32 [2, 1024], P(None, 'mp')
- grad_out_weight: float32 [1024, 1024], P('mp', 'dp')
- grad_up_weight: float32 [1024, 4096], P('dp', 'mp')
- grad_up_bias: float32 [4096], P('mp')
- grad_down_weight: float32 [4096, 1024], P('mp', 'dp')
- grad_vectors: float32 [6, 1024], replicated
The draws below stay inside these ranges and needn't reach their ends.
Inputs may be any that keep to these rules, and one draw needn't show every extreme that they name: `segment_ids`: along a sequence the document numbers never fall; each document has 1 to 512 tokens, one exactly 512. `vectors`: rows 0 and 2 lie in 0.5 to 1.5.
All inputs are finite; a program needn't handle non-finite values. No bound on the sum of `padding` on one device may be relied on, other than what follows from the above.
Results may differ from the reference program's by a relative error of at most 0.023.
Values may be sent and summed in bfloat16 or wider, within the bound.
No kernel may reach another device: no remote copies, remote signals or barrier semaphores. Data moves between devices by JAX's collectives and lax.ppermute only.
A program may use at most 256 MiB of HBM per device.

```python
import math
import jax
import jax.numpy as jnp
import numpy as np
from jax import lax

D = 1024
HEADS = 16
FF = 4096
HEAD_DIM = 64
SEQ = 2048
BLOCK = 512
DOCS = 8
MAXDOC = 512
TSTEPS = 5000
SEQS = 16
TOKENS = 32768


def draw_vectors(key, part):
    base_rows = jnp.clip(jax.random.normal(key, (6, D), jnp.float32) * 0.3, -1.5, 1.5)
    gain_rows = jax.random.uniform(jax.random.fold_in(key, 7), (6, D), jnp.float32, 0.5, 1.5)
    row_ids = jnp.arange(6, dtype=jnp.int32)[:, None]
    chosen = (row_ids == 0) | (row_ids == 2)
    return jnp.where(chosen, gain_rows, base_rows)


def set_ends(array, stream_key, smallest, top_value):
    longest = array.shape.index(max(array.shape))
    spots = []
    for shift in (0, 1):
        where = [jax.random.randint(jax.random.fold_in(stream_key, axis), (), 0, length) for axis, length in enumerate(array.shape)]
        where[longest] = (where[longest] + shift) % array.shape[longest]
        spots.append(tuple(where))
    return array.at[spots[0]].set(smallest).at[spots[1]].set(top_value)


def shard_levels(own_key, extent, shards, smallest, high):
    factor_of, own = 1.0, jax.random.fold_in(own_key, 6)
    for dim, shards_of in shards:
        heights = jnp.exp(jax.random.uniform(jax.random.fold_in(own, dim), (shards_of,), jnp.float32, smallest / len(shards), high / len(shards)))
        factor_of = factor_of * jnp.repeat(heights, extent[dim] // shards_of).reshape([-1 if axis == dim else 1 for axis in range(len(extent))])
    return factor_of


def profile(number_of, total, reach, skew):
    loads = [(1 << 20) // math.isqrt(rank ** skew) + 1 for rank in range(2, number_of + 1)]
    spare, holding = total - reach - (number_of - 1), [1] * (number_of - 1)
    while spare > 0:
        candidates = [i for i in range(number_of - 1) if holding[i] < reach]
        pool, budget = sum([loads[i] for i in candidates]), spare
        for i in candidates:
            extra = min(reach - holding[i], max(1, budget * loads[i] // pool), spare)
            holding[i] = holding[i] + extra
            spare = spare - extra
    return np.array([reach] + holding)


def ragged_sizes(key, count, total, reach, lean):
    if count == 2:
        one = jax.random.randint(key, (), max(1, total - reach), min(reach, total - 1) + 1)
        return jnp.stack([one, total - one])
    sizes = jnp.asarray(profile(count, total, reach, lean), jnp.int32)
    twos = (count - 1) // 2
    source_of, taker = sizes[1:1 + 2 * twos:2], sizes[2:2 + 2 * twos:2]
    room = jnp.minimum(source_of - 1, reach - taker)
    moved = jax.random.randint(jax.random.fold_in(key, 1), (twos,), 0, 1 << 20) % (room + 1)
    sizes = sizes.at[1:1 + 2 * twos:2].set(source_of - moved).at[2:2 + 2 * twos:2].set(taker + moved)
    return sizes[jax.random.permutation(jax.random.fold_in(key, 2), count)]


def gaussian(own_key, extent, deviation, reach, split=(), kind=jnp.bfloat16):
    entries = deviation * jax.random.normal(own_key, extent, jnp.float32)
    if split:
        entries = entries * shard_levels(own_key, extent, split, -0.22, 0.18)
    return jnp.clip(entries, -reach, reach).astype(kind)


def setup_inputs(seed: int = 0) -> dict:
    splits = jax.random.split(jax.random.key(seed), 13)
    tokens_in = gaussian(splits[0], (TOKENS, D), 1.0, 6.0, ((0, 32),))
    timesteps = set_ends(jax.random.randint(splits[1], (SEQS,), 0, TSTEPS), jax.random.fold_in(splits[1], 1), 0, TSTEPS - 1).astype(jnp.int32)
    segment_ids = jax.vmap(lambda own: jnp.searchsorted(jnp.cumsum(ragged_sizes(own, DOCS, SEQ, MAXDOC, 2)), jnp.arange(SEQ), side="right"))(jax.random.split(splits[2], SEQS)).reshape((SEQS, SEQ)).astype(jnp.int32)
    padding = set_ends((jax.random.randint(splits[3], (SEQS, SEQ), 0, 8) < 1).astype(jnp.int32), jax.random.fold_in(splits[3], 1), 0, 1)
    qkv_weight = gaussian(splits[4], (3, D, D), D ** -0.5, 0.1875, ((2, 2),))
    head_bias = gaussian(splits[5], (2, D), 0.3, 1.5, ((1, 2),), jnp.float32)
    out_weight = gaussian(splits[6], (D, D), (D // 16) ** -0.5, 0.75, ((0, 2),))
    up_weight = gaussian(splits[7], (D, FF), D ** -0.5, 0.1875, ((1, 2),))
    up_bias = gaussian(splits[8], (FF,), 0.3, 1.5, ((0, 2),), jnp.float32)
    down_weight = gaussian(splits[9], (FF, D), FF ** -0.5, 0.09375, ((0, 2),))
    vectors = draw_vectors(jax.random.fold_in(splits[12], 71), 0)
    cotangent = gaussian(splits[11], (TOKENS, D), 1.0, 6.0, ((0, 32),))
    return dict(tokens_in=tokens_in, timesteps=timesteps, segment_ids=segment_ids, padding=padding, qkv_weight=qkv_weight, head_bias=head_bias, out_weight=out_weight, up_weight=up_weight, up_bias=up_bias, down_weight=down_weight, vectors=vectors, cotangent=cotangent)


@jax.custom_vjp
def low(v):
    return lax.optimization_barrier(v.astype(jnp.bfloat16)).astype(jnp.float32)

@jax.custom_vjp
def low_back(v):
    return v

def low_keep(v):
    return (low(v), None)

def low_pass(kept, grad):
    return (grad,)

def back_keep(v):
    return (v, None)

def back_low(kept, grad):
    return (low(grad),)
low.defvjp(low_keep, low_pass)
low_back.defvjp(back_keep, back_low)
PRECISE = lax.Precision.HIGHEST
NEG_FILL = -1e+30

def layer_norm(resid, gain_vec, bias_vec):
    row_mean = lax.optimization_barrier(jnp.mean(resid, axis=-1, keepdims=True))
    centered = resid - row_mean
    variance = lax.optimization_barrier(jnp.mean(centered * centered, axis=-1, keepdims=True))
    return centered * lax.rsqrt(variance + 1e-05) * gain_vec + bias_vec

def time_embed(step_vals, model_width):
    half_width = model_width // 2
    frequency = jnp.exp(-math.log(10000.0) * jnp.arange(half_width, dtype=jnp.float32) / half_width)
    angles = step_vals[:, None] * frequency[None, :]
    return jnp.concatenate([jnp.sin(angles), jnp.cos(angles)], axis=-1)

def allowed_mask(seg_query, seg_all, pad_all, row_start):
    query_pos = row_start + jnp.arange(seg_query.shape[0], dtype=jnp.int32)
    key_pos = jnp.arange(seg_all.shape[0], dtype=jnp.int32)
    same_doc = seg_query[:, None] == seg_all[None, :]
    live_key = (pad_all[None, :] == 0) | (query_pos[:, None] == key_pos[None, :])
    return same_doc & live_key

def attend_block(queries, key_rows, value_rows, seg_all, pad_all, seg_query, row_start):
    scores = low_back(jnp.einsum('qhd,khd->hqk', queries, key_rows, precision=PRECISE) * 0.125)
    scores = jnp.where(allowed_mask(seg_query, seg_all, pad_all, row_start)[None], scores, NEG_FILL)
    row_max = lax.optimization_barrier(jnp.max(scores, axis=-1, keepdims=True))
    exp_scores = jnp.exp(scores - row_max)
    attn_probs = exp_scores / lax.optimization_barrier(jnp.sum(exp_scores, axis=-1, keepdims=True))
    return jnp.einsum('hqk,khd->qhd', low(attn_probs), value_rows, precision=PRECISE)

def forward(weights, seq_rows, step_vals, seg_ids, pad_mask):
    qkv_w, head_b, out_w, up_w, up_b, down_w, vec_rows = weights
    inputs = seq_rows + time_embed(step_vals, D)
    inputs_low = low(inputs)
    projected = jnp.einsum('nd,cde->cne', inputs_low, qkv_w, precision=PRECISE)
    queries = low(low_back(projected[0] + head_b[0])).reshape(SEQ, HEADS, HEAD_DIM)
    key_rows = low(low_back(projected[1])).reshape(SEQ, HEADS, HEAD_DIM)
    value_rows = low(low_back(projected[2] + head_b[1])).reshape(SEQ, HEADS, HEAD_DIM)
    num_blocks = SEQ // BLOCK
    query_blocks = queries.reshape(num_blocks, BLOCK, HEADS, HEAD_DIM)
    seg_blocks = seg_ids.reshape(num_blocks, BLOCK)
    block_starts = (jnp.arange(num_blocks, dtype=jnp.int32) * BLOCK).astype(jnp.int32)

    def block_fn(item_parts):
        return attend_block(item_parts[0], key_rows, value_rows, seg_ids, pad_mask, item_parts[1], item_parts[2])
    mixed = lax.map(jax.checkpoint(block_fn), (query_blocks, seg_blocks, block_starts)).reshape(SEQ, D)
    mixed = low(low_back(mixed))
    attn_branch = low_back(jnp.dot(mixed, out_w, precision=PRECISE) + vec_rows[4])
    normed = layer_norm(inputs + attn_branch, vec_rows[0], vec_rows[1])
    up_pre = low_back(jnp.dot(low(normed), up_w, precision=PRECISE) + up_b)
    activated = low(jax.nn.gelu(up_pre, approximate=False))
    ffn_branch = low_back(jnp.dot(activated, down_w, precision=PRECISE) + vec_rows[5])
    return layer_norm(normed + ffn_branch, vec_rows[2], vec_rows[3])

def reference(tokens_in, timesteps, segment_ids, padding, qkv_weight, head_bias, out_weight, up_weight, up_bias, down_weight, vectors, cotangent):
    weights = (qkv_weight.astype(jnp.float32), head_bias.astype(jnp.float32), out_weight.astype(jnp.float32), up_weight.astype(jnp.float32), up_bias.astype(jnp.float32), down_weight.astype(jnp.float32), vectors.astype(jnp.float32))
    seq_inputs = tokens_in.astype(jnp.float32).reshape(SEQS, SEQ, D)
    seq_cotan = cotangent.astype(jnp.float32).reshape(SEQS, SEQ, D)

    def one_seq(carried, item_parts):
        seq_rows, cotan_rows, step_id, seg_ids, pad_mask = item_parts
        step_vals = step_id.astype(jnp.float32) * jnp.ones((SEQ,), jnp.float32)

        def run_layer(weight_set, rows_in):
            return forward(weight_set, rows_in, step_vals, seg_ids, pad_mask)
        outputs_seq, pullback = jax.vjp(run_layer, weights, seq_rows)
        grad_weights, grad_rows = pullback(cotan_rows)
        carried = jax.tree.map(lambda left, right: left + right, carried, grad_weights)
        return (carried, (outputs_seq.astype(jnp.bfloat16), grad_rows.astype(jnp.bfloat16)))
    zero_grads = jax.tree.map(jnp.zeros_like, weights)
    gradients, (outputs_all, grads_all) = lax.scan(one_seq, zero_grads, (seq_inputs, seq_cotan, timesteps, segment_ids, padding))
    return (outputs_all.reshape(TOKENS, D), grads_all.reshape(TOKENS, D), gradients[0], gradients[1], gradients[2], gradients[3], gradients[4], gradients[5], gradients[6])
```

```python
from functools import partial
import math

import jax
import jax.numpy as jnp
from jax import lax
from jax.experimental import pallas as pl
from jax.experimental.pallas import tpu as pltpu
from jax.sharding import PartitionSpec as P

HEAD_DIM = 64
SEQ = 2048
MAXDOC = 512
BQ = 256
BK = 256
RB = 256
HB = 512
NEG_FILL = -1e30
F32 = jnp.float32
BF16 = jnp.bfloat16


def nt(a, b):
    return lax.dot_general(a, b, (((1,), (1,)), ((), ())), preferred_element_type=F32)


def nn(a, b):
    return lax.dot_general(a, b, (((1,), (0,)), ((), ())), preferred_element_type=F32)


def tn(a, b):
    return lax.dot_general(a, b, (((0,), (0,)), ((), ())), preferred_element_type=F32)


def cost(flops, nbytes, trans=0):
    return pl.CostEstimate(flops=int(flops), bytes_accessed=int(nbytes), transcendentals=int(trans))


def whole(shape):
    return pl.BlockSpec(shape, lambda *_: (0,) * len(shape))


def sds(shape, dtype):
    return jax.ShapeDtypeStruct(shape, dtype)


def qkv_own_kernel(tok_ref, emb_ref, w_ref, hb_ref, x_ref, q_ref, k_ref, v_ref):
    x = (tok_ref[...].astype(F32) + emb_ref[...]).astype(BF16)
    x_ref[...] = x
    q_ref[...] = (nn(x, w_ref[0]) + hb_ref[0:1]).astype(BF16)
    k_ref[...] = nn(x, w_ref[1]).astype(BF16)
    v_ref[...] = (nn(x, w_ref[2]) + hb_ref[1:2]).astype(BF16)


def qkv_own(tok, emb, w, hb, keys):
    rows, d = tok.shape
    width = w.shape[2]
    row = lambda n: pl.BlockSpec((RB, n), lambda i: (i, 0))
    return pl.pallas_call(
        qkv_own_kernel,
        grid=(rows // RB,),
        in_specs=[row(d), whole((1, d)), whole(w.shape), whole(hb.shape)],
        out_specs=[row(d), row(width), row(width), row(width)],
        out_shape=[
            sds((rows, d), BF16),
            sds((rows, width), BF16),
            sds((keys, width), BF16),
            sds((keys, width), BF16),
        ],
        cost_estimate=cost(6 * rows * d * width, 2 * (2 * rows * d + 3 * rows * width + 3 * d * width)),
        name="qkv_own",
    )(tok, emb, w, hb)


def kv_halo_kernel(tok_ref, emb_ref, w_ref, hb_ref, k_in, v_in, x_ref, k_ref, v_ref):
    x = (tok_ref[...].astype(F32) + emb_ref[...]).astype(BF16)
    x_ref[...] = x
    k_ref[...] = nn(x, w_ref[1]).astype(BF16)
    v_ref[...] = (nn(x, w_ref[2]) + hb_ref[1:2]).astype(BF16)


def kv_halo(tok, emb, w, hb, k, v):
    rows, d = tok.shape
    width = w.shape[2]
    base = (k.shape[0] - rows) // RB
    row = lambda n: pl.BlockSpec((RB, n), lambda i: (i, 0))
    low = pl.BlockSpec((RB, width), lambda i: (i + base, 0))
    anyspec = pl.BlockSpec(memory_space=pl.ANY)
    return pl.pallas_call(
        kv_halo_kernel,
        grid=(rows // RB,),
        in_specs=[row(d), whole((1, d)), whole(w.shape), whole(hb.shape), anyspec, anyspec],
        out_specs=[row(d), low, low],
        out_shape=[sds((rows, d), BF16), sds(k.shape, BF16), sds(v.shape, BF16)],
        input_output_aliases={4: 1, 5: 2},
        cost_estimate=cost(4 * rows * d * width, 2 * (2 * rows * d + 2 * rows * width + 3 * d * width)),
        name="kv_halo",
    )(tok, emb, w, hb, k, v)


def pair_stack(x2):
    lane = lax.broadcasted_iota(jnp.int32, (1, 128), 1)
    first = (lane < HEAD_DIM).astype(F32).astype(BF16)
    second = (lane >= HEAD_DIM).astype(F32).astype(BF16)
    return jnp.concatenate([x2 * first, x2 * second], axis=0)


def pair_merge(x):
    half = x.shape[0] // 2
    lane = lax.broadcasted_iota(jnp.int32, (half, 128), 1)
    return jnp.where(lane < HEAD_DIM, x[:half], x[half:])


def attn_fwd_kernel(nkb, pairs, cnt_ref, list_ref, q_ref, k_ref, v_ref, segq_ref, codek_ref,
                    o_ref, lse_ref, qs_scr, s_scr, m_scr, l_scr, acc_scr):
    qb = pl.program_id(1)
    count = cnt_ref[qb]
    for p in range(pairs):
        qs_scr[p] = pair_stack(q_ref[:, 128 * p:128 * (p + 1)] * jnp.asarray(0.125, BF16))
    m_scr[...] = jnp.full(m_scr.shape, -3e38, F32)
    l_scr[...] = jnp.zeros(l_scr.shape, F32)
    acc_scr[...] = jnp.zeros(acc_scr.shape, F32)

    def scores(s, carry):
        kb = list_ref[qb * nkb + s]
        off = pl.multiple_of(kb * BK, BK)
        qpos = qb * BQ + lax.broadcasted_iota(jnp.int32, (BQ, BK), 0)
        kpos = kb * BK + lax.broadcasted_iota(jnp.int32, (BQ, BK), 1)
        live = (segq_ref[...] == codek_ref[:, pl.ds(off, BK)]) | (qpos == kpos)
        bias = jnp.where(live, 0.0, NEG_FILL).astype(F32)
        bias = jnp.concatenate([bias, bias], axis=0)
        for p in range(pairs):
            sc = nt(qs_scr[p], k_ref[pl.ds(off, BK), 128 * p:128 * (p + 1)]) + bias
            s_scr[s, p] = sc
            top = jnp.maximum(sc[:, :128], sc[:, 128:])
            m_scr[p] = jnp.maximum(m_scr[p], top)
        return carry

    lax.fori_loop(0, count, scores, 0)
    for p in range(pairs):
        m_scr[p] = jnp.broadcast_to(jnp.max(m_scr[p], axis=1, keepdims=True), m_scr[p].shape)

    def weigh(s, carry):
        kb = list_ref[qb * nkb + s]
        off = pl.multiple_of(kb * BK, BK)
        for p in range(pairs):
            m = m_scr[p]
            e = jnp.exp(s_scr[s, p] - jnp.concatenate([m, m], axis=1))
            l_scr[p] = l_scr[p] + (e[:, :128] + e[:, 128:])
            acc_scr[p] = acc_scr[p] + nn(e.astype(BF16), v_ref[pl.ds(off, BK), 128 * p:128 * (p + 1)])
        return carry

    lax.fori_loop(0, count, weigh, 0)
    lane = lax.broadcasted_iota(jnp.int32, (BQ, 128), 1)
    lse_all = jnp.zeros((BQ, 128), F32)
    for p in range(pairs):
        total = jnp.sum(l_scr[p], axis=1, keepdims=True)
        o_ref[:, 128 * p:128 * (p + 1)] = pair_merge(acc_scr[p] / total).astype(BF16)
        lse = m_scr[p][:, :1] + jnp.log(total)
        lse_all = jnp.where(lane == 2 * p, lse[:BQ], lse_all)
        lse_all = jnp.where(lane == 2 * p + 1, lse[BQ:], lse_all)
    lse_ref[...] = lse_all


GROUP = 512


def attn_fwd(cnt, lst, q, k, v, segq, codek):
    rows, width = q.shape
    keys = k.shape[0]
    nqb, nkb = rows // BQ, keys // BK
    groups, pairs = width // GROUP, GROUP // 128
    est = rows * 2 * BK * width
    return pl.pallas_call(
        partial(attn_fwd_kernel, nkb, pairs),
        grid_spec=pltpu.PrefetchScalarGridSpec(
            num_scalar_prefetch=2,
            grid=(groups, nqb),
            in_specs=[
                pl.BlockSpec((BQ, GROUP), lambda g, i, *_: (i, g)),
                pl.BlockSpec((keys, GROUP), lambda g, i, *_: (0, g)),
                pl.BlockSpec((keys, GROUP), lambda g, i, *_: (0, g)),
                pl.BlockSpec((BQ, 1), lambda g, i, *_: (i, 0)),
                pl.BlockSpec((1, keys), lambda g, i, *_: (0, 0)),
            ],
            out_specs=[
                pl.BlockSpec((BQ, GROUP), lambda g, i, *_: (i, g)),
                pl.BlockSpec((BQ, 128), lambda g, i, *_: (i, g)),
            ],
            scratch_shapes=[
                pltpu.VMEM((pairs, 2 * BQ, 128), BF16),
                pltpu.VMEM((nkb, pairs, 2 * BQ, BK), F32),
                pltpu.VMEM((pairs, 2 * BQ, 128), F32),
                pltpu.VMEM((pairs, 2 * BQ, 128), F32),
                pltpu.VMEM((pairs, 2 * BQ, 128), F32),
            ],
        ),
        out_shape=[sds((rows, width), BF16), sds((rows, 128 * groups), F32)],
        cost_estimate=cost(4 * est, 8 * rows * width, est // 32),
        name="attn_fwd",
    )(cnt, lst, q, k, v, segq, codek)


def attn_bwd_kernel(nkb, pairs, cnt_ref, list_ref, q_ref, k_ref, v_ref, do_ref, o_ref, lse_ref, segq_ref, codek_ref,
                    dq_ref, dk_ref, dv_ref, qs_scr, ds_scr, row_scr, dq_scr, dk_scr, dv_scr):
    qb = pl.program_id(1)

    @pl.when(qb == 0)
    def _():
        dk_scr[...] = jnp.zeros(dk_scr.shape, F32)
        dv_scr[...] = jnp.zeros(dv_scr.shape, F32)

    count = cnt_ref[qb]
    lse_t = jnp.transpose(lse_ref[...])
    for p in range(pairs):
        cols = slice(128 * p, 128 * (p + 1))
        qs_scr[p] = pair_stack(q_ref[:, cols] * jnp.asarray(0.125, BF16))
        ds_scr[p] = pair_stack(do_ref[:, cols])
        prod = jnp.transpose(do_ref[:, cols].astype(F32) * o_ref[:, cols].astype(F32))
        da = jnp.sum(prod[:HEAD_DIM], axis=0, keepdims=True)
        db = jnp.sum(prod[HEAD_DIM:], axis=0, keepdims=True)
        row_scr[p, 0:1] = jnp.concatenate([lse_t[2 * p:2 * p + 1], lse_t[2 * p + 1:2 * p + 2]], axis=1)
        row_scr[p, 1:2] = jnp.concatenate([da, db], axis=1)
    dq_scr[...] = jnp.zeros(dq_scr.shape, F32)

    def step(s, carry):
        kb = list_ref[qb * nkb + s]
        off = pl.multiple_of(kb * BK, BK)
        kpos = kb * BK + lax.broadcasted_iota(jnp.int32, (BK, BQ), 0)
        qpos = qb * BQ + lax.broadcasted_iota(jnp.int32, (BK, BQ), 1)
        live = (codek_ref[pl.ds(off, BK), :] == segq_ref[...]) | (qpos == kpos)
        bias = jnp.where(live, 0.0, NEG_FILL).astype(F32)
        bias = jnp.concatenate([bias, bias], axis=1)
        for p in range(pairs):
            cols = slice(128 * p, 128 * (p + 1))
            k2 = k_ref[pl.ds(off, BK), cols]
            v2 = v_ref[pl.ds(off, BK), cols]
            sc = nt(k2, qs_scr[p]) + bias
            probs = jnp.exp(sc - row_scr[p, 0:1])
            dprobs = nt(v2, ds_scr[p])
            dsc = (probs * (dprobs - row_scr[p, 1:2])).astype(BF16)
            dv_scr[pl.ds(off, BK), cols] += nn(probs.astype(BF16), ds_scr[p])
            dk_scr[pl.ds(off, BK), cols] += nn(dsc, qs_scr[p])
            dq_scr[p] += tn(dsc, k2)
        return carry

    lax.fori_loop(0, count, step, 0)
    for p in range(pairs):
        dq_ref[:, 128 * p:128 * (p + 1)] = (pair_merge(dq_scr[p]) * 0.125).astype(BF16)

    @pl.when(qb == pl.num_programs(1) - 1)
    def _():
        dk_ref[...] = dk_scr[...].astype(BF16)
        dv_ref[...] = dv_scr[...].astype(BF16)


def attn_bwd(cnt, lst, q, k, v, do, o, lse, segq, codek):
    rows, width = q.shape
    keys = k.shape[0]
    nqb, nkb = rows // BQ, keys // BK
    groups, pairs = width // GROUP, GROUP // 128
    est = rows * 2 * BK * width
    qspec = pl.BlockSpec((BQ, GROUP), lambda g, i, *_: (i, g))
    kspec = pl.BlockSpec((keys, GROUP), lambda g, i, *_: (0, g))
    return pl.pallas_call(
        partial(attn_bwd_kernel, nkb, pairs),
        grid_spec=pltpu.PrefetchScalarGridSpec(
            num_scalar_prefetch=2,
            grid=(groups, nqb),
            in_specs=[
                qspec, kspec, kspec, qspec, qspec,
                pl.BlockSpec((BQ, 128), lambda g, i, *_: (i, g)),
                pl.BlockSpec((1, BQ), lambda g, i, *_: (0, i)),
                pl.BlockSpec((keys, 1), lambda g, i, *_: (0, 0)),
            ],
            out_specs=[qspec, kspec, kspec],
            scratch_shapes=[
                pltpu.VMEM((pairs, 2 * BQ, 128), BF16),
                pltpu.VMEM((pairs, 2 * BQ, 128), BF16),
                pltpu.VMEM((pairs, 8, 2 * BQ), F32),
                pltpu.VMEM((pairs, 2 * BQ, 128), F32),
                pltpu.VMEM((keys, GROUP), F32),
                pltpu.VMEM((keys, GROUP), F32),
            ],
        ),
        out_shape=[sds((rows, width), BF16), sds((keys, width), BF16), sds((keys, width), BF16)],
        cost_estimate=cost(10 * est, 16 * rows * width, est // 32),
        name="attn_bwd",
    )(cnt, lst, q, k, v, do, o, lse, segq, codek)


def row_mean(x):
    return jnp.mean(x, axis=-1, keepdims=True)


def out_norm_kernel(parts, tok_ref, emb_ref, vec_ref, *refs):
    mixed, weights = refs[:parts], refs[parts:2 * parts]
    xhat_ref, low_ref, rstd_ref = refs[2 * parts:]
    acc = tok_ref[...].astype(F32) + emb_ref[...] + vec_ref[4:5]
    for m, w in zip(mixed, weights):
        acc = acc + nn(m[...], w[...])
    centered = acc - row_mean(acc)
    rstd = lax.rsqrt(row_mean(centered * centered) + 1e-05)
    xhat = centered * rstd
    xhat_ref[...] = xhat
    rstd_ref[...] = jnp.broadcast_to(rstd, rstd_ref.shape)
    low_ref[...] = (xhat * vec_ref[0:1] + vec_ref[1:2]).astype(BF16)


def out_norm(tok, emb, vec, mixed, weights):
    rows, d = tok.shape
    parts = len(mixed)
    row = lambda n: pl.BlockSpec((RB, n), lambda i: (i, 0))
    return pl.pallas_call(
        partial(out_norm_kernel, parts),
        grid=(rows // RB,),
        in_specs=[row(d), whole((1, d)), whole(vec.shape)]
        + [row(m.shape[1]) for m in mixed]
        + [whole(w.shape) for w in weights],
        out_specs=[row(d), row(d), row(128)],
        out_shape=[sds((rows, d), F32), sds((rows, d), BF16), sds((rows, 128), F32)],
        cost_estimate=cost(2 * rows * d * d, 10 * rows * d + 2 * d * d),
        name="out_norm",
    )(tok, emb, vec, *mixed, *weights)


def gelu_pair(h):
    mag = jnp.abs(h)
    t = 1.0 / (1.0 + (0.3275911 * 0.7071067811865476) * mag)
    e = jnp.exp(-0.5 * (h * h))
    poly = t * (0.127414796 + t * (-0.142248368 + t * (0.7107068705 + t * (-0.7265760135 + t * 0.5307027145))))
    tail = poly * e
    phi = jnp.where(h < 0.0, tail, 1.0 - tail)
    return h * phi, phi + h * (e * 0.3989422804014327)


def ffn_up_kernel(x_ref, w_ref, b_ref, act_ref, gp_ref):
    w = w_ref[...]

    def chunk(i, carry):
        off = pl.multiple_of(i * RB, RB)
        h = nn(x_ref[pl.ds(off, RB), :], w) + b_ref[...]
        act, gp = gelu_pair(h)
        act_ref[pl.ds(off, RB), :] = act.astype(BF16)
        gp_ref[pl.ds(off, RB), :] = gp.astype(BF16)
        return carry

    lax.fori_loop(0, x_ref.shape[0] // RB, chunk, 0)


def ffn_up(x, w, b):
    rows, d = x.shape
    hidden = w.shape[1]
    col = lambda n: pl.BlockSpec((n, HB), lambda i: (0, i))
    return pl.pallas_call(
        ffn_up_kernel,
        grid=(hidden // HB,),
        in_specs=[whole((rows, d)), col(d), col(1)],
        out_specs=[col(rows), col(rows)],
        out_shape=[sds((rows, hidden), BF16), sds((rows, hidden), BF16)],
        cost_estimate=cost(2 * rows * d * hidden, 2 * (rows * d + d * hidden + 2 * rows * hidden), rows * hidden),
        name="ffn_up",
    )(x, w, b)


def ffn_down_kernel(parts, xhat_ref, cot_ref, vec_ref, *refs):
    acts, weights = refs[:parts], refs[parts:2 * parts]
    out_ref, dres_ref, dlow_ref, sums_ref = refs[2 * parts:]
    acc = xhat_ref[...] * vec_ref[0:1] + vec_ref[1:2] + vec_ref[5:6]
    for a, w in zip(acts, weights):
        acc = acc + nn(a[...], w[...])
    centered = acc - row_mean(acc)
    rstd = lax.rsqrt(row_mean(centered * centered) + 1e-05)
    xhat = centered * rstd
    out_ref[...] = (xhat * vec_ref[2:3] + vec_ref[3:4]).astype(BF16)
    cot = cot_ref[...].astype(F32)
    gg = cot * vec_ref[2:3]
    dres = rstd * (gg - row_mean(gg) - xhat * row_mean(gg * xhat))
    dres_ref[...] = dres
    low = dres.astype(BF16)
    dlow_ref[...] = low

    @pl.when(pl.program_id(0) == 0)
    def _():
        sums_ref[...] = jnp.zeros(sums_ref.shape, F32)

    sums_ref[0:1] += jnp.sum(cot * xhat, axis=0, keepdims=True)
    sums_ref[1:2] += jnp.sum(cot, axis=0, keepdims=True)
    sums_ref[2:3] += jnp.sum(low.astype(F32), axis=0, keepdims=True)


def ffn_down(xhat, cot, vec, acts, weights):
    rows, d = xhat.shape
    parts = len(acts)
    hidden = sum(w.shape[0] for w in weights)
    row = lambda n: pl.BlockSpec((RB, n), lambda i: (i, 0))
    return pl.pallas_call(
        partial(ffn_down_kernel, parts),
        grid=(rows // RB,),
        in_specs=[row(d), row(d), whole(vec.shape)]
        + [row(a.shape[1]) for a in acts]
        + [whole(w.shape) for w in weights],
        out_specs=[row(d), row(d), row(d), whole((8, d))],
        out_shape=[sds((rows, d), BF16), sds((rows, d), F32), sds((rows, d), BF16), sds((8, d), F32)],
        cost_estimate=cost(2 * rows * d * hidden, 14 * rows * d + 2 * d * hidden + 2 * rows * hidden),
        name="ffn_down",
    )(xhat, cot, vec, *acts, *weights)


def put_transposed(dst, tmp, src, core):
    if core is None:
        dst[...] = jnp.transpose(src)
        return
    tmp[...] = jnp.transpose(src)
    d = tmp.shape[0]
    for g in range(d // 128):
        mine = pl.multiple_of(g * 128 + core * 64, 64)
        other = pl.multiple_of(g * 128 + (1 - core) * 64, 64)
        dst[g * 64:(g + 1) * 64, :] = tmp[pl.ds(mine, 64), :]
        dst[d // 2 + g * 64:d // 2 + (g + 1) * 64, :] = tmp[pl.ds(other, 64), :]


def put_grad(keep_ref, send_ref, lt, right):
    d = lt.shape[0]
    if send_ref is None:
        for j in range(d // RB):
            keep_ref[j * RB:(j + 1) * RB, :] = nn(lt[j * RB:(j + 1) * RB, :], right).astype(BF16)
        return
    half = d // 2
    for j in range(half // RB):
        keep_ref[j * RB:(j + 1) * RB, :] = nn(lt[j * RB:(j + 1) * RB, :], right).astype(BF16)
        send_ref[j * RB:(j + 1) * RB, :] = nn(lt[half + j * RB:half + (j + 1) * RB, :], right).astype(BF16)


def ffn_bwd_kernel(split, chained, core_ref, *refs):
    d_ref, x_ref, up_ref, down_ref, act_ref, gp_ref = refs[:6]
    refs = refs[6:]
    if chained:
        prev_ref, refs = refs[0], refs[1:]
    dn_ref, sum_ref = refs[:2]
    refs = refs[2:]
    if split:
        gu_keep, gu_send, gd_keep, gd_send = refs[:4]
        refs = refs[4:]
    else:
        (gu_keep, gd_keep), gu_send, gd_send = refs[:2], None, None
        refs = refs[2:]
    xt_scr, dt_scr, tmp_scr, dup_scr = refs
    core = core_ref[0] if split else None

    @pl.when(pl.program_id(0) == 0)
    def _():
        put_transposed(xt_scr, tmp_scr, x_ref[...], core)
        put_transposed(dt_scr, tmp_scr, d_ref[...], core)
        dn_ref[...] = prev_ref[...] if chained else jnp.zeros(dn_ref.shape, F32)

    sum_ref[...] = jnp.zeros(sum_ref.shape, F32)

    def chunk(i, carry):
        rows = pl.ds(pl.multiple_of(i * RB, RB), RB)
        dup = (nt(d_ref[rows, :], down_ref[...]) * gp_ref[rows, :].astype(F32)).astype(BF16)
        dup_scr[rows, :] = dup
        sum_ref[...] += jnp.sum(dup.astype(F32), axis=0, keepdims=True)
        dn_ref[rows, :] += nt(dup, up_ref[...])
        return carry

    lax.fori_loop(0, d_ref.shape[0] // RB, chunk, 0)
    put_grad(gd_keep, gd_send, dt_scr, act_ref[...])
    put_grad(gu_keep, gu_send, xt_scr, dup_scr[...])


def ffn_bwd(core, dlow, x, up, down, act, gp, prev):
    rows, d = x.shape
    hidden = up.shape[1]
    split, chained = core is not None, prev is not None
    col = lambda n: pl.BlockSpec((n, HB), lambda i, *_: (0, i))
    args = [dlow, x, up, down, act, gp] + ([prev] if chained else [])
    in_specs = [whole((rows, d)), whole((rows, d)), col(d), pl.BlockSpec((HB, d), lambda i, *_: (i, 0)), col(rows), col(rows)]
    in_specs += [whole((rows, d))] if chained else []
    gspec = [col(d // 2)] * 4 if split else [col(d)] * 2
    gshape = [sds((d // 2, hidden), BF16)] * 4 if split else [sds((d, hidden), BF16)] * 2
    return pl.pallas_call(
        partial(ffn_bwd_kernel, split, chained),
        grid_spec=pltpu.PrefetchScalarGridSpec(
            num_scalar_prefetch=1,
            grid=(hidden // HB,),
            in_specs=in_specs,
            out_specs=[whole((rows, d)), col(1)] + gspec,
            scratch_shapes=[
                pltpu.VMEM((d, rows), BF16),
                pltpu.VMEM((d, rows), BF16),
                pltpu.VMEM((d, rows), BF16),
                pltpu.VMEM((rows, HB), BF16),
            ],
        ),
        out_shape=[sds((rows, d), F32), sds((1, hidden), F32)] + gshape,
        cost_estimate=cost(8 * rows * d * hidden, 2 * (4 * d * hidden + 2 * rows * hidden) + 12 * rows * d),
        name="ffn_bwd",
    )(core if split else jnp.zeros((1,), jnp.int32), *args)


def norm_bwd_kernel(parts, dres2_ref, dn_ref, xhat_ref, rstd_ref, vec_ref, *refs):
    weights = refs[:parts]
    dres_ref, dlow_ref, sums_ref = refs[parts:parts + 3]
    mixes = refs[parts + 3:]
    dn = dres2_ref[...] + dn_ref[...]
    xhat = xhat_ref[...]
    gg = dn * vec_ref[0:1]
    dres = rstd_ref[:, :1] * (gg - row_mean(gg) - xhat * row_mean(gg * xhat))
    dres_ref[...] = dres
    low = dres.astype(BF16)
    dlow_ref[...] = low

    @pl.when(pl.program_id(0) == 0)
    def _():
        sums_ref[...] = jnp.zeros(sums_ref.shape, F32)

    sums_ref[0:1] += jnp.sum(dn * xhat, axis=0, keepdims=True)
    sums_ref[1:2] += jnp.sum(dn, axis=0, keepdims=True)
    sums_ref[2:3] += jnp.sum(low.astype(F32), axis=0, keepdims=True)
    for w, m in zip(weights, mixes):
        m[...] = nt(low, w[...]).astype(BF16)


def norm_bwd(dres2, dn, xhat, rstd, vec, weights):
    rows, d = dn.shape
    parts = len(weights)
    row = lambda n: pl.BlockSpec((RB, n), lambda i: (i, 0))
    return pl.pallas_call(
        partial(norm_bwd_kernel, parts),
        grid=(rows // RB,),
        in_specs=[row(d), row(d), row(d), row(128), whole(vec.shape)] + [whole(w.shape) for w in weights],
        out_specs=[row(d), row(d), whole((8, d))] + [row(w.shape[0]) for w in weights],
        out_shape=[sds((rows, d), F32), sds((rows, d), BF16), sds((8, d), F32)]
        + [sds((rows, w.shape[0]), BF16) for w in weights],
        cost_estimate=cost(2 * rows * d * d, 20 * rows * d + 2 * d * d),
        name="norm_bwd",
    )(dres2, dn, xhat, rstd, vec, *weights)


def grad_tn_kernel(split, count, core_ref, left_ref, *refs):
    rights = refs[:count]
    refs = refs[count:]
    if split:
        keep_ref, send_ref, sum_ref, lt_scr, tmp_scr = refs
    else:
        keep_ref, sum_ref, lt_scr, tmp_scr = refs
        send_ref = None
    core = core_ref[0] if split else None
    put_transposed(lt_scr, tmp_scr, left_ref[...], core)
    width = rights[0].shape[1]
    for c, right in enumerate(rights):
        rows = right.shape[0]
        cols = slice(c * width, (c + 1) * width)
        put_grad(keep_ref.at[:, cols], None if send_ref is None else send_ref.at[:, cols], lt_scr.at[:, :rows], right[...])
        sum_ref[:, cols] = jnp.sum(right[...].astype(F32), axis=0, keepdims=True)


def grad_tn(core, left, rights):
    rows, d = left.shape
    width = rights[0].shape[1]
    n = width * len(rights)
    split = core is not None
    gshape = [sds((d // 2, n), BF16)] * 2 if split else [sds((d, n), BF16)]
    return pl.pallas_call(
        partial(grad_tn_kernel, split, len(rights)),
        grid_spec=pltpu.PrefetchScalarGridSpec(
            num_scalar_prefetch=1,
            grid=(1,),
            in_specs=[whole(left.shape)] + [whole(r.shape) for r in rights],
            out_specs=[whole(s.shape) for s in gshape] + [whole((1, n))],
            scratch_shapes=[pltpu.VMEM((d, rows), BF16), pltpu.VMEM((d, rows), BF16)],
        ),
        out_shape=gshape + [sds((1, n), F32)],
        cost_estimate=cost(2 * rows * d * n, 2 * (rows * d + rows * n + d * n)),
        name="grad_tn",
    )(core if split else jnp.zeros((1,), jnp.int32), left, *rights)


def in_grad_kernel(n, has_base, *refs):
    if has_base:
        base_ref, refs = refs[0], refs[1:]
    grads, weights, out_ref = refs[:n], refs[n:2 * n], refs[2 * n]
    acc = base_ref[...] if has_base else jnp.zeros(out_ref.shape, F32)
    for g, w in zip(grads, weights):
        acc = acc + nt(g[...], w[...])
    out_ref[...] = acc.astype(out_ref.dtype)


def in_grad(base, grads, weights, start, rows, dtype):
    d = weights[0][0].shape[1]
    n = len(grads)
    first = start // RB
    row = lambda m: pl.BlockSpec((RB, m), lambda i: (i + first, 0))
    wspec = lambda w, c: pl.BlockSpec((None, d, w.shape[2]), lambda i: (c, 0, 0))
    own = pl.BlockSpec((RB, d), lambda i: (i, 0))
    width = sum(g.shape[1] for g in grads)
    return pl.pallas_call(
        partial(in_grad_kernel, n, base is not None),
        grid=(rows // RB,),
        in_specs=([own] if base is not None else []) + [row(g.shape[1]) for g in grads] + [wspec(w, c) for w, c in weights],
        out_specs=own,
        out_shape=sds((rows, d), dtype),
        cost_estimate=cost(2 * rows * d * width, 6 * rows * d + 2 * rows * width + 2 * d * width),
        name="in_grad",
    )(*([base] if base is not None else []), *grads, *[w for w, _ in weights])


class Grid:
    axes = ("dp", "mp")

    def __init__(self):
        i = lax.axis_index("dp")
        self.y = lax.axis_index("mp")
        self.z, self.x, self.c = i // 4, (i // 2) % 2, i % 2
        self.all = [(z, x, c, y) for z in range(4) for x in range(2) for c in range(2) for y in range(2)]

    def permute(self, a, move):
        num = lambda z, x, c, y: ((z * 2 + x) * 2 + c) * 2 + y
        return lax.ppermute(a, self.axes, [(num(*p), num(*move(*p))) for p in self.all])

    def over_y(self, a):
        return self.permute(a, lambda z, x, c, y: (z, x, c, 1 - y))

    def over_x(self, a):
        return self.permute(a, lambda z, x, c, y: (z, 1 - x, c, y))

    def over_c(self, a):
        return self.permute(a, lambda z, x, c, y: (z, x, 1 - c, y))

    def over_zpair(self, a):
        return self.permute(a, lambda z, x, c, y: (z ^ 1, x, c, y))

    def shift_z(self, a, k):
        return self.permute(a, lambda z, x, c, y: ((z + k) % 4, x, c, y))


def join(mine, theirs, bit):
    first = jnp.where(bit == 0, mine, theirs)
    second = jnp.where(bit == 0, theirs, mine)
    return jnp.concatenate([first, second], axis=0)


def fetch_other(grid, w, x_first):
    rows = w.shape[0] // 8
    zbit = grid.z % 2
    if x_first:
        index = grid.c * 4 + zbit * 2 + grid.x
    else:
        index = grid.c * 4 + grid.x * 2 + zbit
    piece = grid.over_y(lax.dynamic_slice_in_dim(w, index * rows, rows, 0))
    if x_first:
        piece = join(piece, grid.over_x(piece), grid.x)
        piece = join(piece, grid.over_zpair(piece), zbit)
    else:
        piece = join(piece, grid.over_zpair(piece), zbit)
        piece = join(piece, grid.over_x(piece), grid.x)
    return join(piece, grid.over_c(piece), grid.c)


def at(a, axis, i):
    return lax.dynamic_index_in_dim(a, i, axis, keepdims=False)


def reduce_scatter(grid, own, oth, y_first):
    n = own[0].shape[1]
    view = lambda a: a.reshape(4, 2, 64, n)
    keep_own, keep_oth = view(own[0]).astype(F32), view(oth[0]).astype(F32)
    got_own = view(grid.over_c(own[1])).astype(F32)
    got_oth = view(grid.over_c(oth[1])).astype(F32)
    if y_first:
        back = grid.over_y((keep_oth + got_oth).astype(BF16)).astype(F32)
        total = keep_own + got_own + back
        send = at(total, 1, 1 - grid.x).astype(BF16)
        total = at(total, 1, grid.x) + grid.over_x(send).astype(F32)
    else:
        send_oth = at(keep_oth + got_oth, 1, 1 - grid.x).astype(BF16)
        send_own = at(keep_own + got_own, 1, 1 - grid.x).astype(BF16)
        side = at(keep_oth + got_oth, 1, grid.x) + grid.over_x(send_oth).astype(F32)
        total = at(keep_own + got_own, 1, grid.x) + grid.over_x(send_own).astype(F32)
        total = total + grid.over_y(side.astype(BF16)).astype(F32)
    parts = [grid.shift_z(at(total, 0, (grid.z + k) % 4).astype(BF16), k) for k in (1, 2, 3)]
    out = at(total, 0, grid.z)
    for p in parts:
        out = out + p.astype(F32)
    return out


def time_embed(step, d):
    half = d // 2
    frequency = jnp.exp(-math.log(10000.0) * jnp.arange(half, dtype=F32) / half)
    angles = step.astype(F32) * frequency[None, :]
    return jnp.concatenate([jnp.sin(angles), jnp.cos(angles)], axis=-1)


def block_lists(seg_own, seg_halo, rows):
    q = seg_own.reshape(-1, BQ)
    keys = jnp.concatenate([seg_own, seg_halo]).reshape(-1, BK)
    need = (keys[None, :, 0] <= q[:, None, -1]) & (keys[None, :, -1] >= q[:, None, 0])
    need = need.astype(jnp.int32)
    nkb = keys.shape[0]
    before = jnp.sum(need[:, None, :] * (jnp.arange(nkb)[None, None, :] < jnp.arange(nkb)[None, :, None]), axis=2)
    slot = jnp.arange(nkb)[None, :, None]
    pick = need[:, None, :] * (before[:, None, :] == slot)
    lst = jnp.sum(pick * jnp.arange(nkb)[None, None, :], axis=2)
    return jnp.sum(need, axis=1).astype(jnp.int32), lst.astype(jnp.int32).reshape(-1)


def per_device(
    fast,
    mp_size,
    tokens_in,
    timesteps,
    segment_ids,
    padding,
    qkv_weight,
    head_bias,
    out_weight,
    up_weight,
    up_bias,
    down_weight,
    vectors,
    cotangent,
):
    rows, d = tokens_in.shape
    assert timesteps.shape[0] == 1
    me = lax.axis_index("mp")
    own_start = me * rows
    emb = time_embed(timesteps[:, None], d)
    seg, pad = segment_ids[0], padding[0]
    seg_own = lax.dynamic_slice_in_dim(seg, own_start, rows)
    pad_own = lax.dynamic_slice_in_dim(pad, own_start, rows)
    if fast:
        grid = Grid()
        core = grid.c.reshape(1).astype(jnp.int32)
        halo = MAXDOC
        edge = jnp.where(me == 0, rows - halo, 0)
        halo_tok = grid.over_y(lax.dynamic_slice_in_dim(tokens_in, edge, halo, 0))
        halo_start = jnp.where(me == 0, rows, own_start - halo)
        seg_halo = lax.dynamic_slice_in_dim(seg, halo_start, halo)
        pad_halo = lax.dynamic_slice_in_dim(pad, halo_start, halo)
    else:
        core = None
        halo = SEQ
        halo_tok = lax.all_gather(tokens_in, "mp", axis=0, tiled=True)
        place = jnp.arange(SEQ, dtype=jnp.int32)
        seg_halo, pad_halo = seg, jnp.where((place >= own_start) & (place < own_start + rows), 1, pad)
    keys = rows + halo
    code = jnp.concatenate([jnp.where(pad_own == 0, seg_own, -1), jnp.where(pad_halo == 0, seg_halo, -1)])
    cnt, lst = block_lists(seg_own, seg_halo, rows)
    segq_col, segq_row = seg_own[:, None], seg_own[None, :]
    code_col, code_row = code[:, None], code[None, :]

    if fast:
        flat = qkv_weight.reshape(3 * d, -1)
        qkv_ws = [qkv_weight, fetch_other(grid, flat, False).reshape(qkv_weight.shape)]
        out_ws = [out_weight, fetch_other(grid, out_weight, True)]
        up_ws = [up_weight, fetch_other(grid, up_weight, False)]
        down_ws = [down_weight, fetch_other(grid, down_weight, True)]
        small = jnp.concatenate([head_bias.reshape(-1), up_bias])
        small = [small, grid.over_y(small)]
        nb = head_bias.size
        hbs = [s[:nb].reshape(head_bias.shape) for s in small]
        up_bs = [s[nb:].reshape(1, -1) for s in small]
    else:
        gather = lambda a, axis: lax.all_gather(a, "mp", axis=axis, tiled=True)
        qkv_ws, out_ws = [gather(qkv_weight, 2)], [gather(out_weight, 0)]
        up_ws, down_ws = [gather(up_weight, 1)], [gather(down_weight, 0)]
        hbs, up_bs = [gather(head_bias, 1)], [gather(up_bias, 0).reshape(1, -1)]
    parts = range(len(qkv_ws))

    qs, ks, vs, mixed, lses = [], [], [], [], []
    for p in parts:
        x_own, q, k, v = qkv_own(tokens_in, emb, qkv_ws[p], hbs[p], keys)
        x_halo, k, v = kv_halo(halo_tok, emb, qkv_ws[p], hbs[p], k, v)
        o, lse = attn_fwd(cnt, lst, q, k, v, segq_col, code_row)
        for held, value in zip((qs, ks, vs, mixed, lses), (q, k, v, o, lse)):
            held.append(value)
    x_all = jnp.concatenate([x_own, x_halo], axis=0)
    xhat1, normed, rstd1 = out_norm(tokens_in, emb, vectors, mixed, out_ws)
    acts, gps = zip(*[ffn_up(normed, up_ws[p], up_bs[p]) for p in parts])
    output, d_res2, d_down, sums2 = ffn_down(xhat1, cotangent, vectors, acts, down_ws)

    dn, ffn_grads, up_sums = None, [None] * len(parts), [None] * len(parts)
    for p in reversed(parts):
        dn, up_sums[p], *ffn_grads[p] = ffn_bwd(core, d_down, normed, up_ws[p], down_ws[p], acts[p], gps[p], dn)
    d_res1, d_attn, sums1, *d_mixed = norm_bwd(d_res2, dn, xhat1, rstd1, vectors, out_ws)
    out_grads, qkv_grads, head_sums = [None] * len(parts), [None] * len(parts), [None] * len(parts)
    d_qkv = [None] * len(parts)
    for p in reversed(parts):
        *out_grads[p], _ = grad_tn(core, d_attn, [mixed[p]])
    for p in reversed(parts):
        d_qkv[p] = attn_bwd(cnt, lst, qs[p], ks[p], vs[p], d_mixed[p], mixed[p], lses[p], segq_row, code_col)
        *qkv_grads[p], head_sums[p] = grad_tn(core, x_all, d_qkv[p])
    pairs = [(d_qkv[p][c], qkv_ws[p], c) for p in parts for c in range(3)]
    halo_grad = in_grad(
        None, [g for g, _, c in pairs if c], [(w, c) for _, w, c in pairs if c], rows, halo, BF16
    )
    own_grad = in_grad(d_res1, [g for g, _, _ in pairs], [(w, c) for _, w, c in pairs], 0, rows, F32)
    if fast:
        back = grid.over_y(halo_grad)
        near = jnp.arange(rows // halo) == 1 - me
        own_grad = own_grad.reshape(rows // halo, halo, d)
        own_grad = own_grad + jnp.where(near[:, None, None], back.astype(F32)[None], 0.0)
        grad_input = own_grad.reshape(rows, d).astype(BF16)
    else:
        back = lax.psum_scatter(halo_grad, "mp", scatter_dimension=0, tiled=True)
        grad_input = (own_grad + back.astype(F32)).astype(BF16)

    head_sum = [s.reshape(3, -1)[0::2] for s in head_sums]
    if fast:
        order = lambda a: jnp.where(me == 0, jnp.concatenate(a, axis=1), jnp.concatenate(a[::-1], axis=1))
        head_sum, up_sum = order(head_sum), order(list(up_sums))
    else:
        head_sum, up_sum = head_sum[0], up_sums[0]
    packed = jnp.concatenate([sums1[:2], sums2[:2], sums1[2:3], sums2[2:3], head_sum, up_sum.reshape(-1, d)], axis=0)
    packed = lax.psum(packed, ("dp", "mp"))
    grad_vectors = packed[:6]
    local = head_bias.shape[1]
    head_bias_sum = lax.dynamic_slice_in_dim(packed[6:8], me * local, local, 1)
    local = up_bias.shape[0]
    up_bias_sum = lax.dynamic_slice_in_dim(packed[8:].reshape(-1), me * local, local, 0)

    if fast:
        gu, gd = [g[:2] for g in ffn_grads], [g[2:] for g in ffn_grads]
        grad_up = reduce_scatter(grid, gu[0], gu[1], True)
        grad_down = reduce_scatter(grid, gd[0], gd[1], False)
        grad_out = reduce_scatter(grid, out_grads[0], out_grads[1], False)
        grad_qkv = reduce_scatter(grid, qkv_grads[0], qkv_grads[1], True)
    else:
        def scatter(g, groups):
            n = g.shape[1] // groups // mp_size
            g = lax.psum_scatter(g, "dp", scatter_dimension=0, tiled=True)
            g = g.reshape(-1, groups, mp_size, n).transpose(2, 0, 1, 3)
            return lax.psum_scatter(g, "mp", scatter_dimension=0, tiled=False).astype(F32).reshape(-1, groups * n)

        grad_up, grad_down = scatter(ffn_grads[0][0], 1), scatter(ffn_grads[0][1], 1)
        grad_out, grad_qkv = scatter(out_grads[0][0], 1), scatter(qkv_grads[0][0], 3)
    grad_qkv = grad_qkv.reshape(grad_qkv.shape[0], 3, -1).transpose(1, 0, 2)
    return (
        output,
        grad_input,
        grad_qkv,
        head_bias_sum,
        grad_out.T,
        grad_up,
        up_bias_sum,
        grad_down.T,
        grad_vectors,
    )


def solution(mesh):
    fast = dict(mesh.shape) == {"dp": 16, "mp": 2}
    return jax.shard_map(
        partial(per_device, fast, mesh.shape["mp"]),
        mesh=mesh,
        in_specs=(
            P(("dp", "mp"), None),
            P("dp"),
            P("dp", None),
            P("dp", None),
            P(None, None, "mp"),
            P(None, "mp"),
            P("mp", None),
            P(None, "mp"),
            P("mp"),
            P("mp", None),
            P(),
            P(("dp", "mp"), None),
        ),
        out_specs=(
            P(("dp", "mp"), None),
            P(("dp", "mp"), None),
            P(None, "dp", "mp"),
            P(None, "mp"),
            P("mp", "dp"),
            P("dp", "mp"),
            P("mp"),
            P("mp", "dp"),
            P(),
        ),
        check_vma=False,
    )
```

```python
from functools import partial
import math

import jax
import jax.numpy as jnp
from jax import lax
from jax.experimental import pallas as pl
from jax.experimental.pallas import tpu as pltpu
from jax.sharding import PartitionSpec as P

HEAD_DIM = 64
SEQ = 2048
MAXDOC = 512
BQ = 256
BK = 256
RB = 256
HB = 512
SCALE = 300.0
GROUP = 512
NEG_FILL = -1e30
F32 = jnp.float32
BF16 = jnp.bfloat16


def nt(a, b):
    return lax.dot_general(a, b, (((1,), (1,)), ((), ())), preferred_element_type=F32)


def nn(a, b):
    return lax.dot_general(a, b, (((1,), (0,)), ((), ())), preferred_element_type=F32)


def tn(a, b):
    return lax.dot_general(a, b, (((0,), (0,)), ((), ())), preferred_element_type=F32)


def cost(flops, nbytes, trans=0):
    return pl.CostEstimate(flops=int(flops * SCALE), bytes_accessed=int(nbytes * SCALE), transcendentals=int(trans * SCALE))


def whole(shape):
    return pl.BlockSpec(shape, lambda *_: (0,) * len(shape))


def sds(shape, dtype):
    return jax.ShapeDtypeStruct(shape, dtype)


def call(kernel, args, *, grid, in_specs, out_specs, out_shape, cost_estimate, name, prefetch=(), deps=(), scratch=(), aliases=None):
    first, skip, offset = len(prefetch) + len(args), len(deps), len(prefetch)

    def body(*refs):
        kernel(*refs[:first], *refs[first + skip:])

    return pl.pallas_call(
        body,
        grid_spec=pltpu.PrefetchScalarGridSpec(
            num_scalar_prefetch=offset,
            grid=grid,
            in_specs=list(in_specs) + [pl.BlockSpec(memory_space=pl.ANY)] * skip,
            out_specs=out_specs,
            scratch_shapes=list(scratch),
        ),
        out_shape=out_shape,
        input_output_aliases={k + offset: v for k, v in (aliases or {}).items()},
        cost_estimate=cost_estimate,
        name=name,
    )(*prefetch, *args, *deps)


def after(x, *deps):
    return lax.optimization_barrier((x, *deps))[0] if deps else x


def qkv_own_kernel(tok_ref, emb_ref, w_ref, hb_ref, x_ref, q_ref, k_ref, v_ref):
    x = (tok_ref[...].astype(F32) + emb_ref[...]).astype(BF16)
    x_ref[...] = x
    q_ref[...] = (nn(x, w_ref[0]) + hb_ref[0:1]).astype(BF16)
    k_ref[...] = nn(x, w_ref[1]).astype(BF16)
    v_ref[...] = (nn(x, w_ref[2]) + hb_ref[1:2]).astype(BF16)


def qkv_own(tok, emb, w, hb, deps=()):
    rows, d = tok.shape
    width = w.shape[2]
    row = lambda n: pl.BlockSpec((RB, n), lambda i, *_: (i, 0))
    return call(
        qkv_own_kernel,
        (tok, emb, w, hb),
        deps=deps,
        grid=(rows // RB,),
        in_specs=[row(d), whole((1, d)), whole(w.shape), whole(hb.shape)],
        out_specs=[row(d), row(width), row(width), row(width)],
        out_shape=[sds((rows, d), BF16)] + [sds((rows, width), BF16)] * 3,
        cost_estimate=cost(6 * rows * d * width, 2 * (2 * rows * d + 3 * rows * width + 3 * d * width)),
        name="qkv_own",
    )


def kv_halo_kernel(tok_ref, emb_ref, w_ref, hb_ref, x_ref, k_ref, v_ref):
    x = (tok_ref[...].astype(F32) + emb_ref[...]).astype(BF16)
    x_ref[...] = x
    k_ref[...] = nn(x, w_ref[1]).astype(BF16)
    v_ref[...] = (nn(x, w_ref[2]) + hb_ref[1:2]).astype(BF16)


def kv_halo(tok, emb, w, hb, deps=()):
    rows, d = tok.shape
    width = w.shape[2]
    row = lambda n: pl.BlockSpec((RB, n), lambda i, *_: (i, 0))
    return call(
        kv_halo_kernel,
        (tok, emb, w, hb),
        deps=deps,
        grid=(rows // RB,),
        in_specs=[row(d), whole((1, d)), whole(w.shape), whole(hb.shape)],
        out_specs=[row(d), row(width), row(width)],
        out_shape=[sds((rows, d), BF16)] + [sds((rows, width), BF16)] * 2,
        cost_estimate=cost(4 * rows * d * width, 2 * (2 * rows * d + 2 * rows * width + 3 * d * width)),
        name="kv_halo",
    )


def pair_stack(x2):
    lane = lax.broadcasted_iota(jnp.int32, (1, 128), 1)
    first = (lane < HEAD_DIM).astype(F32).astype(BF16)
    second = (lane >= HEAD_DIM).astype(F32).astype(BF16)
    return jnp.concatenate([x2 * first, x2 * second], axis=0)


def pair_merge(x):
    half = x.shape[0] // 2
    lane = lax.broadcasted_iota(jnp.int32, (half, 128), 1)
    return jnp.where(lane < HEAD_DIM, x[:half], x[half:])


def load_keys(srcs, dsts, sem, group):
    copies = []
    for pieces, dst in zip(srcs, dsts):
        off = 0
        for src in pieces:
            cols = pl.ds(pl.multiple_of(group * GROUP, GROUP), GROUP)
            copies.append(pltpu.make_async_copy(src.at[:, cols], dst.at[off:off + src.shape[0], :], sem.at[len(copies)]))
            off += src.shape[0]
    for c in copies:
        c.start()
    for c in copies:
        c.wait()


def attn_fwd_kernel(pieces, nkb, pairs, filled, base_ref, cnt_ref, list_ref, q_ref, segq_ref, codek_ref, *refs):
    k_srcs, v_srcs, refs = refs[:pieces], refs[pieces:2 * pieces], refs[2 * pieces + 2 * filled:]
    o_ref, lse_ref, k_ref, v_ref, qs_scr, m_scr, l_scr, acc_scr, sem = refs

    @pl.when(pl.program_id(1) == 0)
    def _():
        load_keys((k_srcs, v_srcs), (k_ref, v_ref), sem, pl.program_id(0))

    qb = pl.program_id(1) + base_ref[0]
    count = cnt_ref[qb]
    for p in range(pairs):
        qs_scr[p] = pair_stack(q_ref[:, 128 * p:128 * (p + 1)] * jnp.asarray(0.125, BF16))
    m_scr[...] = jnp.full(m_scr.shape, -3e38, F32)
    l_scr[...] = jnp.zeros(l_scr.shape, F32)
    acc_scr[...] = jnp.zeros(acc_scr.shape, F32)

    def step(s, carry):
        kb = list_ref[qb * nkb + s]
        off = pl.multiple_of(kb * BK, BK)
        kpos = kb * BK + lax.broadcasted_iota(jnp.int32, (BK, BQ), 0)
        qpos = qb * BQ + lax.broadcasted_iota(jnp.int32, (BK, BQ), 1)
        live = (codek_ref[pl.ds(off, BK), :] == segq_ref[...]) | (qpos == kpos)
        bias = jnp.where(live, 0.0, NEG_FILL).astype(F32)
        bias = jnp.concatenate([bias, bias], axis=1)
        scs = [nt(k_ref[pl.ds(off, BK), 128 * p:128 * (p + 1)], qs_scr[p]) for p in range(pairs)]
        es = []
        for p in range(pairs):
            sc = scs[p] + bias
            old = m_scr[p:p + 1]
            new = jnp.maximum(old, jnp.max(sc, axis=0, keepdims=True))
            e = jnp.exp(sc - new)
            fade = jnp.exp(old - new)
            m_scr[p:p + 1] = new
            l_scr[p:p + 1] = l_scr[p:p + 1] * fade + jnp.sum(e, axis=0, keepdims=True)
            es.append((e.astype(BF16), fade))
        for p in range(pairs):
            acc_scr[p] = acc_scr[p] * es[p][1] + tn(v_ref[pl.ds(off, BK), 128 * p:128 * (p + 1)], es[p][0])
        return carry

    lax.fori_loop(0, count, step, 0)
    lse = m_scr[...] + jnp.log(l_scr[...])
    for p in range(pairs):
        o = acc_scr[p] / l_scr[p:p + 1]
        o = jnp.concatenate([o[:HEAD_DIM, :BQ], o[HEAD_DIM:, BQ:]], axis=0)
        o_ref[:, 128 * p:128 * (p + 1)] = jnp.transpose(o).astype(BF16)
        lse_ref[2 * p:2 * p + 1, :] = lse[p:p + 1, :BQ]
        lse_ref[2 * p + 1:2 * p + 2, :] = lse[p:p + 1, BQ:]


def attn_fwd(base, nqb, cnt, lst, nkb, q, k, v, segq, codek, into=(), deps=()):
    rows, width = q.shape
    pieces, keys = len(k), sum(a.shape[0] for a in k)
    groups, pairs = width // GROUP, GROUP // 128
    est = nqb * BQ * 2 * BK * width
    qspec = lambda n: pl.BlockSpec((BQ, n), lambda g, i, b, *_: (i + b[0], g))
    lspec = pl.BlockSpec((2 * pairs, BQ), lambda g, i, b, *_: (g, i + b[0]))
    anyspec = pl.BlockSpec(memory_space=pl.ANY)
    args = [q, segq, codek, *k, *v, *into]
    first = 3 + 2 * pieces
    return call(
        partial(attn_fwd_kernel, pieces, nkb, pairs, len(into) // 2),
        args,
        prefetch=(base, cnt, lst),
        deps=deps,
        grid=(groups, nqb),
        in_specs=[qspec(GROUP), pl.BlockSpec((1, BQ), lambda g, i, b, *_: (0, i + b[0])), pl.BlockSpec((codek.shape[0], 1), lambda *_: (0, 0))]
        + [anyspec] * (len(args) - 3),
        out_specs=[qspec(GROUP), lspec],
        out_shape=[sds((rows, width), BF16), sds((2 * pairs * groups, rows), F32)],
        aliases={first: 0, first + 1: 1} if into else None,
        scratch=[
            pltpu.VMEM((keys, GROUP), BF16),
            pltpu.VMEM((keys, GROUP), BF16),
            pltpu.VMEM((pairs, 2 * BQ, 128), BF16),
            pltpu.VMEM((pairs, 2 * BQ), F32),
            pltpu.VMEM((pairs, 2 * BQ), F32),
            pltpu.VMEM((pairs, 128, 2 * BQ), F32),
            pltpu.SemaphoreType.DMA((2 * pieces,)),
        ],
        cost_estimate=cost(4 * est, 8 * rows * width, est // 32),
        name="attn_fwd",
    )


def attn_bwd_kernel(pieces, nkb, pairs, cnt_ref, list_ref, q_ref, do_ref, o_ref, lse_ref, segq_ref, codek_ref, *refs):
    k_srcs, v_srcs, refs = refs[:pieces], refs[pieces:2 * pieces], refs[2 * pieces:]
    dq_ref, dk_ref, dv_ref, k_ref, v_ref, qs_scr, ds_scr, row_scr, dq_scr, dk_scr, dv_scr, sem = refs
    qb = pl.program_id(1)

    @pl.when(qb == 0)
    def _():
        load_keys((k_srcs, v_srcs), (k_ref, v_ref), sem, pl.program_id(0))

    @pl.when(qb == 0)
    def _():
        dk_scr[...] = jnp.zeros(dk_scr.shape, F32)
        dv_scr[...] = jnp.zeros(dv_scr.shape, F32)

    count = cnt_ref[qb]
    lse_t = lse_ref[...]
    for p in range(pairs):
        cols = slice(128 * p, 128 * (p + 1))
        qs_scr[p] = pair_stack(q_ref[:, cols] * jnp.asarray(0.125, BF16))
        ds_scr[p] = pair_stack(do_ref[:, cols])
        prod = jnp.transpose(do_ref[:, cols].astype(F32) * o_ref[:, cols].astype(F32))
        da = jnp.sum(prod[:HEAD_DIM], axis=0, keepdims=True)
        db = jnp.sum(prod[HEAD_DIM:], axis=0, keepdims=True)
        row_scr[p, 0:1] = jnp.concatenate([lse_t[2 * p:2 * p + 1], lse_t[2 * p + 1:2 * p + 2]], axis=1)
        row_scr[p, 1:2] = jnp.concatenate([da, db], axis=1)
    dq_scr[...] = jnp.zeros(dq_scr.shape, F32)

    def step(s, carry):
        kb = list_ref[qb * nkb + s]
        off = pl.multiple_of(kb * BK, BK)
        kpos = kb * BK + lax.broadcasted_iota(jnp.int32, (BK, BQ), 0)
        qpos = qb * BQ + lax.broadcasted_iota(jnp.int32, (BK, BQ), 1)
        live = (codek_ref[pl.ds(off, BK), :] == segq_ref[...]) | (qpos == kpos)
        bias = jnp.where(live, 0.0, NEG_FILL).astype(F32)
        bias = jnp.concatenate([bias, bias], axis=1)
        for p in range(pairs):
            cols = slice(128 * p, 128 * (p + 1))
            k2 = k_ref[pl.ds(off, BK), cols]
            v2 = v_ref[pl.ds(off, BK), cols]
            sc = nt(k2, qs_scr[p]) + bias
            probs = jnp.exp(sc - row_scr[p, 0:1])
            dprobs = nt(v2, ds_scr[p])
            dsc = (probs * (dprobs - row_scr[p, 1:2])).astype(BF16)
            dv_scr[pl.ds(off, BK), cols] += nn(probs.astype(BF16), ds_scr[p])
            dk_scr[pl.ds(off, BK), cols] += nn(dsc, qs_scr[p])
            dq_scr[p] += tn(k2, dsc)
        return carry

    lax.fori_loop(0, count, step, 0)
    for p in range(pairs):
        dq = dq_scr[p] * 0.125
        dq = jnp.concatenate([dq[:HEAD_DIM, :BQ], dq[HEAD_DIM:, BQ:]], axis=0)
        dq_ref[:, 128 * p:128 * (p + 1)] = jnp.transpose(dq).astype(BF16)

    @pl.when(qb == pl.num_programs(1) - 1)
    def _():
        dk_ref[...] = dk_scr[...].astype(BF16)
        dv_ref[...] = dv_scr[...].astype(BF16)


def attn_bwd(cnt, lst, nkb, q, k, v, do, o, lse, segq, codek, deps=()):
    rows, width = q.shape
    pieces, keys = len(k), sum(a.shape[0] for a in k)
    groups, pairs = width // GROUP, GROUP // 128
    est = rows * 2 * BK * width
    qspec = pl.BlockSpec((BQ, GROUP), lambda g, i, *_: (i, g))
    kspec = pl.BlockSpec((keys, GROUP), lambda g, i, *_: (0, g))
    return call(
        partial(attn_bwd_kernel, pieces, nkb, pairs),
        (q, do, o, lse, segq, codek, *k, *v),
        prefetch=(cnt, lst),
        deps=deps,
        grid=(groups, rows // BQ),
        in_specs=[
            qspec, qspec, qspec,
            pl.BlockSpec((2 * pairs, BQ), lambda g, i, *_: (g, i)),
            pl.BlockSpec((1, BQ), lambda g, i, *_: (0, i)),
            pl.BlockSpec((keys, 1), lambda g, i, *_: (0, 0)),
        ] + [pl.BlockSpec(memory_space=pl.ANY)] * (2 * pieces),
        out_specs=[qspec, kspec, kspec],
        scratch=[
            pltpu.VMEM((keys, GROUP), BF16),
            pltpu.VMEM((keys, GROUP), BF16),
            pltpu.VMEM((pairs, 2 * BQ, 128), BF16),
            pltpu.VMEM((pairs, 2 * BQ, 128), BF16),
            pltpu.VMEM((pairs, 8, 2 * BQ), F32),
            pltpu.VMEM((pairs, 128, 2 * BQ), F32),
            pltpu.VMEM((keys, GROUP), F32),
            pltpu.VMEM((keys, GROUP), F32),
            pltpu.SemaphoreType.DMA((2 * pieces,)),
        ],
        out_shape=[sds((rows, width), BF16), sds((keys, width), BF16), sds((keys, width), BF16)],
        cost_estimate=cost(10 * est, 16 * rows * width, est // 32),
        name="attn_bwd",
    )


def row_mean(x):
    return jnp.mean(x, axis=-1, keepdims=True)


def out_norm_kernel(parts, tok_ref, emb_ref, vec_ref, *refs):
    mixed, weights = refs[:parts], refs[parts:2 * parts]
    xhat_ref, low_ref, rstd_ref = refs[2 * parts:]
    acc = tok_ref[...].astype(F32) + emb_ref[...] + vec_ref[4:5]
    for m, w in zip(mixed, weights):
        acc = acc + nn(m[...], w[...])
    centered = acc - row_mean(acc)
    rstd = lax.rsqrt(row_mean(centered * centered) + 1e-05)
    xhat = centered * rstd
    xhat_ref[...] = xhat.astype(BF16)
    rstd_ref[...] = jnp.broadcast_to(rstd, rstd_ref.shape)
    low_ref[...] = (xhat * vec_ref[0:1] + vec_ref[1:2]).astype(BF16)


def out_norm(tok, emb, vec, mixed, weights, deps=()):
    rows, d = tok.shape
    parts = len(mixed)
    row = lambda n: pl.BlockSpec((RB, n), lambda i, *_: (i, 0))
    return call(
        partial(out_norm_kernel, parts),
        (tok, emb, vec, *mixed, *weights),
        deps=deps,
        grid=(rows // RB,),
        in_specs=[row(d), whole((1, d)), whole(vec.shape)]
        + [row(m.shape[1]) for m in mixed]
        + [whole(w.shape) for w in weights],
        out_specs=[row(d), row(d), row(128)],
        out_shape=[sds((rows, d), BF16), sds((rows, d), BF16), sds((rows, 128), F32)],
        cost_estimate=cost(2 * rows * d * d, 8 * rows * d + 2 * d * d),
        name="out_norm",
    )


def gelu_pair(h):
    mag = jnp.abs(h)
    t = 1.0 / (1.0 + (0.3275911 * 0.7071067811865476) * mag)
    e = jnp.exp(-0.5 * (h * h))
    poly = t * (0.127414796 + t * (-0.142248368 + t * (0.7107068705 + t * (-0.7265760135 + t * 0.5307027145))))
    tail = poly * e
    phi = jnp.where(h < 0.0, tail, 1.0 - tail)
    return h * phi, phi + h * (e * 0.3989422804014327)


def pick(sel, per):
    if sel is None:
        return lambda j, core: j
    return lambda j, core: j + per * (core[0] if sel == 0 else 1 - core[0])


def ffn_up_kernel(n, core_ref, x_ref, *refs):
    ws, bs, acts, gps = refs[:n], refs[n:2 * n], refs[2 * n:3 * n], refs[3 * n:]
    rows = min(x_ref.shape[0], 512)

    def chunk(i, carry):
        at_rows = pl.ds(pl.multiple_of(i * rows, rows), rows)
        for w, b, a, g in zip(ws, bs, acts, gps):
            h = nn(x_ref[at_rows, :], w[...]) + b[...]
            act, gp = gelu_pair(h)
            a[at_rows, :] = act.astype(BF16)
            g[at_rows, :] = gp.astype(BF16)
        return carry

    lax.fori_loop(0, x_ref.shape[0] // rows, chunk, 0)


def ffn_up(core, x, items, hidden, deps=()):
    rows, d = x.shape
    n, per = len(items), hidden // HB
    col = lambda r, sel: pl.BlockSpec((r, HB), lambda j, c: (0, pick(sel, per)(j, c)))
    out = call(
        partial(ffn_up_kernel, n),
        (x, *[i[0] for i in items], *[i[2] for i in items]),
        prefetch=(core,),
        deps=deps,
        grid=(per,),
        in_specs=[whole((rows, d))] + [col(d, i[1]) for i in items] + [col(1, i[3]) for i in items],
        out_specs=[col(rows, None)] * (2 * n),
        out_shape=[sds((rows, hidden), BF16)] * (2 * n),
        cost_estimate=cost(2 * rows * d * hidden * n, 2 * (rows * d + n * (d + 2 * rows) * hidden), rows * hidden * n),
        name="ffn_up",
    )
    return out[:n], out[n:]


def ffn_down_kernel(parts, core_ref, norm_ref, cot_ref, vec_ref, *refs):
    acts, weights = refs[:parts], refs[parts:2 * parts]
    out_ref, dlow_ref, sums_ref = refs[2 * parts:]
    acc = norm_ref[...].astype(F32) + vec_ref[5:6]
    for a, w in zip(acts, weights):
        acc = acc + nn(a[...], w[...])
    centered = acc - row_mean(acc)
    rstd = lax.rsqrt(row_mean(centered * centered) + 1e-05)
    xhat = centered * rstd
    out_ref[...] = (xhat * vec_ref[2:3] + vec_ref[3:4]).astype(BF16)
    cot = cot_ref[...].astype(F32)
    gg = cot * vec_ref[2:3]
    dres = rstd * (gg - row_mean(gg) - xhat * row_mean(gg * xhat))
    low = dres.astype(BF16)
    dlow_ref[...] = low

    @pl.when(pl.program_id(0) == 0)
    def _():
        sums_ref[...] = jnp.zeros(sums_ref.shape, F32)

    sums_ref[0:1] += jnp.sum(cot * xhat, axis=0, keepdims=True)
    sums_ref[1:2] += jnp.sum(cot, axis=0, keepdims=True)
    sums_ref[2:3] += jnp.sum(low.astype(F32), axis=0, keepdims=True)


def ffn_down(core, normed, cot, vec, acts, weights, deps=()):
    rows, d = normed.shape
    parts = len(acts)
    hidden = sum(a.shape[1] for a in acts)
    row = lambda n: pl.BlockSpec((RB, n), lambda i, *_: (i, 0))
    wspec = lambda a, sel: pl.BlockSpec((a.shape[1], d), lambda i, c: (pick(sel, 1)(0, c), 0))
    return call(
        partial(ffn_down_kernel, parts),
        (normed, cot, vec, *acts, *[w for w, _ in weights]),
        prefetch=(core,),
        deps=deps,
        grid=(rows // RB,),
        in_specs=[row(d), row(d), whole(vec.shape)]
        + [row(a.shape[1]) for a in acts]
        + [wspec(a, sel) for a, (_, sel) in zip(acts, weights)],
        out_specs=[row(d), row(d), whole((8, d))],
        out_shape=[sds((rows, d), BF16), sds((rows, d), BF16), sds((8, d), F32)],
        cost_estimate=cost(2 * rows * d * hidden, 8 * rows * d + 2 * d * hidden + 2 * rows * hidden),
        name="ffn_down",
    )


def ffn_dup_kernel(n, core_ref, d_ref, *refs):
    ups, downs, gps, refs = refs[:n], refs[n:2 * n], refs[2 * n:3 * n], refs[3 * n:]
    dn_ref, dups, sums, acc_ref = refs[0], refs[1:n + 1], refs[n + 1:2 * n + 1], refs[2 * n + 1]
    rows = min(d_ref.shape[0], 512)
    first = pl.program_id(0) == 0
    last = pl.program_id(0) == pl.num_programs(0) - 1

    for s in sums:
        s[...] = jnp.zeros(s.shape, F32)

    def chunk(i, carry):
        at_rows = pl.ds(pl.multiple_of(i * rows, rows), rows)
        total = None
        for up, down, gp, dup_ref, s in zip(ups, downs, gps, dups, sums):
            dup = (nt(d_ref[at_rows, :], down[...]) * gp[at_rows, :].astype(F32)).astype(BF16)
            dup_ref[at_rows, :] = dup
            s[...] += jnp.sum(dup.astype(F32), axis=0, keepdims=True)
            term = nt(dup, up[...])
            total = term if total is None else total + term
        acc_ref[at_rows, :] = jnp.where(first, total, acc_ref[at_rows, :] + total)
        return carry

    lax.fori_loop(0, d_ref.shape[0] // rows, chunk, 0)

    @pl.when(last)
    def _():
        dn_ref[...] = acc_ref[...].astype(BF16)


def ffn_dup(core, dlow, items, hidden, deps=()):
    rows, d = dlow.shape
    n, per = len(items), hidden // HB
    col = lambda r, sel: pl.BlockSpec((r, HB), lambda j, c: (0, pick(sel, per)(j, c)))
    down = lambda sel: pl.BlockSpec((HB, d), lambda j, c: (pick(sel, per)(j, c), 0))
    out = call(
        partial(ffn_dup_kernel, n),
        (dlow, *[i[0] for i in items], *[i[2] for i in items], *[i[4] for i in items]),
        prefetch=(core,),
        deps=deps,
        grid=(per,),
        in_specs=[whole((rows, d))] + [col(d, i[1]) for i in items] + [down(i[3]) for i in items] + [col(rows, None)] * n,
        out_specs=[whole((rows, d))] + [col(rows, None)] * n + [col(1, None)] * n,
        scratch=[pltpu.VMEM((rows, d), F32)],
        out_shape=[sds((rows, d), BF16)] + [sds((rows, hidden), BF16)] * n + [sds((1, hidden), F32)] * n,
        cost_estimate=cost(4 * rows * d * hidden * n, 2 * n * (2 * d + 2 * rows) * hidden + 4 * rows * d),
        name="ffn_dup",
    )
    return out[0], out[1:n + 1], out[n + 1:]


def put_transposed(dst, tmp, src, core):
    if core is None:
        dst[...] = jnp.transpose(src)
        return
    tmp[...] = jnp.transpose(src)
    d = tmp.shape[0]
    for g in range(d // 128):
        mine = pl.multiple_of(g * 128 + core * 64, 64)
        other = pl.multiple_of(g * 128 + (1 - core) * 64, 64)
        dst[g * 64:(g + 1) * 64, :] = tmp[pl.ds(mine, 64), :]
        dst[d // 2 + g * 64:d // 2 + (g + 1) * 64, :] = tmp[pl.ds(other, 64), :]


def put_grad(keep_ref, send_ref, lt, right):
    d = lt.shape[0]
    if send_ref is None:
        for j in range(d // RB):
            keep_ref[j * RB:(j + 1) * RB, :] = nn(lt[j * RB:(j + 1) * RB, :], right).astype(BF16)
        return
    half = d // 2
    keep_ref[...] = nn(lt[:half, :], right).astype(BF16)
    send_ref[...] = nn(lt[half:, :], right).astype(BF16)


def wide_grad_kernel(n, count, steps, *refs):
    lefts, rights, refs = refs[:n], refs[n:n + n * count], refs[n + n * count:]
    outs, lt = refs[:count * steps], refs[count * steps]
    step = pl.program_id(0)
    cols, off = [], 0
    for left in lefts:
        cols.append(slice(off, off + left.shape[0]))
        off += left.shape[0]

    @pl.when(step == 0)
    def _():
        for c, left in zip(cols, lefts):
            lt[:, c] = jnp.transpose(left[...])

    d = lt.shape[0]
    for p in range(count):
        mine = rights[p * n:(p + 1) * n]
        for s in range(steps):
            @pl.when(step == s)
            def _(s=s, p=p, mine=mine):
                out = outs[p * steps + s]

                def chunk(i, carry):
                    r = pl.ds(pl.multiple_of(i * 512, 512), 512)
                    acc = nn(lt[r, cols[0]], mine[0][...])
                    for c, right in zip(cols[1:], mine[1:]):
                        acc = acc + nn(lt[r, c], right[...])
                    out[r, :] = acc.astype(BF16)
                    return carry

                lax.fori_loop(0, d // 512, chunk, 0)


def wide_grad(lefts, items, deps=()):
    d, hidden = lefts[0].shape[1], items[0][0].shape[1]
    n, count, steps = len(lefts), len(items), hidden // HB
    rows = sum(a.shape[0] for a in lefts)
    flat = [a for i in items for a in i]
    out = call(
        partial(wide_grad_kernel, n, count, steps),
        (*lefts, *flat),
        deps=deps,
        grid=(steps,),
        in_specs=[whole(a.shape) for a in lefts] + [pl.BlockSpec((a.shape[0], HB), lambda j: (0, j)) for a in flat],
        out_specs=[whole((d, HB))] * (count * steps),
        scratch=[pltpu.VMEM((d, rows), BF16)],
        out_shape=[sds((d, HB), BF16)] * (count * steps),
        cost_estimate=cost(2 * rows * d * hidden * count, 2 * (rows * d + count * (rows + d) * hidden)),
        name="wide_grad",
    )
    return [out[p * steps:(p + 1) * steps] for p in range(count)]


def norm_bwd_kernel(parts, terms, xhat_ref, rstd_ref, vec_ref, *refs):
    weights, dns, refs = refs[:parts], refs[parts:parts + terms], refs[parts + terms:]
    dlow_ref, sums_ref, mixes = refs[0], refs[1], refs[2:]
    dn = dns[0][...].astype(F32)
    for t in dns[1:]:
        dn = dn + t[...].astype(F32)
    xhat = xhat_ref[...].astype(F32)
    gg = dn * vec_ref[0:1]
    low = (rstd_ref[:, :1] * (gg - row_mean(gg) - xhat * row_mean(gg * xhat))).astype(BF16)
    dlow_ref[...] = low

    @pl.when(pl.program_id(0) == 0)
    def _():
        sums_ref[...] = jnp.zeros(sums_ref.shape, F32)

    sums_ref[0:1] += jnp.sum(dn * xhat, axis=0, keepdims=True)
    sums_ref[1:2] += jnp.sum(dn, axis=0, keepdims=True)
    sums_ref[2:3] += jnp.sum(low.astype(F32), axis=0, keepdims=True)
    for w, m in zip(weights, mixes):
        m[...] = nt(low, w[...]).astype(BF16)


def norm_bwd(dns, xhat, rstd, vec, weights, deps=()):
    rows, d = xhat.shape
    parts, terms = len(weights), len(dns)
    row = lambda n: pl.BlockSpec((RB, n), lambda i, *_: (i, 0))
    return call(
        partial(norm_bwd_kernel, parts, terms),
        (xhat, rstd, vec, *weights, *dns),
        deps=deps,
        grid=(rows // RB,),
        in_specs=[row(d), row(128), whole(vec.shape)] + [whole(w.shape) for w in weights] + [row(d)] * terms,
        out_specs=[row(d), whole((8, d))] + [row(w.shape[0]) for w in weights],
        out_shape=[sds((rows, d), BF16), sds((8, d), F32)] + [sds((rows, w.shape[0]), BF16) for w in weights],
        cost_estimate=cost(2 * rows * d * d, 14 * rows * d + 2 * d * d),
        name="norm_bwd",
    )


def grad_tn_kernel(split, lefts, count, core_ref, *refs):
    left_refs, rights, refs = refs[:lefts], refs[lefts:lefts + count], refs[lefts + count:]
    if split:
        keep_ref, send_ref, sum_ref, lt_scr, tmp_scr = refs
    else:
        keep_ref, sum_ref, lt_scr, tmp_scr = refs
        send_ref = None
    off = 0
    for left in left_refs:
        cols = slice(off, off + left.shape[0])
        put_transposed(lt_scr.at[:, cols], tmp_scr.at[:, cols], left[...], core_ref[0] if split else None)
        off += left.shape[0]
    width = rights[0].shape[1]
    for c, right in enumerate(rights):
        cols = slice(c * width, (c + 1) * width)
        put_grad(keep_ref.at[:, cols], None if send_ref is None else send_ref.at[:, cols], lt_scr.at[:, :right.shape[0]], right[...])
        sum_ref[:, cols] = jnp.sum(right[...].astype(F32), axis=0, keepdims=True)


def grad_tn(core, lefts, rights, deps=()):
    rows, d = sum(a.shape[0] for a in lefts), lefts[0].shape[1]
    width = rights[0].shape[1]
    n = width * len(rights)
    split = core is not None
    gshape = [sds((d // 2, n), BF16)] * 2 if split else [sds((d, n), BF16)]
    return call(
        partial(grad_tn_kernel, split, len(lefts), len(rights)),
        (*lefts, *rights),
        prefetch=(core if split else jnp.zeros((1,), jnp.int32),),
        deps=deps,
        grid=(1,),
        in_specs=[whole(a.shape) for a in (*lefts, *rights)],
        out_specs=[whole(a.shape) for a in gshape] + [whole((1, n))],
        scratch=[pltpu.VMEM((d, rows), BF16), pltpu.VMEM((d, rows), BF16)],
        out_shape=gshape + [sds((1, n), F32)],
        cost_estimate=cost(2 * rows * d * n, 2 * (rows * d + rows * n + d * n)),
        name="grad_tn",
    )


def in_grad_kernel(n, has_base, *refs):
    if has_base:
        base_ref, refs = refs[0], refs[1:]
    grads, weights, out_ref = refs[:n], refs[n:2 * n], refs[2 * n]
    acc = base_ref[...].astype(F32) if has_base else jnp.zeros(out_ref.shape, F32)
    for g, w in zip(grads, weights):
        acc = acc + nt(g[...], w[...])
    out_ref[...] = acc.astype(out_ref.dtype)


def in_grad(base, grads, weights, start, rows, deps=()):
    d = weights[0][0].shape[1]
    n = len(grads)
    first = start // RB
    row = lambda m: pl.BlockSpec((RB, m), lambda i, *_: (i + first, 0))
    wspec = lambda w, c: pl.BlockSpec((None, d, w.shape[2]), lambda i, *_: (c, 0, 0))
    own = pl.BlockSpec((RB, d), lambda i, *_: (i, 0))
    width = sum(g.shape[1] for g in grads)
    return call(
        partial(in_grad_kernel, n, base is not None),
        (*([base] if base is not None else []), *grads, *[w for w, _ in weights]),
        deps=deps,
        grid=(rows // RB,),
        in_specs=([own] if base is not None else []) + [row(g.shape[1]) for g in grads] + [wspec(w, c) for w, c in weights],
        out_specs=own,
        out_shape=sds((rows, d), BF16),
        cost_estimate=cost(2 * rows * d * width, 6 * rows * d + 2 * rows * width + 2 * d * width),
        name="in_grad",
    )


class Grid:
    axes = ("dp", "mp")

    def __init__(self):
        i = lax.axis_index("dp")
        self.y = lax.axis_index("mp")
        self.z, self.x, self.c = i // 4, (i // 2) % 2, i % 2
        self.all = [(z, x, c, y) for z in range(4) for x in range(2) for c in range(2) for y in range(2)]

    def permute(self, a, move):
        num = lambda z, x, c, y: ((z * 2 + x) * 2 + c) * 2 + y
        return lax.ppermute(a, self.axes, [(num(*p), num(*move(*p))) for p in self.all])

    def over_y(self, a):
        return self.permute(a, lambda z, x, c, y: (z, x, c, 1 - y))

    def over_x(self, a):
        return self.permute(a, lambda z, x, c, y: (z, 1 - x, c, y))

    def over_c(self, a):
        return self.permute(a, lambda z, x, c, y: (z, x, 1 - c, y))

    def over_zpair(self, a):
        return self.permute(a, lambda z, x, c, y: (z ^ 1, x, c, y))

    def shift_z(self, a, k):
        return self.permute(a, lambda z, x, c, y: ((z + k) % 4, x, c, y))


def join(mine, theirs, bit):
    first = jnp.where(bit == 0, mine, theirs)
    second = jnp.where(bit == 0, theirs, mine)
    return jnp.concatenate([first, second], axis=0)


class Fetch:
    def __init__(self, grid, w, x_first, cut):
        self.grid, self.x_first = grid, x_first
        self.zbit = grid.z % 2
        pair = (self.zbit * 2 + grid.x) if x_first else (grid.x * 2 + self.zbit)
        self.cut = lambda *deps: cut(after(w, *deps), grid.c, pair)

    def prepare(self, *deps):
        self.op = self.cut(*deps)
        return self.op

    def send_y(self, *deps):
        self.op = after(self.op, *deps)
        self.got = self.grid.over_y(self.op)
        return self.op

    def send(self, by_x):
        self.bit = self.grid.x if by_x else self.zbit
        self.got = self.grid.over_x(self.op) if by_x else self.grid.over_zpair(self.op)
        return self.op

    def first(self, token):
        self.op = after(self.got, token)
        return self.send(self.x_first)

    def second(self, token):
        self.op = join(self.op, after(self.got, token), self.bit)
        return self.send(not self.x_first)

    def third(self, token):
        self.op = join(self.op, after(self.got, token), self.bit)
        self.got = self.grid.over_c(self.op)
        return self.op

    def last(self, token):
        return after(self.got, token)


def at(a, axis, i):
    return lax.dynamic_index_in_dim(a, i, axis, keepdims=False)


class Reduce:
    def __init__(self, grid, own_a=None, oth_a=None, own_b=None, oth_b=None):
        self.grid, self.waiting = grid, {}
        self.own_a, self.oth_a, self.own_b, self.oth_b = own_a, oth_a, own_b, oth_b

    def view(self, a):
        return a.reshape(4, 2, a.shape[0] // 8, a.shape[1])

    def half(self, a, mine):
        g = self.grid
        return at(self.view(a), 1, g.x if mine else 1 - g.x).astype(F32)

    def cores(self, name, keep, send):
        self.waiting[name] = self.grid.over_c(send)
        setattr(self, "keep_" + "_".join(name), keep)
        return send

    def take(self, token):
        for name, got in self.waiting.items():
            got = [after(a, token) for a in got] if isinstance(got, list) else after(got, token)
            if isinstance(name, tuple):
                if not name[0].startswith("x_"):
                    got = (getattr(self, "keep_" + "_".join(name)).astype(F32) + got.astype(F32)).astype(BF16)
                width = got.shape[-1] // len(name)
                for i, n in enumerate(name):
                    setattr(self, n, got[..., i * width:(i + 1) * width])
            else:
                setattr(self, name, got)
        taken, self.waiting = [getattr(self, n) for name in self.waiting for n in ((name,) if isinstance(name, str) else name)], {}
        return [a for t in taken for a in (t if isinstance(t, list) else [t])]

    def a_over_y(self):
        self.waiting["back_a"] = self.grid.over_y(self.oth_a)
        return self.oth_a

    def a_over_x(self):
        op = (self.half(self.own_a, False) + self.half(self.back_a, False)).astype(BF16)
        self.waiting["x_a"] = self.grid.over_x(op)
        return op

    def b_over_x(self, which):
        op = jnp.concatenate([self.half(getattr(self, n), False).astype(BF16) for n in which], axis=-1)
        self.waiting[tuple("x_" + n for n in which)] = self.grid.over_x(op)
        return op

    def b_over_y(self):
        op = (self.half(self.oth_b, True) + self.x_oth_b.astype(F32)).astype(BF16)
        self.waiting["back_b"] = self.grid.over_y(op)
        return op

    def half_a(self):
        return (self.half(self.own_a, True) + self.half(self.back_a, True) + self.x_a.astype(F32)).astype(BF16)

    def over_z(self, *more):
        g = self.grid
        b = self.half(self.own_b, True) + self.x_own_b.astype(F32) + self.back_b.astype(F32)
        self.kept = lax.optimization_barrier(jnp.concatenate([self.half_a(), b.astype(BF16), *[m.half_a() for m in more]], axis=2))
        ops = [at(self.kept, 0, (g.z + k) % 4) for k in (1, 2, 3)]
        self.waiting["z_got"] = [g.shift_z(op, k) for k, op in zip((1, 2, 3), ops)]
        return ops

    def total(self):
        a, b, c = [p.astype(F32) for p in self.z_got]
        return (at(self.kept, 0, self.grid.z).astype(F32) + a) + (b + c)

    def ends(self):
        self.all = self.total().reshape(2, 64, -1)
        op = at(self.all, 0, 1 - self.grid.c).astype(BF16)
        self.waiting["end"] = self.grid.over_c(op)
        return op

    def result(self):
        mine, got = at(self.all, 0, self.grid.c), self.end.astype(F32)
        c = self.grid.c
        return jnp.concatenate([jnp.where(c == 0, mine, got), jnp.where(c == 0, got, mine)], axis=1)


class Small:
    def __init__(self, grid):
        self.grid = grid

    def send_y(self, own, oth):
        self.value, self.got = own, self.grid.over_y(oth)
        return oth

    def send_c(self, token):
        self.value = self.value + after(self.got, token)
        self.got = self.grid.over_c(self.value)
        return self.value

    def send_x(self, token):
        self.value = self.value + after(self.got, token)
        self.got = self.grid.over_x(self.value)
        return self.value

    def send_z(self, token):
        self.value = self.value + after(self.got, token)
        self.got = [self.grid.shift_z(self.value, k) for k in (1, 2, 3)]
        return self.value

    def total(self, token):
        z = self.grid.z
        ring = jnp.stack([self.value, *[after(g, token) for g in self.got]])
        terms = [at(ring, 0, (z - s) % 4) for s in range(4)]
        return (terms[0] + terms[1]) + (terms[2] + terms[3])


def time_embed(step, d):
    half = d // 2
    frequency = jnp.exp(-math.log(10000.0) * jnp.arange(half, dtype=F32) / half)
    angles = step.astype(F32) * frequency[None, :]
    return jnp.concatenate([jnp.sin(angles), jnp.cos(angles)], axis=-1)


def block_lists(seg_own, seg_halo, rows):
    q = seg_own.reshape(-1, BQ)
    keys = jnp.concatenate([seg_own, seg_halo]).reshape(-1, BK)
    need = (keys[None, :, 0] <= q[:, None, -1]) & (keys[None, :, -1] >= q[:, None, 0])
    need = need.astype(jnp.int32)
    nkb = keys.shape[0]
    before = jnp.sum(need[:, None, :] * (jnp.arange(nkb)[None, None, :] < jnp.arange(nkb)[None, :, None]), axis=2)
    slot = jnp.arange(nkb)[None, :, None]
    pick = need[:, None, :] * (before[:, None, :] == slot)
    lst = jnp.sum(pick * jnp.arange(nkb)[None, None, :], axis=2)
    return jnp.sum(need, axis=1).astype(jnp.int32), lst.astype(jnp.int32).reshape(-1)


def finish(output, grad_input, grad_qkv, head_bias_sum, grad_out, grad_up, up_bias_sum, grad_down, grad_vectors):
    grad_qkv = grad_qkv.reshape(grad_qkv.shape[0], 3, -1).transpose(1, 0, 2)
    return (
        output,
        grad_input,
        grad_qkv,
        head_bias_sum,
        grad_out.T,
        grad_up,
        up_bias_sum,
        grad_down.T,
        grad_vectors,
    )


def per_device_fast(
    tokens_in,
    timesteps,
    segment_ids,
    padding,
    qkv_weight,
    head_bias,
    out_weight,
    up_weight,
    up_bias,
    down_weight,
    vectors,
    cotangent,
):
    rows, d = tokens_in.shape
    assert timesteps.shape[0] == 1
    grid = Grid()
    me, halo = grid.y, MAXDOC
    core = grid.c.reshape(1).astype(jnp.int32)
    own_start = me * rows
    sub = up_weight.shape[1] // 2
    width = qkv_weight.shape[2]
    by_rows = lambda a, c, q: lax.dynamic_slice_in_dim(a, (c * 4 + q) * (a.shape[0] // 8), a.shape[0] // 8, 0)
    by_cols = lambda a, c, q: lax.dynamic_slice(a, (q * (a.shape[0] // 4), c * sub), (a.shape[0] // 4, sub))
    flat_qkv = qkv_weight.reshape(3 * d, width)

    def outer(a, c, q):
        o = by_rows(out_weight, c, q)
        return jnp.concatenate([by_rows(a, c, q), o[:, :width], o[:, width:]], axis=0)

    def split_outer(mine, theirs):
        n, m = 3 * d // 8, out_weight.shape[0] // 8
        mine, theirs = [t.reshape(4, n + 2 * m, width) for t in (mine, theirs)]
        cols = [join(mine[:, a:b].reshape(-1, width), theirs[:, a:b].reshape(-1, width), grid.c) for a, b in ((0, n), (n, n + m), (n + m, n + 2 * m))]
        return cols[0].reshape(qkv_weight.shape), jnp.concatenate(cols[1:], axis=1)

    fq = Fetch(grid, flat_qkv, False, outer)
    fu = Fetch(grid, up_weight, False, by_cols)
    fd = Fetch(grid, down_weight, True, by_rows)
    small_w = jnp.concatenate([head_bias.reshape(-1), up_bias])
    small_o = grid.over_y(small_w)
    fq.prepare()
    begin = [fq.send_y(), small_w]

    emb = time_embed(timesteps[:, None], d)
    seg, pad = segment_ids[0], padding[0]
    seg_own = lax.dynamic_slice_in_dim(seg, own_start, rows)
    pad_own = lax.dynamic_slice_in_dim(pad, own_start, rows)
    halo_start = jnp.where(me == 0, rows, own_start - halo)
    seg_halo = lax.dynamic_slice_in_dim(seg, halo_start, halo)
    pad_halo = lax.dynamic_slice_in_dim(pad, halo_start, halo)
    code = jnp.concatenate([jnp.where(pad_own == 0, seg_own, -1), jnp.where(pad_halo == 0, seg_halo, -1)])
    cnt, lst = block_lists(seg_own, seg_halo, rows)
    nkb = (rows + halo) // BK
    segq_row, code_col = seg_own[None, :], code[:, None]
    nb = head_bias.size

    far_blocks = (rows - halo) // BQ
    far = jnp.where(me == 0, 0, rows // BQ - far_blocks).reshape(1).astype(jnp.int32)
    near = jnp.where(me == 0, far_blocks, 0).reshape(1).astype(jnp.int32)
    zero = jnp.zeros((1,), jnp.int32)
    x_own, q0, k0, v0 = qkv_own(tokens_in, emb, qkv_weight, head_bias, deps=begin)
    ops = [fq.first(k0)]
    edge = jnp.where(me == 0, rows - halo, 0)
    halo_op = lax.dynamic_slice_in_dim(after(tokens_in, ops[0]), edge, halo, 0)
    halo_tok = grid.over_y(halo_op)
    part = attn_fwd(far, far_blocks, cnt, lst, nkb, q0, [k0], [v0], segq_row, code_col, deps=[*ops, halo_op])
    ops = [fq.second(part[1]), fu.prepare(part[1]), fd.prepare(part[1])]
    x_halo, kh0, vh0 = kv_halo(after(halo_tok, part[1]), emb, qkv_weight, head_bias, deps=ops)
    ops = [fq.third(kh0), fu.send_y(kh0), fd.send_y(kh0)]
    o0, lse0 = attn_fwd(near, rows // BQ - far_blocks, cnt, lst, nkb, q0, [k0, kh0], [v0, vh0], segq_row, code_col, into=part, deps=ops)
    small_o = after(small_o, lse0)
    hb_o, up_b_o = small_o[:nb].reshape(head_bias.shape), small_o[nb:].reshape(1, -1)
    qkv_o, out_o = split_outer(fq.op, fq.last(lse0))
    out_ws = [out_weight, out_o]
    _, q1, k1, v1 = qkv_own(tokens_in, emb, qkv_o, hb_o)
    _, kh1, vh1 = kv_halo(halo_tok, emb, qkv_o, hb_o, deps=[q1])
    ops = [fu.first(kh1), fd.first(kh1)]
    o1, lse1 = attn_fwd(zero, rows // BQ, cnt, lst, nkb, q1, [k1, kh1], [v1, vh1], segq_row, code_col, deps=ops)
    ops = [fu.second(lse1), fd.second(lse1)]
    xhat1, normed, rstd1 = out_norm(tokens_in, emb, vectors, [o0, o1], out_ws, deps=ops)
    up_b = up_bias.reshape(1, -1)
    (a0, b0), (ga0, gb0) = ffn_up(core, normed, [(up_weight, 0, up_b, 0), (up_weight, 1, up_b, 1)], sub)
    ops = [fu.third(ga0), fd.third(ga0)]
    b0_got, normed_got = grid.over_c(b0), grid.over_c(normed)
    (a1,), (ga1,) = ffn_up(core, normed, [(fu.op, None, up_b_o, 0)], sub, deps=ops)
    up_b1, down_b1 = fu.last(ga1), fd.last(ga1)
    (b1,), (gb1,) = ffn_up(core, normed, [(up_b1, None, up_b_o, 1)], sub, deps=[ga1])
    b1_got = grid.over_c(b1)
    output, d_down, sums2 = ffn_down(
        core, normed, cotangent, vectors, [a0, b0, a1, b1], [(down_weight, 0), (down_weight, 1), (fd.op, None), (down_b1, None)]
    )

    d_got = grid.over_c(d_down)
    dn1, (ua1, ub1), us1 = ffn_dup(core, d_down, [(fu.op, None, fd.op, None, ga1), (up_b1, None, down_b1, None, gb1)], sub)
    ub1_got = grid.over_c(ub1)
    gd1, gd0 = wide_grad([d_down, after(d_got, ua1)], [(a1, after(b1_got, d_down)), (a0, after(b0_got, d_down))], deps=[ua1])
    rd = Reduce(grid, gd0[0], gd1[0], gd0[1], gd1[1])
    both = ("own_b", "oth_b")
    ops = [rd.a_over_y(), rd.b_over_x(both)]
    dn0, (ua0, ub0), us0 = ffn_dup(core, d_down, [(up_weight, 0, down_weight, 0, ga0), (up_weight, 1, down_weight, 1, gb0)], sub, deps=ops)
    ub0_got = grid.over_c(ub0)
    got = rd.take(dn0)
    d_attn, sums1, dm0, dm1 = norm_bwd([d_down, dn1, dn0], xhat1, rstd1, vectors, out_ws)
    ops = [rd.a_over_x(), rd.b_over_y(), *got]
    *og, os = grad_tn(core, [d_attn], [o0, o1], deps=[sums1, *ops])
    ro = Reduce(grid)
    ops = [ro.cores(("own_a", "oth_a"), *og)]
    gu1, gu0 = wide_grad([normed, after(normed_got, sums1)], [(ua1, after(ub1_got, sums1)), (ua0, after(ub0_got, sums1))], deps=ops)
    ru = Reduce(grid, gu0[0], gu1[0], gu0[1], gu1[1])
    got = rd.take(gu0[1]) + ro.take(gu0[1])
    ops = [*rd.over_z(), ru.a_over_y(), ru.b_over_x(both), *got]
    dqkv1 = attn_bwd(cnt, lst, nkb, q1, [k1, kh1], [v1, vh1], dm1, o1, lse1, segq_row, code_col, deps=ops)
    got = rd.take(dqkv1[0]) + ru.take(dqkv1[0])
    ops = [ru.a_over_x(), ru.b_over_y(), rd.ends(), *got]
    rq = Reduce(grid)
    *qg1, hs1 = grad_tn(core, [x_own, x_halo], dqkv1, deps=ops)
    got = ru.take(hs1) + rd.take(hs1)
    grad_down = rd.result()
    rq.cores(("oth_a", "oth_b"), *qg1)
    got += rq.take(hs1)
    ops = [rq.a_over_y(), rq.b_over_x(("oth_b",)), *ru.over_z(), ro.a_over_y(), grad_down, *got]
    dqkv0 = attn_bwd(cnt, lst, nkb, q0, [k0, kh0], [v0, vh0], dm0, o0, lse0, segq_row, code_col, deps=ops)
    got = rq.take(dqkv0[0]) + ru.take(dqkv0[0]) + ro.take(dqkv0[0])
    ops = [rq.b_over_y(), ro.a_over_x(), ru.ends(), *got]
    *qg0, hs0 = grad_tn(core, [x_own, x_halo], dqkv0, deps=ops)
    got = rq.take(hs0) + ru.take(hs0) + ro.take(hs0)
    grad_up = ru.result()
    vec6 = jnp.concatenate([sums1[:2], sums2[:2], sums1[2:3], sums2[2:3]], axis=0)
    up_sum = lambda us: jnp.where(grid.c == 0, jnp.concatenate(us, axis=0), jnp.concatenate(us[::-1], axis=0))
    head_sum = lambda hs: hs.reshape(3, -1)[0::2].reshape(1, -1)
    small = Small(grid)
    ops = [
        rq.cores(("own_a", "own_b"), *qg0),
        small.send_y(*[jnp.concatenate([vec6, up_sum(us), head_sum(hs)], axis=0) for us, hs in ((us0, hs0), (us1, hs1))]),
        grad_up, *got,
    ]
    pairs = [(g[c], w, c) for g, w in ((dqkv0, qkv_weight), (dqkv1, qkv_o)) for c in range(3)]
    kv_pairs = [(g, (w, c)) for g, w, c in pairs if c]
    halo_grad = in_grad(None, [g for g, _ in kv_pairs], [w for _, w in kv_pairs], rows, halo, deps=ops)
    got = rq.take(halo_grad)
    back = grid.over_y(halo_grad)
    ops = [rq.a_over_x(), rq.b_over_x(("own_b",)), small.send_c(halo_grad), halo_grad, *got]
    own_grad = in_grad(d_attn, [g for g, _, _ in pairs], [(w, c) for _, w, c in pairs], 0, rows, deps=ops)
    rq.take(own_grad)
    rq.over_z(ro)
    rq.take(own_grad)
    small.send_x(own_grad)
    small.send_z(own_grad)
    near_rows = (jnp.arange(rows // halo) == 1 - me)[:, None, None]
    back = after(back, own_grad).astype(F32)
    grad_input = (own_grad.reshape(rows // halo, halo, d).astype(F32) + jnp.where(near_rows, back[None], 0.0)).astype(BF16).reshape(rows, d)
    total = rq.total()
    small = small.total(total)
    qkv_cols = 3 * width
    return finish(
        output, grad_input, total[:, :qkv_cols], small[8:].reshape(2, -1), total[:, qkv_cols:], grad_up,
        small[6:8].reshape(-1), grad_down, small[:6],
    )


def per_device(
    mp_size,
    tokens_in,
    timesteps,
    segment_ids,
    padding,
    qkv_weight,
    head_bias,
    out_weight,
    up_weight,
    up_bias,
    down_weight,
    vectors,
    cotangent,
):
    rows, d = tokens_in.shape
    assert timesteps.shape[0] == 1
    me = lax.axis_index("mp")
    own_start = me * rows
    emb = time_embed(timesteps[:, None], d)
    seg, pad = segment_ids[0], padding[0]
    seg_own = lax.dynamic_slice_in_dim(seg, own_start, rows)
    pad_own = lax.dynamic_slice_in_dim(pad, own_start, rows)
    halo_tok = lax.all_gather(tokens_in, "mp", axis=0, tiled=True)
    place = jnp.arange(SEQ, dtype=jnp.int32)
    pad_halo = jnp.where((place >= own_start) & (place < own_start + rows), 1, pad)
    code = jnp.concatenate([jnp.where(pad_own == 0, seg_own, -1), jnp.where(pad_halo == 0, seg, -1)])
    cnt, lst = block_lists(seg_own, seg, rows)
    nkb = (rows + SEQ) // BK
    segq_row, code_col = seg_own[None, :], code[:, None]
    gather = lambda a, axis: lax.all_gather(a, "mp", axis=axis, tiled=True)
    qkv_w, out_w, up_w, down_w = gather(qkv_weight, 2), gather(out_weight, 0), gather(up_weight, 1), gather(down_weight, 0)
    hb, up_b = gather(head_bias, 1), gather(up_bias, 0).reshape(1, -1)

    x_own, q, k, v = qkv_own(tokens_in, emb, qkv_w, hb)
    x_halo, kh, vh = kv_halo(halo_tok, emb, qkv_w, hb)
    k, v = [k, kh], [v, vh]
    o, lse = attn_fwd(jnp.zeros((1,), jnp.int32), rows // BQ, cnt, lst, nkb, q, k, v, segq_row, code_col)
    xhat1, normed, rstd1 = out_norm(tokens_in, emb, vectors, [o], [out_w])
    core, hidden = jnp.zeros((1,), jnp.int32), up_w.shape[1]
    acts, gps = ffn_up(core, normed, [(up_w, None, up_b, None)], hidden)
    output, d_down, sums2 = ffn_down(core, normed, cotangent, vectors, acts, [(down_w, None)])

    dn, dups, (up_sum,) = ffn_dup(core, d_down, [(up_w, None, down_w, None, gps[0])], hidden)
    grad_up = jnp.concatenate(wide_grad([normed], [dups])[0], axis=1)
    grad_down = jnp.concatenate(wide_grad([d_down], [acts])[0], axis=1)
    d_attn, sums1, d_mixed = norm_bwd([d_down, dn], xhat1, rstd1, vectors, [out_w])
    grad_out, _ = grad_tn(None, [d_attn], [o])
    d_qkv = attn_bwd(cnt, lst, nkb, q, k, v, d_mixed, o, lse, segq_row, code_col)
    grad_qkv, head_sum = grad_tn(None, [x_own, x_halo], d_qkv)
    halo_grad = in_grad(None, d_qkv[1:], [(qkv_w, 1), (qkv_w, 2)], rows, SEQ)
    own_grad = in_grad(d_attn, d_qkv, [(qkv_w, c) for c in range(3)], 0, rows)
    back = lax.psum_scatter(halo_grad, "mp", scatter_dimension=0, tiled=True)
    grad_input = (own_grad.astype(F32) + back.astype(F32)).astype(BF16)

    packed = [sums1[:2], sums2[:2], sums1[2:3], sums2[2:3], head_sum.reshape(3, -1)[0::2], up_sum.reshape(-1, d)]
    packed = lax.psum(jnp.concatenate(packed, axis=0), ("dp", "mp"))
    local = head_bias.shape[1]
    head_bias_sum = lax.dynamic_slice_in_dim(packed[6:8], me * local, local, 1)
    local = up_bias.shape[0]
    up_bias_sum = lax.dynamic_slice_in_dim(packed[8:].reshape(-1), me * local, local, 0)

    def scatter(g, groups):
        n = g.shape[1] // groups // mp_size
        g = lax.psum_scatter(g, "dp", scatter_dimension=0, tiled=True)
        g = g.reshape(-1, groups, mp_size, n).transpose(2, 0, 1, 3)
        return lax.psum_scatter(g, "mp", scatter_dimension=0, tiled=False).astype(F32).reshape(-1, groups * n)

    return finish(
        output,
        grad_input,
        scatter(grad_qkv, 3),
        head_bias_sum,
        scatter(grad_out, 1),
        scatter(grad_up, 1),
        up_bias_sum,
        scatter(grad_down, 1),
        packed[:6],
    )


def solution(mesh):
    fast = dict(mesh.shape) == {"dp": 16, "mp": 2}
    return jax.shard_map(
        per_device_fast if fast else partial(per_device, mesh.shape["mp"]),
        mesh=mesh,
        in_specs=(
            P(("dp", "mp"), None),
            P("dp"),
            P("dp", None),
            P("dp", None),
            P(None, None, "mp"),
            P(None, "mp"),
            P("mp", None),
            P(None, "mp"),
            P("mp"),
            P("mp", None),
            P(),
            P(("dp", "mp"), None),
        ),
        out_specs=(
            P(("dp", "mp"), None),
            P(("dp", "mp"), None),
            P(None, "dp", "mp"),
            P(None, "mp"),
            P("mp", "dp"),
            P("dp", "mp"),
            P("mp"),
            P("mp", "dp"),
            P(),
        ),
        check_vma=False,
    )
```

```python
from functools import partial
import math

import jax
import jax.numpy as jnp
from jax import lax
from jax.experimental import pallas as pl
from jax.experimental.pallas import tpu as pltpu
from jax.sharding import PartitionSpec as P

HEAD_DIM = 64
SEQ = 2048
MAXDOC = 512
BQ = 256
BK = 256
RB = 256
HB = 512
SCALE = 300.0
VMEM_MIB = {
    "qkv_own": 12, "kv_halo": 12, "attn_fwd": 12, "out_norm": 14, "ffn_up": 20, "ffn_down": 24,
    "ffn_dup": 25, "wide_grad": 24, "norm_bwd": 14, "grad_tn": 16, "attn_bwd": 18, "in_grad": 14,
}
LIMITED = [True]
GROUP = 512
NEG_FILL = -1e30
F32 = jnp.float32
BF16 = jnp.bfloat16


def nt(a, b):
    return lax.dot_general(a, b, (((1,), (1,)), ((), ())), preferred_element_type=F32)


def nn(a, b):
    return lax.dot_general(a, b, (((1,), (0,)), ((), ())), preferred_element_type=F32)


def tn(a, b):
    return lax.dot_general(a, b, (((0,), (0,)), ((), ())), preferred_element_type=F32)


def cost(flops, nbytes, trans=0):
    return pl.CostEstimate(flops=int(flops * SCALE), bytes_accessed=int(nbytes * SCALE), transcendentals=int(trans * SCALE))


def whole(shape):
    return pl.BlockSpec(shape, lambda *_: (0,) * len(shape))


def sds(shape, dtype):
    return jax.ShapeDtypeStruct(shape, dtype)


def call(kernel, args, *, grid, in_specs, out_specs, out_shape, cost_estimate, name, prefetch=(), deps=(), scratch=(), aliases=None):
    first, skip, offset = len(prefetch) + len(args), len(deps), len(prefetch)

    def body(*refs):
        kernel(*refs[:first], *refs[first + skip:])

    return pl.pallas_call(
        body,
        grid_spec=pltpu.PrefetchScalarGridSpec(
            num_scalar_prefetch=offset,
            grid=grid,
            in_specs=list(in_specs) + [pl.BlockSpec(memory_space=pl.ANY)] * skip,
            out_specs=out_specs,
            scratch_shapes=list(scratch),
        ),
        out_shape=out_shape,
        input_output_aliases={k + offset: v for k, v in (aliases or {}).items()},
        cost_estimate=cost_estimate,
        compiler_params=pltpu.CompilerParams(vmem_limit_bytes=VMEM_MIB[name] << 20) if LIMITED[0] else None,
        name=name,
    )(*prefetch, *args, *deps)


def after(x, *deps):
    return lax.optimization_barrier((x, *deps))[0] if deps else x


def qkv_own_kernel(tok_ref, emb_ref, w_ref, hb_ref, x_ref, q_ref, k_ref, v_ref):
    x = (tok_ref[...].astype(F32) + emb_ref[...]).astype(BF16)
    x_ref[...] = x
    q_ref[...] = (nn(x, w_ref[0]) + hb_ref[0:1]).astype(BF16)
    k_ref[...] = nn(x, w_ref[1]).astype(BF16)
    v_ref[...] = (nn(x, w_ref[2]) + hb_ref[1:2]).astype(BF16)


def qkv_own(tok, emb, w, hb, deps=()):
    rows, d = tok.shape
    width = w.shape[2]
    row = lambda n: pl.BlockSpec((RB, n), lambda i, *_: (i, 0))
    return call(
        qkv_own_kernel,
        (tok, emb, w, hb),
        deps=deps,
        grid=(rows // RB,),
        in_specs=[row(d), whole((1, d)), whole(w.shape), whole(hb.shape)],
        out_specs=[row(d), row(width), row(width), row(width)],
        out_shape=[sds((rows, d), BF16)] + [sds((rows, width), BF16)] * 3,
        cost_estimate=cost(6 * rows * d * width, 2 * (2 * rows * d + 3 * rows * width + 3 * d * width)),
        name="qkv_own",
    )


def kv_halo_kernel(tok_ref, emb_ref, w_ref, hb_ref, x_ref, k_ref, v_ref):
    x = (tok_ref[...].astype(F32) + emb_ref[...]).astype(BF16)
    x_ref[...] = x
    k_ref[...] = nn(x, w_ref[1]).astype(BF16)
    v_ref[...] = (nn(x, w_ref[2]) + hb_ref[1:2]).astype(BF16)


def kv_halo(tok, emb, w, hb, deps=()):
    rows, d = tok.shape
    width = w.shape[2]
    row = lambda n: pl.BlockSpec((RB, n), lambda i, *_: (i, 0))
    return call(
        kv_halo_kernel,
        (tok, emb, w, hb),
        deps=deps,
        grid=(rows // RB,),
        in_specs=[row(d), whole((1, d)), whole(w.shape), whole(hb.shape)],
        out_specs=[row(d), row(width), row(width)],
        out_shape=[sds((rows, d), BF16)] + [sds((rows, width), BF16)] * 2,
        cost_estimate=cost(4 * rows * d * width, 2 * (2 * rows * d + 2 * rows * width + 3 * d * width)),
        name="kv_halo",
    )


def pair_stack(x2):
    lane = lax.broadcasted_iota(jnp.int32, (1, 128), 1)
    first = (lane < HEAD_DIM).astype(F32).astype(BF16)
    second = (lane >= HEAD_DIM).astype(F32).astype(BF16)
    return jnp.concatenate([x2 * first, x2 * second], axis=0)


def pair_merge(x):
    half = x.shape[0] // 2
    lane = lax.broadcasted_iota(jnp.int32, (half, 128), 1)
    return jnp.where(lane < HEAD_DIM, x[:half], x[half:])


def load_keys(srcs, dsts, sem, group):
    copies = []
    for pieces, dst in zip(srcs, dsts):
        off = 0
        for src in pieces:
            cols = pl.ds(pl.multiple_of(group * GROUP, GROUP), GROUP)
            copies.append(pltpu.make_async_copy(src.at[:, cols], dst.at[off:off + src.shape[0], :], sem.at[len(copies)]))
            off += src.shape[0]
    for c in copies:
        c.start()
    for c in copies:
        c.wait()


def attn_fwd_kernel(pieces, nkb, pairs, filled, base_ref, cnt_ref, list_ref, q_ref, segq_ref, codek_ref, *refs):
    k_srcs, v_srcs, refs = refs[:pieces], refs[pieces:2 * pieces], refs[2 * pieces + 2 * filled:]
    o_ref, lse_ref, k_ref, v_ref, qs_scr, m_scr, l_scr, acc_scr, sem = refs

    @pl.when(pl.program_id(1) == 0)
    def _():
        load_keys((k_srcs, v_srcs), (k_ref, v_ref), sem, pl.program_id(0))

    qb = pl.program_id(1) + base_ref[0]
    count = cnt_ref[qb]
    for p in range(pairs):
        qs_scr[p] = pair_stack(q_ref[:, 128 * p:128 * (p + 1)] * jnp.asarray(0.125, BF16))
    m_scr[...] = jnp.full(m_scr.shape, -3e38, F32)
    l_scr[...] = jnp.zeros(l_scr.shape, F32)
    acc_scr[...] = jnp.zeros(acc_scr.shape, F32)

    def step(s, carry):
        kb = list_ref[qb * nkb + s]
        off = pl.multiple_of(kb * BK, BK)
        kpos = kb * BK + lax.broadcasted_iota(jnp.int32, (BK, BQ), 0)
        qpos = qb * BQ + lax.broadcasted_iota(jnp.int32, (BK, BQ), 1)
        live = (codek_ref[pl.ds(off, BK), :] == segq_ref[...]) | (qpos == kpos)
        bias = jnp.where(live, 0.0, NEG_FILL).astype(F32)
        bias = jnp.concatenate([bias, bias], axis=1)
        scs = [nt(k_ref[pl.ds(off, BK), 128 * p:128 * (p + 1)], qs_scr[p]) for p in range(pairs)]
        es = []
        for p in range(pairs):
            sc = scs[p] + bias
            old = m_scr[p:p + 1]
            new = jnp.maximum(old, jnp.max(sc, axis=0, keepdims=True))
            e = jnp.exp(sc - new)
            fade = jnp.exp(old - new)
            m_scr[p:p + 1] = new
            l_scr[p:p + 1] = l_scr[p:p + 1] * fade + jnp.sum(e, axis=0, keepdims=True)
            es.append((e.astype(BF16), fade))
        for p in range(pairs):
            acc_scr[p] = acc_scr[p] * es[p][1] + tn(v_ref[pl.ds(off, BK), 128 * p:128 * (p + 1)], es[p][0])
        return carry

    lax.fori_loop(0, count, step, 0)
    lse = m_scr[...] + jnp.log(l_scr[...])
    for p in range(pairs):
        o = acc_scr[p] / l_scr[p:p + 1]
        o = jnp.concatenate([o[:HEAD_DIM, :BQ], o[HEAD_DIM:, BQ:]], axis=0)
        o_ref[:, 128 * p:128 * (p + 1)] = jnp.transpose(o).astype(BF16)
        lse_ref[2 * p:2 * p + 1, :] = lse[p:p + 1, :BQ]
        lse_ref[2 * p + 1:2 * p + 2, :] = lse[p:p + 1, BQ:]


def attn_fwd(base, nqb, cnt, lst, nkb, q, k, v, segq, codek, into=(), deps=()):
    rows, width = q.shape
    pieces, keys = len(k), sum(a.shape[0] for a in k)
    groups, pairs = width // GROUP, GROUP // 128
    est = nqb * BQ * 2 * BK * width
    qspec = lambda n: pl.BlockSpec((BQ, n), lambda g, i, b, *_: (i + b[0], g))
    lspec = pl.BlockSpec((2 * pairs, BQ), lambda g, i, b, *_: (g, i + b[0]))
    anyspec = pl.BlockSpec(memory_space=pl.ANY)
    args = [q, segq, codek, *k, *v, *into]
    first = 3 + 2 * pieces
    return call(
        partial(attn_fwd_kernel, pieces, nkb, pairs, len(into) // 2),
        args,
        prefetch=(base, cnt, lst),
        deps=deps,
        grid=(groups, nqb),
        in_specs=[qspec(GROUP), pl.BlockSpec((1, BQ), lambda g, i, b, *_: (0, i + b[0])), pl.BlockSpec((codek.shape[0], 1), lambda *_: (0, 0))]
        + [anyspec] * (len(args) - 3),
        out_specs=[qspec(GROUP), lspec],
        out_shape=[sds((rows, width), BF16), sds((2 * pairs * groups, rows), F32)],
        aliases={first: 0, first + 1: 1} if into else None,
        scratch=[
            pltpu.VMEM((keys, GROUP), BF16),
            pltpu.VMEM((keys, GROUP), BF16),
            pltpu.VMEM((pairs, 2 * BQ, 128), BF16),
            pltpu.VMEM((pairs, 2 * BQ), F32),
            pltpu.VMEM((pairs, 2 * BQ), F32),
            pltpu.VMEM((pairs, 128, 2 * BQ), F32),
            pltpu.SemaphoreType.DMA((2 * pieces,)),
        ],
        cost_estimate=cost(4 * est, 8 * rows * width, est // 32),
        name="attn_fwd",
    )


def attn_bwd_kernel(pieces, nkb, pairs, cnt_ref, list_ref, q_ref, do_ref, o_ref, lse_ref, segq_ref, codek_ref, *refs):
    k_srcs, v_srcs, refs = refs[:pieces], refs[pieces:2 * pieces], refs[2 * pieces:]
    dq_ref, dk_ref, dv_ref, k_ref, v_ref, qs_scr, ds_scr, row_scr, dq_scr, dk_scr, dv_scr, sem = refs
    qb = pl.program_id(1)

    @pl.when(qb == 0)
    def _():
        load_keys((k_srcs, v_srcs), (k_ref, v_ref), sem, pl.program_id(0))

    @pl.when(qb == 0)
    def _():
        dk_scr[...] = jnp.zeros(dk_scr.shape, F32)
        dv_scr[...] = jnp.zeros(dv_scr.shape, F32)

    count = cnt_ref[qb]
    lse_t = lse_ref[...]
    for p in range(pairs):
        cols = slice(128 * p, 128 * (p + 1))
        qs_scr[p] = pair_stack(q_ref[:, cols] * jnp.asarray(0.125, BF16))
        ds_scr[p] = pair_stack(do_ref[:, cols])
        prod = jnp.transpose(do_ref[:, cols].astype(F32) * o_ref[:, cols].astype(F32))
        da = jnp.sum(prod[:HEAD_DIM], axis=0, keepdims=True)
        db = jnp.sum(prod[HEAD_DIM:], axis=0, keepdims=True)
        row_scr[p, 0:1] = jnp.concatenate([lse_t[2 * p:2 * p + 1], lse_t[2 * p + 1:2 * p + 2]], axis=1)
        row_scr[p, 1:2] = jnp.concatenate([da, db], axis=1)
    dq_scr[...] = jnp.zeros(dq_scr.shape, F32)

    def step(s, carry):
        kb = list_ref[qb * nkb + s]
        off = pl.multiple_of(kb * BK, BK)
        kpos = kb * BK + lax.broadcasted_iota(jnp.int32, (BK, BQ), 0)
        qpos = qb * BQ + lax.broadcasted_iota(jnp.int32, (BK, BQ), 1)
        live = (codek_ref[pl.ds(off, BK), :] == segq_ref[...]) | (qpos == kpos)
        bias = jnp.where(live, 0.0, NEG_FILL).astype(F32)
        bias = jnp.concatenate([bias, bias], axis=1)
        for p in range(pairs):
            cols = slice(128 * p, 128 * (p + 1))
            k2 = k_ref[pl.ds(off, BK), cols]
            v2 = v_ref[pl.ds(off, BK), cols]
            sc = nt(k2, qs_scr[p]) + bias
            probs = jnp.exp(sc - row_scr[p, 0:1])
            dprobs = nt(v2, ds_scr[p])
            dsc = (probs * (dprobs - row_scr[p, 1:2])).astype(BF16)
            dv_scr[pl.ds(off, BK), cols] += nn(probs.astype(BF16), ds_scr[p])
            dk_scr[pl.ds(off, BK), cols] += nn(dsc, qs_scr[p])
            dq_scr[p] += tn(k2, dsc)
        return carry

    lax.fori_loop(0, count, step, 0)
    for p in range(pairs):
        dq = dq_scr[p] * 0.125
        dq = jnp.concatenate([dq[:HEAD_DIM, :BQ], dq[HEAD_DIM:, BQ:]], axis=0)
        dq_ref[:, 128 * p:128 * (p + 1)] = jnp.transpose(dq).astype(BF16)

    @pl.when(qb == pl.num_programs(1) - 1)
    def _():
        dk_ref[...] = dk_scr[...].astype(BF16)
        dv_ref[...] = dv_scr[...].astype(BF16)


def attn_bwd(cnt, lst, nkb, q, k, v, do, o, lse, segq, codek, deps=()):
    rows, width = q.shape
    pieces, keys = len(k), sum(a.shape[0] for a in k)
    groups, pairs = width // GROUP, GROUP // 128
    est = rows * 2 * BK * width
    qspec = pl.BlockSpec((BQ, GROUP), lambda g, i, *_: (i, g))
    kspec = pl.BlockSpec((keys, GROUP), lambda g, i, *_: (0, g))
    return call(
        partial(attn_bwd_kernel, pieces, nkb, pairs),
        (q, do, o, lse, segq, codek, *k, *v),
        prefetch=(cnt, lst),
        deps=deps,
        grid=(groups, rows // BQ),
        in_specs=[
            qspec, qspec, qspec,
            pl.BlockSpec((2 * pairs, BQ), lambda g, i, *_: (g, i)),
            pl.BlockSpec((1, BQ), lambda g, i, *_: (0, i)),
            pl.BlockSpec((keys, 1), lambda g, i, *_: (0, 0)),
        ] + [pl.BlockSpec(memory_space=pl.ANY)] * (2 * pieces),
        out_specs=[qspec, kspec, kspec],
        scratch=[
            pltpu.VMEM((keys, GROUP), BF16),
            pltpu.VMEM((keys, GROUP), BF16),
            pltpu.VMEM((pairs, 2 * BQ, 128), BF16),
            pltpu.VMEM((pairs, 2 * BQ, 128), BF16),
            pltpu.VMEM((pairs, 8, 2 * BQ), F32),
            pltpu.VMEM((pairs, 128, 2 * BQ), F32),
            pltpu.VMEM((keys, GROUP), F32),
            pltpu.VMEM((keys, GROUP), F32),
            pltpu.SemaphoreType.DMA((2 * pieces,)),
        ],
        out_shape=[sds((rows, width), BF16), sds((keys, width), BF16), sds((keys, width), BF16)],
        cost_estimate=cost(10 * est, 16 * rows * width, est // 32),
        name="attn_bwd",
    )


def row_mean(x):
    return jnp.mean(x, axis=-1, keepdims=True)


def out_norm_kernel(parts, tok_ref, emb_ref, vec_ref, *refs):
    mixed, weights = refs[:parts], refs[parts:2 * parts]
    xhat_ref, low_ref, rstd_ref = refs[2 * parts:]
    acc = tok_ref[...].astype(F32) + emb_ref[...] + vec_ref[4:5]
    for m, w in zip(mixed, weights):
        acc = acc + nn(m[...], w[...])
    centered = acc - row_mean(acc)
    rstd = lax.rsqrt(row_mean(centered * centered) + 1e-05)
    xhat = centered * rstd
    xhat_ref[...] = xhat.astype(BF16)
    rstd_ref[...] = jnp.broadcast_to(rstd, rstd_ref.shape)
    low_ref[...] = (xhat * vec_ref[0:1] + vec_ref[1:2]).astype(BF16)


def out_norm(tok, emb, vec, mixed, weights, deps=()):
    rows, d = tok.shape
    parts = len(mixed)
    row = lambda n: pl.BlockSpec((RB, n), lambda i, *_: (i, 0))
    return call(
        partial(out_norm_kernel, parts),
        (tok, emb, vec, *mixed, *weights),
        deps=deps,
        grid=(rows // RB,),
        in_specs=[row(d), whole((1, d)), whole(vec.shape)]
        + [row(m.shape[1]) for m in mixed]
        + [whole(w.shape) for w in weights],
        out_specs=[row(d), row(d), row(128)],
        out_shape=[sds((rows, d), BF16), sds((rows, d), BF16), sds((rows, 128), F32)],
        cost_estimate=cost(2 * rows * d * d, 8 * rows * d + 2 * d * d),
        name="out_norm",
    )


def gelu_pair(h):
    mag = jnp.abs(h)
    t = 1.0 / (1.0 + (0.3275911 * 0.7071067811865476) * mag)
    e = jnp.exp(-0.5 * (h * h))
    poly = t * (0.127414796 + t * (-0.142248368 + t * (0.7107068705 + t * (-0.7265760135 + t * 0.5307027145))))
    tail = poly * e
    phi = jnp.where(h < 0.0, tail, 1.0 - tail)
    return h * phi, phi + h * (e * 0.3989422804014327)


def pick(sel, per):
    if sel is None:
        return lambda j, core: j
    return lambda j, core: j + per * (core[0] if sel == 0 else 1 - core[0])


def ffn_up_kernel(n, core_ref, x_ref, *refs):
    ws, bs, acts, gps = refs[:n], refs[n:2 * n], refs[2 * n:3 * n], refs[3 * n:]
    rows = min(x_ref.shape[0], 512)

    def chunk(i, carry):
        at_rows = pl.ds(pl.multiple_of(i * rows, rows), rows)
        for w, b, a, g in zip(ws, bs, acts, gps):
            h = nn(x_ref[at_rows, :], w[...]) + b[...]
            act, gp = gelu_pair(h)
            a[at_rows, :] = act.astype(BF16)
            g[at_rows, :] = gp.astype(BF16)
        return carry

    lax.fori_loop(0, x_ref.shape[0] // rows, chunk, 0)


def ffn_up(core, x, items, hidden, deps=()):
    rows, d = x.shape
    n, per = len(items), hidden // HB
    col = lambda r, sel: pl.BlockSpec((r, HB), lambda j, c: (0, pick(sel, per)(j, c)))
    out = call(
        partial(ffn_up_kernel, n),
        (x, *[i[0] for i in items], *[i[2] for i in items]),
        prefetch=(core,),
        deps=deps,
        grid=(per,),
        in_specs=[whole((rows, d))] + [col(d, i[1]) for i in items] + [col(1, i[3]) for i in items],
        out_specs=[col(rows, None)] * (2 * n),
        out_shape=[sds((rows, hidden), BF16)] * (2 * n),
        cost_estimate=cost(2 * rows * d * hidden * n, 2 * (rows * d + n * (d + 2 * rows) * hidden), rows * hidden * n),
        name="ffn_up",
    )
    return out[:n], out[n:]


def ffn_down_kernel(parts, core_ref, norm_ref, cot_ref, vec_ref, *refs):
    acts, weights = refs[:parts], refs[parts:2 * parts]
    out_ref, dlow_ref, sums_ref = refs[2 * parts:]
    acc = norm_ref[...].astype(F32) + vec_ref[5:6]
    for a, w in zip(acts, weights):
        acc = acc + nn(a[...], w[...])
    centered = acc - row_mean(acc)
    rstd = lax.rsqrt(row_mean(centered * centered) + 1e-05)
    xhat = centered * rstd
    out_ref[...] = (xhat * vec_ref[2:3] + vec_ref[3:4]).astype(BF16)
    cot = cot_ref[...].astype(F32)
    gg = cot * vec_ref[2:3]
    dres = rstd * (gg - row_mean(gg) - xhat * row_mean(gg * xhat))
    low = dres.astype(BF16)
    dlow_ref[...] = low

    @pl.when(pl.program_id(0) == 0)
    def _():
        sums_ref[...] = jnp.zeros(sums_ref.shape, F32)

    sums_ref[0:1] += jnp.sum(cot * xhat, axis=0, keepdims=True)
    sums_ref[1:2] += jnp.sum(cot, axis=0, keepdims=True)
    sums_ref[2:3] += jnp.sum(low.astype(F32), axis=0, keepdims=True)


def ffn_down(core, normed, cot, vec, acts, weights, deps=()):
    rows, d = normed.shape
    parts = len(acts)
    hidden = sum(a.shape[1] for a in acts)
    row = lambda n: pl.BlockSpec((RB, n), lambda i, *_: (i, 0))
    wspec = lambda a, sel: pl.BlockSpec((a.shape[1], d), lambda i, c: (pick(sel, 1)(0, c), 0))
    return call(
        partial(ffn_down_kernel, parts),
        (normed, cot, vec, *acts, *[w for w, _ in weights]),
        prefetch=(core,),
        deps=deps,
        grid=(rows // RB,),
        in_specs=[row(d), row(d), whole(vec.shape)]
        + [row(a.shape[1]) for a in acts]
        + [wspec(a, sel) for a, (_, sel) in zip(acts, weights)],
        out_specs=[row(d), row(d), whole((8, d))],
        out_shape=[sds((rows, d), BF16), sds((rows, d), BF16), sds((8, d), F32)],
        cost_estimate=cost(2 * rows * d * hidden, 8 * rows * d + 2 * d * hidden + 2 * rows * hidden),
        name="ffn_down",
    )


def ffn_dup_kernel(n, core_ref, d_ref, *refs):
    ups, downs, gps, refs = refs[:n], refs[n:2 * n], refs[2 * n:3 * n], refs[3 * n:]
    dn_ref, dups, sums, acc_ref = refs[0], refs[1:n + 1], refs[n + 1:2 * n + 1], refs[2 * n + 1]
    rows = min(d_ref.shape[0], 512)
    first = pl.program_id(0) == 0
    last = pl.program_id(0) == pl.num_programs(0) - 1

    for s in sums:
        s[...] = jnp.zeros(s.shape, F32)

    def chunk(i, carry):
        at_rows = pl.ds(pl.multiple_of(i * rows, rows), rows)
        total = None
        for up, down, gp, dup_ref, s in zip(ups, downs, gps, dups, sums):
            dup = (nt(d_ref[at_rows, :], down[...]) * gp[at_rows, :].astype(F32)).astype(BF16)
            dup_ref[at_rows, :] = dup
            s[...] += jnp.sum(dup.astype(F32), axis=0, keepdims=True)
            term = nt(dup, up[...])
            total = term if total is None else total + term
        acc_ref[at_rows, :] = jnp.where(first, total, acc_ref[at_rows, :] + total)
        return carry

    lax.fori_loop(0, d_ref.shape[0] // rows, chunk, 0)

    @pl.when(last)
    def _():
        dn_ref[...] = acc_ref[...].astype(BF16)


def ffn_dup(core, dlow, items, hidden, deps=()):
    rows, d = dlow.shape
    n, per = len(items), hidden // HB
    col = lambda r, sel: pl.BlockSpec((r, HB), lambda j, c: (0, pick(sel, per)(j, c)))
    down = lambda sel: pl.BlockSpec((HB, d), lambda j, c: (pick(sel, per)(j, c), 0))
    out = call(
        partial(ffn_dup_kernel, n),
        (dlow, *[i[0] for i in items], *[i[2] for i in items], *[i[4] for i in items]),
        prefetch=(core,),
        deps=deps,
        grid=(per,),
        in_specs=[whole((rows, d))] + [col(d, i[1]) for i in items] + [down(i[3]) for i in items] + [col(rows, None)] * n,
        out_specs=[whole((rows, d))] + [col(rows, None)] * n + [col(1, None)] * n,
        scratch=[pltpu.VMEM((rows, d), F32)],
        out_shape=[sds((rows, d), BF16)] + [sds((rows, hidden), BF16)] * n + [sds((1, hidden), F32)] * n,
        cost_estimate=cost(4 * rows * d * hidden * n, 2 * n * (2 * d + 2 * rows) * hidden + 4 * rows * d),
        name="ffn_dup",
    )
    return out[0], out[1:n + 1], out[n + 1:]


def put_transposed(dst, tmp, src, core):
    if core is None:
        dst[...] = jnp.transpose(src)
        return
    tmp[...] = jnp.transpose(src)
    d = tmp.shape[0]
    for g in range(d // 128):
        mine = pl.multiple_of(g * 128 + core * 64, 64)
        other = pl.multiple_of(g * 128 + (1 - core) * 64, 64)
        dst[g * 64:(g + 1) * 64, :] = tmp[pl.ds(mine, 64), :]
        dst[d // 2 + g * 64:d // 2 + (g + 1) * 64, :] = tmp[pl.ds(other, 64), :]


def put_grad(keep_ref, send_ref, lt, right):
    d = lt.shape[0]
    if send_ref is None:
        for j in range(d // RB):
            keep_ref[j * RB:(j + 1) * RB, :] = nn(lt[j * RB:(j + 1) * RB, :], right).astype(BF16)
        return
    half = d // 2
    keep_ref[...] = nn(lt[:half, :], right).astype(BF16)
    send_ref[...] = nn(lt[half:, :], right).astype(BF16)


def wide_grad_kernel(n, count, steps, *refs):
    lefts, rights, refs = refs[:n], refs[n:n + n * count], refs[n + n * count:]
    outs, lt = refs[:count * steps], refs[count * steps]
    step = pl.program_id(0)
    cols, off = [], 0
    for left in lefts:
        cols.append(slice(off, off + left.shape[0]))
        off += left.shape[0]

    @pl.when(step == 0)
    def _():
        for c, left in zip(cols, lefts):
            lt[:, c] = jnp.transpose(left[...])

    d = lt.shape[0]
    for p in range(count):
        mine = rights[p * n:(p + 1) * n]
        for s in range(steps):
            @pl.when(step == s)
            def _(s=s, p=p, mine=mine):
                out = outs[p * steps + s]

                def chunk(i, carry):
                    r = pl.ds(pl.multiple_of(i * 512, 512), 512)
                    acc = nn(lt[r, cols[0]], mine[0][...])
                    for c, right in zip(cols[1:], mine[1:]):
                        acc = acc + nn(lt[r, c], right[...])
                    out[r, :] = acc.astype(BF16)
                    return carry

                lax.fori_loop(0, d // 512, chunk, 0)


def wide_grad(lefts, items, deps=()):
    d, hidden = lefts[0].shape[1], items[0][0].shape[1]
    n, count, steps = len(lefts), len(items), hidden // HB
    rows = sum(a.shape[0] for a in lefts)
    flat = [a for i in items for a in i]
    out = call(
        partial(wide_grad_kernel, n, count, steps),
        (*lefts, *flat),
        deps=deps,
        grid=(steps,),
        in_specs=[whole(a.shape) for a in lefts] + [pl.BlockSpec((a.shape[0], HB), lambda j: (0, j)) for a in flat],
        out_specs=[whole((d, HB))] * (count * steps),
        scratch=[pltpu.VMEM((d, rows), BF16)],
        out_shape=[sds((d, HB), BF16)] * (count * steps),
        cost_estimate=cost(2 * rows * d * hidden * count, 2 * (rows * d + count * (rows + d) * hidden)),
        name="wide_grad",
    )
    return [out[p * steps:(p + 1) * steps] for p in range(count)]


def norm_bwd_kernel(parts, terms, xhat_ref, rstd_ref, vec_ref, *refs):
    weights, dns, refs = refs[:parts], refs[parts:parts + terms], refs[parts + terms:]
    dlow_ref, sums_ref, mixes = refs[0], refs[1], refs[2:]
    dn = dns[0][...].astype(F32)
    for t in dns[1:]:
        dn = dn + t[...].astype(F32)
    xhat = xhat_ref[...].astype(F32)
    gg = dn * vec_ref[0:1]
    low = (rstd_ref[:, :1] * (gg - row_mean(gg) - xhat * row_mean(gg * xhat))).astype(BF16)
    dlow_ref[...] = low

    @pl.when(pl.program_id(0) == 0)
    def _():
        sums_ref[...] = jnp.zeros(sums_ref.shape, F32)

    sums_ref[0:1] += jnp.sum(dn * xhat, axis=0, keepdims=True)
    sums_ref[1:2] += jnp.sum(dn, axis=0, keepdims=True)
    sums_ref[2:3] += jnp.sum(low.astype(F32), axis=0, keepdims=True)
    for w, m in zip(weights, mixes):
        m[...] = nt(low, w[...]).astype(BF16)


def norm_bwd(dns, xhat, rstd, vec, weights, deps=()):
    rows, d = xhat.shape
    parts, terms = len(weights), len(dns)
    row = lambda n: pl.BlockSpec((RB, n), lambda i, *_: (i, 0))
    return call(
        partial(norm_bwd_kernel, parts, terms),
        (xhat, rstd, vec, *weights, *dns),
        deps=deps,
        grid=(rows // RB,),
        in_specs=[row(d), row(128), whole(vec.shape)] + [whole(w.shape) for w in weights] + [row(d)] * terms,
        out_specs=[row(d), whole((8, d))] + [row(w.shape[0]) for w in weights],
        out_shape=[sds((rows, d), BF16), sds((8, d), F32)] + [sds((rows, w.shape[0]), BF16) for w in weights],
        cost_estimate=cost(2 * rows * d * d, 14 * rows * d + 2 * d * d),
        name="norm_bwd",
    )


def grad_tn_kernel(split, lefts, count, core_ref, *refs):
    left_refs, rights, refs = refs[:lefts], refs[lefts:lefts + count], refs[lefts + count:]
    if split:
        keep_ref, send_ref, sum_ref, lt_scr, tmp_scr = refs
    else:
        keep_ref, sum_ref, lt_scr, tmp_scr = refs
        send_ref = None
    off = 0
    for left in left_refs:
        cols = slice(off, off + left.shape[0])
        put_transposed(lt_scr.at[:, cols], tmp_scr.at[:, cols], left[...], core_ref[0] if split else None)
        off += left.shape[0]
    width = rights[0].shape[1]
    for c, right in enumerate(rights):
        cols = slice(c * width, (c + 1) * width)
        put_grad(keep_ref.at[:, cols], None if send_ref is None else send_ref.at[:, cols], lt_scr.at[:, :right.shape[0]], right[...])
        sum_ref[:, cols] = jnp.sum(right[...].astype(F32), axis=0, keepdims=True)


def grad_tn(core, lefts, rights, deps=()):
    rows, d = sum(a.shape[0] for a in lefts), lefts[0].shape[1]
    width = rights[0].shape[1]
    n = width * len(rights)
    split = core is not None
    gshape = [sds((d // 2, n), BF16)] * 2 if split else [sds((d, n), BF16)]
    return call(
        partial(grad_tn_kernel, split, len(lefts), len(rights)),
        (*lefts, *rights),
        prefetch=(core if split else jnp.zeros((1,), jnp.int32),),
        deps=deps,
        grid=(1,),
        in_specs=[whole(a.shape) for a in (*lefts, *rights)],
        out_specs=[whole(a.shape) for a in gshape] + [whole((1, n))],
        scratch=[pltpu.VMEM((d, rows), BF16), pltpu.VMEM((d, rows), BF16)],
        out_shape=gshape + [sds((1, n), F32)],
        cost_estimate=cost(2 * rows * d * n, 2 * (rows * d + rows * n + d * n)),
        name="grad_tn",
    )


def in_grad_kernel(n, has_base, *refs):
    if has_base:
        base_ref, refs = refs[0], refs[1:]
    grads, weights, out_ref = refs[:n], refs[n:2 * n], refs[2 * n]
    acc = base_ref[...].astype(F32) if has_base else jnp.zeros(out_ref.shape, F32)
    for g, w in zip(grads, weights):
        acc = acc + nt(g[...], w[...])
    out_ref[...] = acc.astype(out_ref.dtype)


def in_grad(base, grads, weights, start, rows, deps=()):
    d = weights[0][0].shape[1]
    n = len(grads)
    first = start // RB
    row = lambda m: pl.BlockSpec((RB, m), lambda i, *_: (i + first, 0))
    wspec = lambda w, c: pl.BlockSpec((None, d, w.shape[2]), lambda i, *_: (c, 0, 0))
    own = pl.BlockSpec((RB, d), lambda i, *_: (i, 0))
    width = sum(g.shape[1] for g in grads)
    return call(
        partial(in_grad_kernel, n, base is not None),
        (*([base] if base is not None else []), *grads, *[w for w, _ in weights]),
        deps=deps,
        grid=(rows // RB,),
        in_specs=([own] if base is not None else []) + [row(g.shape[1]) for g in grads] + [wspec(w, c) for w, c in weights],
        out_specs=own,
        out_shape=sds((rows, d), BF16),
        cost_estimate=cost(2 * rows * d * width, 6 * rows * d + 2 * rows * width + 2 * d * width),
        name="in_grad",
    )


class Grid:
    axes = ("dp", "mp")

    def __init__(self):
        i = lax.axis_index("dp")
        self.y = lax.axis_index("mp")
        self.z, self.x, self.c = i // 4, (i // 2) % 2, i % 2
        self.all = [(z, x, c, y) for z in range(4) for x in range(2) for c in range(2) for y in range(2)]

    def permute(self, a, move):
        num = lambda z, x, c, y: ((z * 2 + x) * 2 + c) * 2 + y
        return lax.ppermute(a, self.axes, [(num(*p), num(*move(*p))) for p in self.all])

    def over_y(self, a):
        return self.permute(a, lambda z, x, c, y: (z, x, c, 1 - y))

    def over_x(self, a):
        return self.permute(a, lambda z, x, c, y: (z, 1 - x, c, y))

    def over_c(self, a):
        return self.permute(a, lambda z, x, c, y: (z, x, 1 - c, y))

    def over_zpair(self, a):
        return self.permute(a, lambda z, x, c, y: (z ^ 1, x, c, y))

    def shift_z(self, a, k):
        return self.permute(a, lambda z, x, c, y: ((z + k) % 4, x, c, y))


def join(mine, theirs, bit):
    first = jnp.where(bit == 0, mine, theirs)
    second = jnp.where(bit == 0, theirs, mine)
    return jnp.concatenate([first, second], axis=0)


class Fetch:
    def __init__(self, grid, w, x_first, cut):
        self.grid, self.x_first = grid, x_first
        self.zbit = grid.z % 2
        pair = (self.zbit * 2 + grid.x) if x_first else (grid.x * 2 + self.zbit)
        self.cut = lambda *deps: cut(after(w, *deps), grid.c, pair)

    def prepare(self, *deps):
        self.op = self.cut(*deps)
        return self.op

    def send_y(self, *deps):
        self.op = after(self.op, *deps)
        self.got = self.grid.over_y(self.op)
        return self.op

    def send(self, by_x):
        self.bit = self.grid.x if by_x else self.zbit
        self.got = self.grid.over_x(self.op) if by_x else self.grid.over_zpair(self.op)
        return self.op

    def first(self, token):
        self.op = after(self.got, token)
        return self.send(self.x_first)

    def second(self, token):
        self.op = join(self.op, after(self.got, token), self.bit)
        return self.send(not self.x_first)

    def third(self, token):
        self.op = join(self.op, after(self.got, token), self.bit)
        self.got = self.grid.over_c(self.op)
        return self.op

    def last(self, token):
        return after(self.got, token)


def at(a, axis, i):
    return lax.dynamic_index_in_dim(a, i, axis, keepdims=False)


class Reduce:
    def __init__(self, grid, own_a=None, oth_a=None, own_b=None, oth_b=None):
        self.grid, self.waiting = grid, {}
        self.own_a, self.oth_a, self.own_b, self.oth_b = own_a, oth_a, own_b, oth_b

    def view(self, a):
        return a.reshape(4, 2, a.shape[0] // 8, a.shape[1])

    def half(self, a, mine):
        g = self.grid
        return at(self.view(a), 1, g.x if mine else 1 - g.x).astype(F32)

    def cores(self, name, keep, send):
        self.waiting[name] = self.grid.over_c(send)
        setattr(self, "keep_" + "_".join(name), keep)
        return send

    def take(self, token):
        for name, got in self.waiting.items():
            got = [after(a, token) for a in got] if isinstance(got, list) else after(got, token)
            if isinstance(name, tuple):
                if not name[0].startswith("x_"):
                    got = (getattr(self, "keep_" + "_".join(name)).astype(F32) + got.astype(F32)).astype(BF16)
                width = got.shape[-1] // len(name)
                for i, n in enumerate(name):
                    setattr(self, n, got[..., i * width:(i + 1) * width])
            else:
                setattr(self, name, got)
        taken, self.waiting = [getattr(self, n) for name in self.waiting for n in ((name,) if isinstance(name, str) else name)], {}
        return [a for t in taken for a in (t if isinstance(t, list) else [t])]

    def a_over_y(self):
        self.waiting["back_a"] = self.grid.over_y(self.oth_a)
        return self.oth_a

    def a_over_x(self):
        op = (self.half(self.own_a, False) + self.half(self.back_a, False)).astype(BF16)
        self.waiting["x_a"] = self.grid.over_x(op)
        return op

    def b_over_x(self, which):
        op = jnp.concatenate([self.half(getattr(self, n), False).astype(BF16) for n in which], axis=-1)
        self.waiting[tuple("x_" + n for n in which)] = self.grid.over_x(op)
        return op

    def b_over_y(self):
        op = (self.half(self.oth_b, True) + self.x_oth_b.astype(F32)).astype(BF16)
        self.waiting["back_b"] = self.grid.over_y(op)
        return op

    def half_a(self):
        return (self.half(self.own_a, True) + self.half(self.back_a, True) + self.x_a.astype(F32)).astype(BF16)

    def over_z(self, *more):
        g = self.grid
        b = self.half(self.own_b, True) + self.x_own_b.astype(F32) + self.back_b.astype(F32)
        self.kept = lax.optimization_barrier(jnp.concatenate([self.half_a(), b.astype(BF16), *[m.half_a() for m in more]], axis=2))
        ops = [at(self.kept, 0, (g.z + k) % 4) for k in (1, 2, 3)]
        self.waiting["z_got"] = [g.shift_z(op, k) for k, op in zip((1, 2, 3), ops)]
        return ops

    def total(self):
        a, b, c = [p.astype(F32) for p in self.z_got]
        return (at(self.kept, 0, self.grid.z).astype(F32) + a) + (b + c)

    def ends(self):
        self.all = self.total().reshape(2, 64, -1)
        op = at(self.all, 0, 1 - self.grid.c).astype(BF16)
        self.waiting["end"] = self.grid.over_c(op)
        return op

    def result(self):
        mine, got = at(self.all, 0, self.grid.c), self.end.astype(F32)
        c = self.grid.c
        return jnp.concatenate([jnp.where(c == 0, mine, got), jnp.where(c == 0, got, mine)], axis=1)


class Small:
    def __init__(self, grid):
        self.grid = grid

    def send_y(self, own, oth):
        self.value, self.got = own, self.grid.over_y(oth)
        return oth

    def send_c(self, token):
        self.value = self.value + after(self.got, token)
        self.got = self.grid.over_c(self.value)
        return self.value

    def send_x(self, token):
        self.value = self.value + after(self.got, token)
        self.got = self.grid.over_x(self.value)
        return self.value

    def send_z(self, token):
        self.value = self.value + after(self.got, token)
        self.got = [self.grid.shift_z(self.value, k) for k in (1, 2, 3)]
        return self.value

    def total(self, token):
        z = self.grid.z
        ring = jnp.stack([self.value, *[after(g, token) for g in self.got]])
        terms = [at(ring, 0, (z - s) % 4) for s in range(4)]
        return (terms[0] + terms[1]) + (terms[2] + terms[3])


def time_embed(step, d):
    half = d // 2
    frequency = jnp.exp(-math.log(10000.0) * jnp.arange(half, dtype=F32) / half)
    angles = step.astype(F32) * frequency[None, :]
    return jnp.concatenate([jnp.sin(angles), jnp.cos(angles)], axis=-1)


def block_lists(seg_own, seg_halo, rows):
    q = seg_own.reshape(-1, BQ)
    keys = jnp.concatenate([seg_own, seg_halo]).reshape(-1, BK)
    need = (keys[None, :, 0] <= q[:, None, -1]) & (keys[None, :, -1] >= q[:, None, 0])
    need = need.astype(jnp.int32)
    nkb = keys.shape[0]
    before = jnp.sum(need[:, None, :] * (jnp.arange(nkb)[None, None, :] < jnp.arange(nkb)[None, :, None]), axis=2)
    slot = jnp.arange(nkb)[None, :, None]
    pick = need[:, None, :] * (before[:, None, :] == slot)
    lst = jnp.sum(pick * jnp.arange(nkb)[None, None, :], axis=2)
    return jnp.sum(need, axis=1).astype(jnp.int32), lst.astype(jnp.int32).reshape(-1)


def finish(output, grad_input, grad_qkv, head_bias_sum, grad_out, grad_up, up_bias_sum, grad_down, grad_vectors):
    grad_qkv = grad_qkv.reshape(grad_qkv.shape[0], 3, -1).transpose(1, 0, 2)
    return (
        output,
        grad_input,
        grad_qkv,
        head_bias_sum,
        grad_out.T,
        grad_up,
        up_bias_sum,
        grad_down.T,
        grad_vectors,
    )


def per_device_fast(
    tokens_in,
    timesteps,
    segment_ids,
    padding,
    qkv_weight,
    head_bias,
    out_weight,
    up_weight,
    up_bias,
    down_weight,
    vectors,
    cotangent,
):
    rows, d = tokens_in.shape
    assert timesteps.shape[0] == 1
    LIMITED[0] = True
    grid = Grid()
    me, halo = grid.y, MAXDOC
    core = grid.c.reshape(1).astype(jnp.int32)
    own_start = me * rows
    sub = up_weight.shape[1] // 2
    width = qkv_weight.shape[2]
    by_rows = lambda a, c, q: lax.dynamic_slice_in_dim(a, (c * 4 + q) * (a.shape[0] // 8), a.shape[0] // 8, 0)
    by_cols = lambda a, c, q: lax.dynamic_slice(a, (q * (a.shape[0] // 4), c * sub), (a.shape[0] // 4, sub))
    flat_qkv = qkv_weight.reshape(3 * d, width)

    def outer(a, c, q):
        o = by_rows(out_weight, c, q)
        return jnp.concatenate([by_rows(a, c, q), o[:, :width], o[:, width:]], axis=0)

    def split_outer(mine, theirs):
        n, m = 3 * d // 8, out_weight.shape[0] // 8
        mine, theirs = [t.reshape(4, n + 2 * m, width) for t in (mine, theirs)]
        cols = [join(mine[:, a:b].reshape(-1, width), theirs[:, a:b].reshape(-1, width), grid.c) for a, b in ((0, n), (n, n + m), (n + m, n + 2 * m))]
        return cols[0].reshape(qkv_weight.shape), jnp.concatenate(cols[1:], axis=1)

    fq = Fetch(grid, flat_qkv, False, outer)
    fu = Fetch(grid, up_weight, False, by_cols)
    fd = Fetch(grid, down_weight, True, by_rows)
    small_w = jnp.concatenate([head_bias.reshape(-1), up_bias])
    small_o = grid.over_y(small_w)
    fq.prepare()
    begin = [fq.send_y(), small_w]

    emb = time_embed(timesteps[:, None], d)
    seg, pad = segment_ids[0], padding[0]
    seg_own = lax.dynamic_slice_in_dim(seg, own_start, rows)
    pad_own = lax.dynamic_slice_in_dim(pad, own_start, rows)
    halo_start = jnp.where(me == 0, rows, own_start - halo)
    seg_halo = lax.dynamic_slice_in_dim(seg, halo_start, halo)
    pad_halo = lax.dynamic_slice_in_dim(pad, halo_start, halo)
    code = jnp.concatenate([jnp.where(pad_own == 0, seg_own, -1), jnp.where(pad_halo == 0, seg_halo, -1)])
    cnt, lst = block_lists(seg_own, seg_halo, rows)
    nkb = (rows + halo) // BK
    segq_row, code_col = seg_own[None, :], code[:, None]
    nb = head_bias.size

    far_blocks = (rows - halo) // BQ
    far = jnp.where(me == 0, 0, rows // BQ - far_blocks).reshape(1).astype(jnp.int32)
    near = jnp.where(me == 0, far_blocks, 0).reshape(1).astype(jnp.int32)
    zero = jnp.zeros((1,), jnp.int32)
    x_own, q0, k0, v0 = qkv_own(tokens_in, emb, qkv_weight, head_bias, deps=begin)
    ops = [fq.first(k0)]
    edge = jnp.where(me == 0, rows - halo, 0)
    halo_op = lax.dynamic_slice_in_dim(after(tokens_in, ops[0]), edge, halo, 0)
    halo_tok = grid.over_y(halo_op)
    part = attn_fwd(far, far_blocks, cnt, lst, nkb, q0, [k0], [v0], segq_row, code_col, deps=[*ops, halo_op])
    ops = [fq.second(part[1]), fu.prepare(part[1]), fd.prepare(part[1])]
    x_halo, kh0, vh0 = kv_halo(after(halo_tok, part[1]), emb, qkv_weight, head_bias, deps=ops)
    ops = [fu.send_y(kh0), fd.send_y(kh0)]
    o0, lse0 = attn_fwd(near, rows // BQ - far_blocks, cnt, lst, nkb, q0, [k0, kh0], [v0, vh0], segq_row, code_col, into=part, deps=ops)
    fq.third(lse0)
    small_o = after(small_o, lse0)
    hb_o, up_b_o = small_o[:nb].reshape(head_bias.shape), small_o[nb:].reshape(1, -1)
    qkv_o, out_o = split_outer(fq.op, fq.last(lse0))
    out_ws = [out_weight, out_o]
    _, q1, k1, v1 = qkv_own(tokens_in, emb, qkv_o, hb_o)
    _, kh1, vh1 = kv_halo(halo_tok, emb, qkv_o, hb_o, deps=[q1])
    ops = [fu.first(lse0), fd.first(lse0), kh1]
    o1, lse1 = attn_fwd(zero, rows // BQ, cnt, lst, nkb, q1, [k1, kh1], [v1, vh1], segq_row, code_col, deps=ops)
    ops = [fu.second(lse1), fd.second(lse1)]
    xhat1, normed, rstd1 = out_norm(tokens_in, emb, vectors, [o0, o1], out_ws, deps=ops)
    up_b = up_bias.reshape(1, -1)
    (a0, b0), (ga0, gb0) = ffn_up(core, normed, [(up_weight, 0, up_b, 0), (up_weight, 1, up_b, 1)], sub)
    ops = [fu.third(ga0), fd.third(ga0)]
    b0_got, normed_got = grid.over_c(b0), grid.over_c(normed)
    (a1,), (ga1,) = ffn_up(core, normed, [(fu.op, None, up_b_o, 0)], sub, deps=ops)
    up_b1, down_b1 = fu.last(ga1), fd.last(ga1)
    (b1,), (gb1,) = ffn_up(core, normed, [(up_b1, None, up_b_o, 1)], sub, deps=[ga1])
    b1_got = grid.over_c(b1)
    output, d_down, sums2 = ffn_down(
        core, normed, cotangent, vectors, [a0, b0, a1, b1], [(down_weight, 0), (down_weight, 1), (fd.op, None), (down_b1, None)]
    )

    d_got = grid.over_c(d_down)
    dn1, (ua1, ub1), us1 = ffn_dup(core, d_down, [(fu.op, None, fd.op, None, ga1), (up_b1, None, down_b1, None, gb1)], sub)
    ub1_got = grid.over_c(ub1)
    gd1, gd0 = wide_grad([d_down, after(d_got, ua1)], [(a1, after(b1_got, d_down)), (a0, after(b0_got, d_down))], deps=[ua1])
    rd = Reduce(grid, gd0[0], gd1[0], gd0[1], gd1[1])
    both = ("own_b", "oth_b")
    ops = [rd.a_over_y(), rd.b_over_x(both)]
    dn0, (ua0, ub0), us0 = ffn_dup(core, d_down, [(up_weight, 0, down_weight, 0, ga0), (up_weight, 1, down_weight, 1, gb0)], sub, deps=ops)
    ub0_got = grid.over_c(ub0)
    got = rd.take(dn0)
    d_attn, sums1, dm0, dm1 = norm_bwd([d_down, dn1, dn0], xhat1, rstd1, vectors, out_ws)
    ops = [rd.a_over_x(), rd.b_over_y(), *got]
    *og, os = grad_tn(core, [d_attn], [o0, o1], deps=[sums1, *ops])
    ro = Reduce(grid)
    ops = [ro.cores(("own_a", "oth_a"), *og)]
    gu1, gu0 = wide_grad([normed, after(normed_got, sums1)], [(ua1, after(ub1_got, sums1)), (ua0, after(ub0_got, sums1))], deps=ops)
    ru = Reduce(grid, gu0[0], gu1[0], gu0[1], gu1[1])
    got = rd.take(gu0[1]) + ro.take(gu0[1])
    ops = [*rd.over_z(), ru.a_over_y(), ru.b_over_x(both), *got]
    dqkv1 = attn_bwd(cnt, lst, nkb, q1, [k1, kh1], [v1, vh1], dm1, o1, lse1, segq_row, code_col, deps=ops)
    got = rd.take(dqkv1[0]) + ru.take(dqkv1[0])
    ops = [ru.a_over_x(), ru.b_over_y(), rd.ends(), *got]
    rq = Reduce(grid)
    *qg1, hs1 = grad_tn(core, [x_own, x_halo], dqkv1, deps=ops)
    got = ru.take(hs1) + rd.take(hs1)
    grad_down = rd.result()
    rq.cores(("oth_a", "oth_b"), *qg1)
    got += rq.take(hs1)
    ops = [rq.a_over_y(), rq.b_over_x(("oth_b",)), *ru.over_z(), ro.a_over_y(), grad_down, *got]
    dqkv0 = attn_bwd(cnt, lst, nkb, q0, [k0, kh0], [v0, vh0], dm0, o0, lse0, segq_row, code_col, deps=ops)
    got = rq.take(dqkv0[0]) + ru.take(dqkv0[0]) + ro.take(dqkv0[0])
    ops = [rq.b_over_y(), ro.a_over_x(), ru.ends(), *got]
    *qg0, hs0 = grad_tn(core, [x_own, x_halo], dqkv0, deps=ops)
    got = rq.take(hs0) + ru.take(hs0) + ro.take(hs0)
    grad_up = ru.result()
    vec6 = jnp.concatenate([sums1[:2], sums2[:2], sums1[2:3], sums2[2:3]], axis=0)
    up_sum = lambda us: jnp.where(grid.c == 0, jnp.concatenate(us, axis=0), jnp.concatenate(us[::-1], axis=0))
    head_sum = lambda hs: hs.reshape(3, -1)[0::2].reshape(1, -1)
    small = Small(grid)
    ops = [
        rq.cores(("own_a", "own_b"), *qg0),
        small.send_y(*[jnp.concatenate([vec6, up_sum(us), head_sum(hs)], axis=0) for us, hs in ((us0, hs0), (us1, hs1))]),
        grad_up, *got,
    ]
    pairs = [(g[c], w, c) for g, w in ((dqkv0, qkv_weight), (dqkv1, qkv_o)) for c in range(3)]
    kv_pairs = [(g, (w, c)) for g, w, c in pairs if c]
    halo_grad = in_grad(None, [g for g, _ in kv_pairs], [w for _, w in kv_pairs], rows, halo, deps=ops)
    got = rq.take(halo_grad)
    back = grid.over_y(halo_grad)
    ops = [rq.a_over_x(), rq.b_over_x(("own_b",)), small.send_c(halo_grad), halo_grad, *got]
    own_grad = in_grad(d_attn, [g for g, _, _ in pairs], [(w, c) for _, w, c in pairs], 0, rows, deps=ops)
    rq.take(own_grad)
    rq.over_z(ro)
    rq.take(own_grad)
    small.send_x(own_grad)
    small.send_z(own_grad)
    near_rows = (jnp.arange(rows // halo) == 1 - me)[:, None, None]
    back = after(back, own_grad).astype(F32)
    grad_input = (own_grad.reshape(rows // halo, halo, d).astype(F32) + jnp.where(near_rows, back[None], 0.0)).astype(BF16).reshape(rows, d)
    total = rq.total()
    small = small.total(total)
    qkv_cols = 3 * width
    return finish(
        output, grad_input, total[:, :qkv_cols], small[8:].reshape(2, -1), total[:, qkv_cols:], grad_up,
        small[6:8].reshape(-1), grad_down, small[:6],
    )


def per_device(
    mp_size,
    tokens_in,
    timesteps,
    segment_ids,
    padding,
    qkv_weight,
    head_bias,
    out_weight,
    up_weight,
    up_bias,
    down_weight,
    vectors,
    cotangent,
):
    rows, d = tokens_in.shape
    assert timesteps.shape[0] == 1
    LIMITED[0] = False
    me = lax.axis_index("mp")
    own_start = me * rows
    emb = time_embed(timesteps[:, None], d)
    seg, pad = segment_ids[0], padding[0]
    seg_own = lax.dynamic_slice_in_dim(seg, own_start, rows)
    pad_own = lax.dynamic_slice_in_dim(pad, own_start, rows)
    halo_tok = lax.all_gather(tokens_in, "mp", axis=0, tiled=True)
    place = jnp.arange(SEQ, dtype=jnp.int32)
    pad_halo = jnp.where((place >= own_start) & (place < own_start + rows), 1, pad)
    code = jnp.concatenate([jnp.where(pad_own == 0, seg_own, -1), jnp.where(pad_halo == 0, seg, -1)])
    cnt, lst = block_lists(seg_own, seg, rows)
    nkb = (rows + SEQ) // BK
    segq_row, code_col = seg_own[None, :], code[:, None]
    gather = lambda a, axis: lax.all_gather(a, "mp", axis=axis, tiled=True)
    qkv_w, out_w, up_w, down_w = gather(qkv_weight, 2), gather(out_weight, 0), gather(up_weight, 1), gather(down_weight, 0)
    hb, up_b = gather(head_bias, 1), gather(up_bias, 0).reshape(1, -1)

    x_own, q, k, v = qkv_own(tokens_in, emb, qkv_w, hb)
    x_halo, kh, vh = kv_halo(halo_tok, emb, qkv_w, hb)
    k, v = [k, kh], [v, vh]
    o, lse = attn_fwd(jnp.zeros((1,), jnp.int32), rows // BQ, cnt, lst, nkb, q, k, v, segq_row, code_col)
    xhat1, normed, rstd1 = out_norm(tokens_in, emb, vectors, [o], [out_w])
    core, hidden = jnp.zeros((1,), jnp.int32), up_w.shape[1]
    acts, gps = ffn_up(core, normed, [(up_w, None, up_b, None)], hidden)
    output, d_down, sums2 = ffn_down(core, normed, cotangent, vectors, acts, [(down_w, None)])

    dn, dups, (up_sum,) = ffn_dup(core, d_down, [(up_w, None, down_w, None, gps[0])], hidden)
    grad_up = jnp.concatenate(wide_grad([normed], [dups])[0], axis=1)
    grad_down = jnp.concatenate(wide_grad([d_down], [acts])[0], axis=1)
    d_attn, sums1, d_mixed = norm_bwd([d_down, dn], xhat1, rstd1, vectors, [out_w])
    grad_out, _ = grad_tn(None, [d_attn], [o])
    d_qkv = attn_bwd(cnt, lst, nkb, q, k, v, d_mixed, o, lse, segq_row, code_col)
    grad_qkv, head_sum = grad_tn(None, [x_own, x_halo], d_qkv)
    halo_grad = in_grad(None, d_qkv[1:], [(qkv_w, 1), (qkv_w, 2)], rows, SEQ)
    own_grad = in_grad(d_attn, d_qkv, [(qkv_w, c) for c in range(3)], 0, rows)
    back = lax.psum_scatter(halo_grad, "mp", scatter_dimension=0, tiled=True)
    grad_input = (own_grad.astype(F32) + back.astype(F32)).astype(BF16)

    packed = [sums1[:2], sums2[:2], sums1[2:3], sums2[2:3], head_sum.reshape(3, -1)[0::2], up_sum.reshape(-1, d)]
    packed = lax.psum(jnp.concatenate(packed, axis=0), ("dp", "mp"))
    local = head_bias.shape[1]
    head_bias_sum = lax.dynamic_slice_in_dim(packed[6:8], me * local, local, 1)
    local = up_bias.shape[0]
    up_bias_sum = lax.dynamic_slice_in_dim(packed[8:].reshape(-1), me * local, local, 0)

    def scatter(g, groups):
        n = g.shape[1] // groups // mp_size
        g = lax.psum_scatter(g, "dp", scatter_dimension=0, tiled=True)
        g = g.reshape(-1, groups, mp_size, n).transpose(2, 0, 1, 3)
        return lax.psum_scatter(g, "mp", scatter_dimension=0, tiled=False).astype(F32).reshape(-1, groups * n)

    return finish(
        output,
        grad_input,
        scatter(grad_qkv, 3),
        head_bias_sum,
        scatter(grad_out, 1),
        scatter(grad_up, 1),
        up_bias_sum,
        scatter(grad_down, 1),
        packed[:6],
    )


def solution(mesh):
    fast = dict(mesh.shape) == {"dp": 16, "mp": 2}
    return jax.shard_map(
        per_device_fast if fast else partial(per_device, mesh.shape["mp"]),
        mesh=mesh,
        in_specs=(
            P(("dp", "mp"), None),
            P("dp"),
            P("dp", None),
            P("dp", None),
            P(None, None, "mp"),
            P(None, "mp"),
            P("mp", None),
            P(None, "mp"),
            P("mp"),
            P("mp", None),
            P(),
            P(("dp", "mp"), None),
        ),
        out_specs=(
            P(("dp", "mp"), None),
            P(("dp", "mp"), None),
            P(None, "dp", "mp"),
            P(None, "mp"),
            P("mp", "dp"),
            P("dp", "mp"),
            P("mp"),
            P("mp", "dp"),
            P(),
        ),
        check_vma=False,
    )
```

```python
from functools import partial
import math

import jax
import jax.numpy as jnp
from jax import lax
from jax.experimental import pallas as pl
from jax.experimental.pallas import tpu as pltpu
from jax.sharding import PartitionSpec as P

HEAD_DIM = 64
SEQ = 2048
MAXDOC = 512
BQ = 256
BK = 256
RB = 256
HB = 512
SCALE = 300.0
VMEM_MIB = {
    "qkv_own": 12, "kv_halo": 12, "attn_fwd": 12, "out_norm": 14, "ffn_up": 20, "ffn_down": 24,
    "ffn_dup": 25, "wide_grad": 24, "norm_bwd": 14, "grad_tn": 16, "attn_bwd": 18, "in_grad": 14, "place": 18,
}
LIMITED = [True]
GROUP = 512
NEG_FILL = -1e30
F32 = jnp.float32
BF16 = jnp.bfloat16


def nt(a, b):
    return lax.dot_general(a, b, (((1,), (1,)), ((), ())), preferred_element_type=F32)


def nn(a, b):
    return lax.dot_general(a, b, (((1,), (0,)), ((), ())), preferred_element_type=F32)


def tn(a, b):
    return lax.dot_general(a, b, (((0,), (0,)), ((), ())), preferred_element_type=F32)


def cost(flops, nbytes, trans=0):
    return pl.CostEstimate(flops=int(flops * SCALE), bytes_accessed=int(nbytes * SCALE), transcendentals=int(trans * SCALE))


def whole(shape):
    return pl.BlockSpec(shape, lambda *_: (0,) * len(shape))


def sds(shape, dtype):
    return jax.ShapeDtypeStruct(shape, dtype)


def call(kernel, args, *, grid, in_specs, out_specs, out_shape, cost_estimate, name, prefetch=(), deps=(), scratch=(), aliases=None):
    first, skip, offset = len(prefetch) + len(args), len(deps), len(prefetch)

    def body(*refs):
        kernel(*refs[:first], *refs[first + skip:])

    return pl.pallas_call(
        body,
        grid_spec=pltpu.PrefetchScalarGridSpec(
            num_scalar_prefetch=offset,
            grid=grid,
            in_specs=list(in_specs) + [pl.BlockSpec(memory_space=pl.ANY)] * skip,
            out_specs=out_specs,
            scratch_shapes=list(scratch),
        ),
        out_shape=out_shape,
        input_output_aliases={k + offset: v for k, v in (aliases or {}).items()},
        cost_estimate=cost_estimate,
        compiler_params=pltpu.CompilerParams(vmem_limit_bytes=VMEM_MIB[name] << 20) if LIMITED[0] else None,
        name=name,
    )(*prefetch, *args, *deps)


def after(x, *deps):
    return lax.optimization_barrier((x, *deps))[0] if deps else x


def qkv_own_kernel(tok_ref, emb_ref, w_ref, hb_ref, x_ref, q_ref, k_ref, v_ref):
    x = (tok_ref[...].astype(F32) + emb_ref[...]).astype(BF16)
    x_ref[...] = x
    q_ref[...] = (nn(x, w_ref[0]) + hb_ref[0:1]).astype(BF16)
    k_ref[...] = nn(x, w_ref[1]).astype(BF16)
    v_ref[...] = (nn(x, w_ref[2]) + hb_ref[1:2]).astype(BF16)


def qkv_own(tok, emb, w, hb, deps=()):
    rows, d = tok.shape
    width = w.shape[2]
    row = lambda n: pl.BlockSpec((RB, n), lambda i, *_: (i, 0))
    return call(
        qkv_own_kernel,
        (tok, emb, w, hb),
        deps=deps,
        grid=(rows // RB,),
        in_specs=[row(d), whole((1, d)), whole(w.shape), whole(hb.shape)],
        out_specs=[row(d), row(width), row(width), row(width)],
        out_shape=[sds((rows, d), BF16)] + [sds((rows, width), BF16)] * 3,
        cost_estimate=cost(6 * rows * d * width, 2 * (2 * rows * d + 3 * rows * width + 3 * d * width)),
        name="qkv_own",
    )


def kv_halo_kernel(tok_ref, emb_ref, w_ref, hb_ref, x_ref, k_ref, v_ref):
    x = (tok_ref[...].astype(F32) + emb_ref[...]).astype(BF16)
    x_ref[...] = x
    k_ref[...] = nn(x, w_ref[1]).astype(BF16)
    v_ref[...] = (nn(x, w_ref[2]) + hb_ref[1:2]).astype(BF16)


def kv_halo(tok, emb, w, hb, deps=()):
    rows, d = tok.shape
    width = w.shape[2]
    row = lambda n: pl.BlockSpec((RB, n), lambda i, *_: (i, 0))
    return call(
        kv_halo_kernel,
        (tok, emb, w, hb),
        deps=deps,
        grid=(rows // RB,),
        in_specs=[row(d), whole((1, d)), whole(w.shape), whole(hb.shape)],
        out_specs=[row(d), row(width), row(width)],
        out_shape=[sds((rows, d), BF16)] + [sds((rows, width), BF16)] * 2,
        cost_estimate=cost(4 * rows * d * width, 2 * (2 * rows * d + 2 * rows * width + 3 * d * width)),
        name="kv_halo",
    )


def pair_stack(x2):
    lane = lax.broadcasted_iota(jnp.int32, (1, 128), 1)
    first = (lane < HEAD_DIM).astype(F32).astype(BF16)
    second = (lane >= HEAD_DIM).astype(F32).astype(BF16)
    return jnp.concatenate([x2 * first, x2 * second], axis=0)


def pair_merge(x):
    half = x.shape[0] // 2
    lane = lax.broadcasted_iota(jnp.int32, (half, 128), 1)
    return jnp.where(lane < HEAD_DIM, x[:half], x[half:])


def load_keys(srcs, dsts, sem, group):
    copies = []
    for pieces, dst in zip(srcs, dsts):
        off = 0
        for src in pieces:
            cols = pl.ds(pl.multiple_of(group * GROUP, GROUP), GROUP)
            copies.append(pltpu.make_async_copy(src.at[:, cols], dst.at[off:off + src.shape[0], :], sem.at[len(copies)]))
            off += src.shape[0]
    for c in copies:
        c.start()
    for c in copies:
        c.wait()


def attn_fwd_kernel(pieces, nkb, pairs, filled, base_ref, cnt_ref, list_ref, q_ref, segq_ref, codek_ref, *refs):
    k_srcs, v_srcs, refs = refs[:pieces], refs[pieces:2 * pieces], refs[2 * pieces + 2 * filled:]
    o_ref, lse_ref, k_ref, v_ref, qs_scr, m_scr, l_scr, acc_scr, sem = refs

    @pl.when(pl.program_id(1) == 0)
    def _():
        load_keys((k_srcs, v_srcs), (k_ref, v_ref), sem, pl.program_id(0))

    qb = pl.program_id(1) + base_ref[0]
    count = cnt_ref[qb]
    for p in range(pairs):
        qs_scr[p] = pair_stack(q_ref[:, 128 * p:128 * (p + 1)] * jnp.asarray(0.125, BF16))
    m_scr[...] = jnp.full(m_scr.shape, -3e38, F32)
    l_scr[...] = jnp.zeros(l_scr.shape, F32)
    acc_scr[...] = jnp.zeros(acc_scr.shape, F32)

    def step(s, carry):
        kb = list_ref[qb * nkb + s]
        off = pl.multiple_of(kb * BK, BK)
        kpos = kb * BK + lax.broadcasted_iota(jnp.int32, (BK, BQ), 0)
        qpos = qb * BQ + lax.broadcasted_iota(jnp.int32, (BK, BQ), 1)
        live = (codek_ref[pl.ds(off, BK), :] == segq_ref[...]) | (qpos == kpos)
        bias = jnp.where(live, 0.0, NEG_FILL).astype(F32)
        bias = jnp.concatenate([bias, bias], axis=1)
        scs = [nt(k_ref[pl.ds(off, BK), 128 * p:128 * (p + 1)], qs_scr[p]) for p in range(pairs)]
        es = []
        for p in range(pairs):
            sc = scs[p] + bias
            old = m_scr[p:p + 1]
            new = jnp.maximum(old, jnp.max(sc, axis=0, keepdims=True))
            e = jnp.exp(sc - new)
            fade = jnp.exp(old - new)
            m_scr[p:p + 1] = new
            l_scr[p:p + 1] = l_scr[p:p + 1] * fade + jnp.sum(e, axis=0, keepdims=True)
            es.append((e.astype(BF16), fade))
        for p in range(pairs):
            acc_scr[p] = acc_scr[p] * es[p][1] + tn(v_ref[pl.ds(off, BK), 128 * p:128 * (p + 1)], es[p][0])
        return carry

    lax.fori_loop(0, count, step, 0)
    lse = m_scr[...] + jnp.log(l_scr[...])
    for p in range(pairs):
        o = acc_scr[p] / l_scr[p:p + 1]
        o = jnp.concatenate([o[:HEAD_DIM, :BQ], o[HEAD_DIM:, BQ:]], axis=0)
        o_ref[:, 128 * p:128 * (p + 1)] = jnp.transpose(o).astype(BF16)
        lse_ref[2 * p:2 * p + 1, :] = lse[p:p + 1, :BQ]
        lse_ref[2 * p + 1:2 * p + 2, :] = lse[p:p + 1, BQ:]


def attn_fwd(base, nqb, cnt, lst, nkb, q, k, v, segq, codek, into=(), deps=()):
    rows, width = q.shape
    pieces, keys = len(k), sum(a.shape[0] for a in k)
    groups, pairs = width // GROUP, GROUP // 128
    est = nqb * BQ * 2 * BK * width
    qspec = lambda n: pl.BlockSpec((BQ, n), lambda g, i, b, *_: (i + b[0], g))
    lspec = pl.BlockSpec((2 * pairs, BQ), lambda g, i, b, *_: (g, i + b[0]))
    anyspec = pl.BlockSpec(memory_space=pl.ANY)
    args = [q, segq, codek, *k, *v, *into]
    first = 3 + 2 * pieces
    return call(
        partial(attn_fwd_kernel, pieces, nkb, pairs, len(into) // 2),
        args,
        prefetch=(base, cnt, lst),
        deps=deps,
        grid=(groups, nqb),
        in_specs=[qspec(GROUP), pl.BlockSpec((1, BQ), lambda g, i, b, *_: (0, i + b[0])), pl.BlockSpec((codek.shape[0], 1), lambda *_: (0, 0))]
        + [anyspec] * (len(args) - 3),
        out_specs=[qspec(GROUP), lspec],
        out_shape=[sds((rows, width), BF16), sds((2 * pairs * groups, rows), F32)],
        aliases={first: 0, first + 1: 1} if into else None,
        scratch=[
            pltpu.VMEM((keys, GROUP), BF16),
            pltpu.VMEM((keys, GROUP), BF16),
            pltpu.VMEM((pairs, 2 * BQ, 128), BF16),
            pltpu.VMEM((pairs, 2 * BQ), F32),
            pltpu.VMEM((pairs, 2 * BQ), F32),
            pltpu.VMEM((pairs, 128, 2 * BQ), F32),
            pltpu.SemaphoreType.DMA((2 * pieces,)),
        ],
        cost_estimate=cost(4 * est, 8 * rows * width, est // 32),
        name="attn_fwd",
    )


def attn_bwd_kernel(pieces, nkb, pairs, cnt_ref, list_ref, q_ref, do_ref, o_ref, lse_ref, segq_ref, codek_ref, *refs):
    k_srcs, v_srcs, refs = refs[:pieces], refs[pieces:2 * pieces], refs[2 * pieces:]
    dq_ref, dk_ref, dv_ref, sum_ref, k_ref, v_ref, qs_scr, ds_scr, row_scr, dq_scr, dk_scr, dv_scr, sem = refs
    qb = pl.program_id(1)

    @pl.when(qb == 0)
    def _():
        load_keys((k_srcs, v_srcs), (k_ref, v_ref), sem, pl.program_id(0))

    @pl.when(qb == 0)
    def _():
        dk_scr[...] = jnp.zeros(dk_scr.shape, F32)
        dv_scr[...] = jnp.zeros(dv_scr.shape, F32)

    count = cnt_ref[qb]
    lse_t = lse_ref[...]
    for p in range(pairs):
        cols = slice(128 * p, 128 * (p + 1))
        qs_scr[p] = pair_stack(q_ref[:, cols] * jnp.asarray(0.125, BF16))
        ds_scr[p] = pair_stack(do_ref[:, cols])
        prod = jnp.transpose(do_ref[:, cols].astype(F32) * o_ref[:, cols].astype(F32))
        da = jnp.sum(prod[:HEAD_DIM], axis=0, keepdims=True)
        db = jnp.sum(prod[HEAD_DIM:], axis=0, keepdims=True)
        row_scr[p, 0:1] = jnp.concatenate([lse_t[2 * p:2 * p + 1], lse_t[2 * p + 1:2 * p + 2]], axis=1)
        row_scr[p, 1:2] = jnp.concatenate([da, db], axis=1)
    dq_scr[...] = jnp.zeros(dq_scr.shape, F32)

    def step(s, carry):
        kb = list_ref[qb * nkb + s]
        off = pl.multiple_of(kb * BK, BK)
        kpos = kb * BK + lax.broadcasted_iota(jnp.int32, (BK, BQ), 0)
        qpos = qb * BQ + lax.broadcasted_iota(jnp.int32, (BK, BQ), 1)
        live = (codek_ref[pl.ds(off, BK), :] == segq_ref[...]) | (qpos == kpos)
        bias = jnp.where(live, 0.0, NEG_FILL).astype(F32)
        bias = jnp.concatenate([bias, bias], axis=1)
        for p in range(pairs):
            cols = slice(128 * p, 128 * (p + 1))
            k2 = k_ref[pl.ds(off, BK), cols]
            v2 = v_ref[pl.ds(off, BK), cols]
            sc = nt(k2, qs_scr[p]) + bias
            probs = jnp.exp(sc - row_scr[p, 0:1])
            dprobs = nt(v2, ds_scr[p])
            dsc = (probs * (dprobs - row_scr[p, 1:2])).astype(BF16)
            dv_scr[pl.ds(off, BK), cols] += nn(probs.astype(BF16), ds_scr[p])
            dk_scr[pl.ds(off, BK), cols] += nn(dsc, qs_scr[p])
            dq_scr[p] += tn(k2, dsc)
        return carry

    lax.fori_loop(0, count, step, 0)
    for p in range(pairs):
        dq = dq_scr[p] * 0.125
        dq = jnp.concatenate([dq[:HEAD_DIM, :BQ], dq[HEAD_DIM:, BQ:]], axis=0)
        dq = jnp.transpose(dq).astype(BF16)
        cols = slice(128 * p, 128 * (p + 1))
        dq_ref[:, cols] = dq
        so_far = jnp.where(qb == 0, 0.0, sum_ref[0:1, cols])
        sum_ref[0:1, cols] = so_far + jnp.sum(dq.astype(F32), axis=0, keepdims=True)

    @pl.when(qb == pl.num_programs(1) - 1)
    def _():
        dk_ref[...] = dk_scr[...].astype(BF16)
        dv_ref[...] = dv_scr[...].astype(BF16)
        sum_ref[1:2, :] = jnp.sum(dv_scr[...], axis=0, keepdims=True)


def attn_bwd(cnt, lst, nkb, q, k, v, do, o, lse, segq, codek, deps=()):
    rows, width = q.shape
    pieces, keys = len(k), sum(a.shape[0] for a in k)
    groups, pairs = width // GROUP, GROUP // 128
    est = rows * 2 * BK * width
    qspec = pl.BlockSpec((BQ, GROUP), lambda g, i, *_: (i, g))
    kspec = pl.BlockSpec((keys, GROUP), lambda g, i, *_: (0, g))
    return call(
        partial(attn_bwd_kernel, pieces, nkb, pairs),
        (q, do, o, lse, segq, codek, *k, *v),
        prefetch=(cnt, lst),
        deps=deps,
        grid=(groups, rows // BQ),
        in_specs=[
            qspec, qspec, qspec,
            pl.BlockSpec((2 * pairs, BQ), lambda g, i, *_: (g, i)),
            pl.BlockSpec((1, BQ), lambda g, i, *_: (0, i)),
            pl.BlockSpec((keys, 1), lambda g, i, *_: (0, 0)),
        ] + [pl.BlockSpec(memory_space=pl.ANY)] * (2 * pieces),
        out_specs=[qspec, kspec, kspec, pl.BlockSpec((2, GROUP), lambda g, i, *_: (0, g))],
        scratch=[
            pltpu.VMEM((keys, GROUP), BF16),
            pltpu.VMEM((keys, GROUP), BF16),
            pltpu.VMEM((pairs, 2 * BQ, 128), BF16),
            pltpu.VMEM((pairs, 2 * BQ, 128), BF16),
            pltpu.VMEM((pairs, 8, 2 * BQ), F32),
            pltpu.VMEM((pairs, 128, 2 * BQ), F32),
            pltpu.VMEM((keys, GROUP), F32),
            pltpu.VMEM((keys, GROUP), F32),
            pltpu.SemaphoreType.DMA((2 * pieces,)),
        ],
        out_shape=[sds((rows, width), BF16), sds((keys, width), BF16), sds((keys, width), BF16), sds((2, width), F32)],
        cost_estimate=cost(10 * est, 16 * rows * width, est // 32),
        name="attn_bwd",
    )


def row_mean(x):
    return jnp.mean(x, axis=-1, keepdims=True)


def out_norm_kernel(parts, tok_ref, emb_ref, vec_ref, *refs):
    mixed, weights = refs[:parts], refs[parts:2 * parts]
    xhat_ref, low_ref, rstd_ref = refs[2 * parts:]
    acc = tok_ref[...].astype(F32) + emb_ref[...] + vec_ref[4:5]
    for m, w in zip(mixed, weights):
        acc = acc + nn(m[...], w[...])
    centered = acc - row_mean(acc)
    rstd = lax.rsqrt(row_mean(centered * centered) + 1e-05)
    xhat = centered * rstd
    xhat_ref[...] = xhat.astype(BF16)
    rstd_ref[...] = jnp.broadcast_to(rstd, rstd_ref.shape)
    low_ref[...] = (xhat * vec_ref[0:1] + vec_ref[1:2]).astype(BF16)


def out_norm(tok, emb, vec, mixed, weights, deps=()):
    rows, d = tok.shape
    parts = len(mixed)
    row = lambda n: pl.BlockSpec((RB, n), lambda i, *_: (i, 0))
    return call(
        partial(out_norm_kernel, parts),
        (tok, emb, vec, *mixed, *weights),
        deps=deps,
        grid=(rows // RB,),
        in_specs=[row(d), whole((1, d)), whole(vec.shape)]
        + [row(m.shape[1]) for m in mixed]
        + [whole(w.shape) for w in weights],
        out_specs=[row(d), row(d), row(128)],
        out_shape=[sds((rows, d), BF16), sds((rows, d), BF16), sds((rows, 128), F32)],
        cost_estimate=cost(2 * rows * d * d, 8 * rows * d + 2 * d * d),
        name="out_norm",
    )


def gelu_pair(h):
    mag = jnp.abs(h)
    t = 1.0 / (1.0 + (0.3275911 * 0.7071067811865476) * mag)
    e = jnp.exp(-0.5 * (h * h))
    poly = t * (0.127414796 + t * (-0.142248368 + t * (0.7107068705 + t * (-0.7265760135 + t * 0.5307027145))))
    tail = poly * e
    phi = jnp.where(h < 0.0, tail, 1.0 - tail)
    return h * phi, phi + h * (e * 0.3989422804014327)


def pick(sel, per):
    if sel is None:
        return lambda j, core: j
    return lambda j, core: j + per * (core[0] if sel == 0 else 1 - core[0])


def ffn_up_kernel(n, core_ref, x_ref, *refs):
    ws, bs, acts, gps = refs[:n], refs[n:2 * n], refs[2 * n:3 * n], refs[3 * n:]
    rows = min(x_ref.shape[0], 512)

    def chunk(i, carry):
        at_rows = pl.ds(pl.multiple_of(i * rows, rows), rows)
        for w, b, a, g in zip(ws, bs, acts, gps):
            h = nn(x_ref[at_rows, :], w[...]) + b[...]
            act, gp = gelu_pair(h)
            a[at_rows, :] = act.astype(BF16)
            g[at_rows, :] = gp.astype(BF16)
        return carry

    lax.fori_loop(0, x_ref.shape[0] // rows, chunk, 0)


def ffn_up(core, x, items, hidden, deps=()):
    rows, d = x.shape
    n, per = len(items), hidden // HB
    col = lambda r, sel: pl.BlockSpec((r, HB), lambda j, c: (0, pick(sel, per)(j, c)))
    out = call(
        partial(ffn_up_kernel, n),
        (x, *[i[0] for i in items], *[i[2] for i in items]),
        prefetch=(core,),
        deps=deps,
        grid=(per,),
        in_specs=[whole((rows, d))] + [col(d, i[1]) for i in items] + [col(1, i[3]) for i in items],
        out_specs=[col(rows, None)] * (2 * n),
        out_shape=[sds((rows, hidden), BF16)] * (2 * n),
        cost_estimate=cost(2 * rows * d * hidden * n, 2 * (rows * d + n * (d + 2 * rows) * hidden), rows * hidden * n),
        name="ffn_up",
    )
    return out[:n], out[n:]


def ffn_down_kernel(parts, core_ref, norm_ref, cot_ref, vec_ref, *refs):
    acts, weights = refs[:parts], refs[parts:2 * parts]
    out_ref, dlow_ref, sums_ref = refs[2 * parts:]
    acc = norm_ref[...].astype(F32) + vec_ref[5:6]
    for a, w in zip(acts, weights):
        acc = acc + nn(a[...], w[...])
    centered = acc - row_mean(acc)
    rstd = lax.rsqrt(row_mean(centered * centered) + 1e-05)
    xhat = centered * rstd
    out_ref[...] = (xhat * vec_ref[2:3] + vec_ref[3:4]).astype(BF16)
    cot = cot_ref[...].astype(F32)
    gg = cot * vec_ref[2:3]
    dres = rstd * (gg - row_mean(gg) - xhat * row_mean(gg * xhat))
    low = dres.astype(BF16)
    dlow_ref[...] = low

    @pl.when(pl.program_id(0) == 0)
    def _():
        sums_ref[...] = jnp.zeros(sums_ref.shape, F32)

    sums_ref[0:1] += jnp.sum(cot * xhat, axis=0, keepdims=True)
    sums_ref[1:2] += jnp.sum(cot, axis=0, keepdims=True)
    sums_ref[2:3] += jnp.sum(low.astype(F32), axis=0, keepdims=True)


def ffn_down(core, normed, cot, vec, acts, weights, deps=()):
    rows, d = normed.shape
    parts = len(acts)
    hidden = sum(a.shape[1] for a in acts)
    row = lambda n: pl.BlockSpec((RB, n), lambda i, *_: (i, 0))
    wspec = lambda a, sel: pl.BlockSpec((a.shape[1], d), lambda i, c: (pick(sel, 1)(0, c), 0))
    return call(
        partial(ffn_down_kernel, parts),
        (normed, cot, vec, *acts, *[w for w, _ in weights]),
        prefetch=(core,),
        deps=deps,
        grid=(rows // RB,),
        in_specs=[row(d), row(d), whole(vec.shape)]
        + [row(a.shape[1]) for a in acts]
        + [wspec(a, sel) for a, (_, sel) in zip(acts, weights)],
        out_specs=[row(d), row(d), whole((8, d))],
        out_shape=[sds((rows, d), BF16), sds((rows, d), BF16), sds((8, d), F32)],
        cost_estimate=cost(2 * rows * d * hidden, 8 * rows * d + 2 * d * hidden + 2 * rows * hidden),
        name="ffn_down",
    )


def ffn_dup_kernel(n, core_ref, d_ref, *refs):
    ups, downs, gps, refs = refs[:n], refs[n:2 * n], refs[2 * n:3 * n], refs[3 * n:]
    dn_ref, dups, sums, acc_ref = refs[0], refs[1:n + 1], refs[n + 1:2 * n + 1], refs[2 * n + 1]
    rows = min(d_ref.shape[0], 512)
    first = pl.program_id(0) == 0
    last = pl.program_id(0) == pl.num_programs(0) - 1

    for s in sums:
        s[...] = jnp.zeros(s.shape, F32)

    def chunk(i, carry):
        at_rows = pl.ds(pl.multiple_of(i * rows, rows), rows)
        total = None
        for up, down, gp, dup_ref, s in zip(ups, downs, gps, dups, sums):
            dup = (nt(d_ref[at_rows, :], down[...]) * gp[at_rows, :].astype(F32)).astype(BF16)
            dup_ref[at_rows, :] = dup
            s[...] += jnp.sum(dup.astype(F32), axis=0, keepdims=True)
            term = nt(dup, up[...])
            total = term if total is None else total + term
        acc_ref[at_rows, :] = jnp.where(first, total, acc_ref[at_rows, :] + total)
        return carry

    lax.fori_loop(0, d_ref.shape[0] // rows, chunk, 0)

    @pl.when(last)
    def _():
        dn_ref[...] = acc_ref[...].astype(BF16)


def ffn_dup(core, dlow, items, hidden, deps=()):
    rows, d = dlow.shape
    n, per = len(items), hidden // HB
    col = lambda r, sel: pl.BlockSpec((r, HB), lambda j, c: (0, pick(sel, per)(j, c)))
    down = lambda sel: pl.BlockSpec((HB, d), lambda j, c: (pick(sel, per)(j, c), 0))
    out = call(
        partial(ffn_dup_kernel, n),
        (dlow, *[i[0] for i in items], *[i[2] for i in items], *[i[4] for i in items]),
        prefetch=(core,),
        deps=deps,
        grid=(per,),
        in_specs=[whole((rows, d))] + [col(d, i[1]) for i in items] + [down(i[3]) for i in items] + [col(rows, None)] * n,
        out_specs=[whole((rows, d))] + [col(rows, None)] * n + [col(1, None)] * n,
        scratch=[pltpu.VMEM((rows, d), F32)],
        out_shape=[sds((rows, d), BF16)] + [sds((rows, hidden), BF16)] * n + [sds((1, hidden), F32)] * n,
        cost_estimate=cost(4 * rows * d * hidden * n, 2 * n * (2 * d + 2 * rows) * hidden + 4 * rows * d),
        name="ffn_dup",
    )
    return out[0], out[1:n + 1], out[n + 1:]


def put_transposed(dst, tmp, src, core):
    if core is None:
        dst[...] = jnp.transpose(src)
        return
    tmp[...] = jnp.transpose(src)
    d = tmp.shape[0]
    for g in range(d // 128):
        mine = pl.multiple_of(g * 128 + core * 64, 64)
        other = pl.multiple_of(g * 128 + (1 - core) * 64, 64)
        dst[g * 64:(g + 1) * 64, :] = tmp[pl.ds(mine, 64), :]
        dst[d // 2 + g * 64:d // 2 + (g + 1) * 64, :] = tmp[pl.ds(other, 64), :]


def put_grad(keep_ref, send_ref, lt, right):
    d = lt.shape[0]
    if send_ref is None:
        for j in range(d // RB):
            keep_ref[j * RB:(j + 1) * RB, :] = nn(lt[j * RB:(j + 1) * RB, :], right).astype(BF16)
        return
    half = d // 2
    keep_ref[...] = nn(lt[:half, :], right).astype(BF16)
    send_ref[...] = nn(lt[half:, :], right).astype(BF16)


def wide_grad_kernel(n, count, steps, *refs):
    lefts, rights, refs = refs[:n], refs[n:n + n * count], refs[n + n * count:]
    outs, lt = refs[:count * steps], refs[count * steps]
    step = pl.program_id(0)
    cols, off = [], 0
    for left in lefts:
        cols.append(slice(off, off + left.shape[0]))
        off += left.shape[0]

    @pl.when(step == 0)
    def _():
        for c, left in zip(cols, lefts):
            lt[:, c] = jnp.transpose(left[...])

    d = lt.shape[0]
    for p in range(count):
        mine = rights[p * n:(p + 1) * n]
        for s in range(steps):
            @pl.when(step == s)
            def _(s=s, p=p, mine=mine):
                out = outs[p * steps + s]

                def chunk(i, carry):
                    r = pl.ds(pl.multiple_of(i * 512, 512), 512)
                    acc = nn(lt[r, cols[0]], mine[0][...])
                    for c, right in zip(cols[1:], mine[1:]):
                        acc = acc + nn(lt[r, c], right[...])
                    out[r, :] = acc.astype(BF16)
                    return carry

                lax.fori_loop(0, d // 512, chunk, 0)


def wide_grad(lefts, items, deps=()):
    d, hidden = lefts[0].shape[1], items[0][0].shape[1]
    n, count, steps = len(lefts), len(items), hidden // HB
    rows = sum(a.shape[0] for a in lefts)
    flat = [a for i in items for a in i]
    out = call(
        partial(wide_grad_kernel, n, count, steps),
        (*lefts, *flat),
        deps=deps,
        grid=(steps,),
        in_specs=[whole(a.shape) for a in lefts] + [pl.BlockSpec((a.shape[0], HB), lambda j: (0, j)) for a in flat],
        out_specs=[whole((d, HB))] * (count * steps),
        scratch=[pltpu.VMEM((d, rows), BF16)],
        out_shape=[sds((d, HB), BF16)] * (count * steps),
        cost_estimate=cost(2 * rows * d * hidden * count, 2 * (rows * d + count * (rows + d) * hidden)),
        name="wide_grad",
    )
    return [out[p * steps:(p + 1) * steps] for p in range(count)]


def norm_bwd_kernel(parts, terms, xhat_ref, rstd_ref, vec_ref, *refs):
    weights, dns, refs = refs[:parts], refs[parts:parts + terms], refs[parts + terms:]
    dlow_ref, sums_ref, mixes = refs[0], refs[1], refs[2:]
    dn = dns[0][...].astype(F32)
    for t in dns[1:]:
        dn = dn + t[...].astype(F32)
    xhat = xhat_ref[...].astype(F32)
    gg = dn * vec_ref[0:1]
    low = (rstd_ref[:, :1] * (gg - row_mean(gg) - xhat * row_mean(gg * xhat))).astype(BF16)
    dlow_ref[...] = low

    @pl.when(pl.program_id(0) == 0)
    def _():
        sums_ref[...] = jnp.zeros(sums_ref.shape, F32)

    sums_ref[0:1] += jnp.sum(dn * xhat, axis=0, keepdims=True)
    sums_ref[1:2] += jnp.sum(dn, axis=0, keepdims=True)
    sums_ref[2:3] += jnp.sum(low.astype(F32), axis=0, keepdims=True)
    for w, m in zip(weights, mixes):
        m[...] = nt(low, w[...]).astype(BF16)


def norm_bwd(dns, xhat, rstd, vec, weights, deps=()):
    rows, d = xhat.shape
    parts, terms = len(weights), len(dns)
    row = lambda n: pl.BlockSpec((RB, n), lambda i, *_: (i, 0))
    return call(
        partial(norm_bwd_kernel, parts, terms),
        (xhat, rstd, vec, *weights, *dns),
        deps=deps,
        grid=(rows // RB,),
        in_specs=[row(d), row(128), whole(vec.shape)] + [whole(w.shape) for w in weights] + [row(d)] * terms,
        out_specs=[row(d), whole((8, d))] + [row(w.shape[0]) for w in weights],
        out_shape=[sds((rows, d), BF16), sds((8, d), F32)] + [sds((rows, w.shape[0]), BF16) for w in weights],
        cost_estimate=cost(2 * rows * d * d, 14 * rows * d + 2 * d * d),
        name="norm_bwd",
    )


def grad_tn_kernel(split, lefts, count, core_ref, *refs):
    left_refs, rights, refs = refs[:lefts], refs[lefts:lefts + count], refs[lefts + count:]
    if split:
        keep_ref, send_ref, done_ref, lt_scr, tmp_scr = refs
    else:
        keep_ref, done_ref, lt_scr, tmp_scr = refs
        send_ref = None
    off = 0
    for left in left_refs:
        cols = slice(off, off + left.shape[0])
        put_transposed(lt_scr.at[:, cols], tmp_scr.at[:, cols], left[...], core_ref[0] if split else None)
        off += left.shape[0]
    done_ref[...] = jnp.zeros(done_ref.shape, F32)
    width = rights[0].shape[1]
    for c, right in enumerate(rights):
        cols = slice(c * width, (c + 1) * width)
        put_grad(keep_ref.at[:, cols], None if send_ref is None else send_ref.at[:, cols], lt_scr.at[:, :right.shape[0]], right[...])


def grad_tn(core, lefts, rights, deps=()):
    rows, d = sum(a.shape[0] for a in lefts), lefts[0].shape[1]
    width = rights[0].shape[1]
    n = width * len(rights)
    split = core is not None
    gshape = [sds((d // 2, n), BF16)] * 2 if split else [sds((d, n), BF16)]
    return call(
        partial(grad_tn_kernel, split, len(lefts), len(rights)),
        (*lefts, *rights),
        prefetch=(core if split else jnp.zeros((1,), jnp.int32),),
        deps=deps,
        grid=(1,),
        in_specs=[whole(a.shape) for a in (*lefts, *rights)],
        out_specs=[whole(a.shape) for a in gshape] + [whole((8, 128))],
        scratch=[pltpu.VMEM((d, rows), BF16), pltpu.VMEM((d, rows), BF16)],
        out_shape=gshape + [sds((8, 128), F32)],
        cost_estimate=cost(2 * rows * d * n, 2 * (rows * d + rows * n + d * n)),
        name="grad_tn",
    )


def in_grad_kernel(n, has_base, *refs):
    if has_base:
        base_ref, refs = refs[0], refs[1:]
    grads, weights, out_ref = refs[:n], refs[n:2 * n], refs[2 * n]
    acc = base_ref[...].astype(F32) if has_base else jnp.zeros(out_ref.shape, F32)
    for g, w in zip(grads, weights):
        acc = acc + nt(g[...], w[...])
    out_ref[...] = acc.astype(out_ref.dtype)


def in_grad(base, grads, weights, start, rows, deps=()):
    d = weights[0][0].shape[1]
    n = len(grads)
    first = start // RB
    row = lambda m: pl.BlockSpec((RB, m), lambda i, *_: (i + first, 0))
    wspec = lambda w, c: pl.BlockSpec((None, d, w.shape[2]), lambda i, *_: (c, 0, 0))
    own = pl.BlockSpec((RB, d), lambda i, *_: (i, 0))
    width = sum(g.shape[1] for g in grads)
    return call(
        partial(in_grad_kernel, n, base is not None),
        (*([base] if base is not None else []), *grads, *[w for w, _ in weights]),
        deps=deps,
        grid=(rows // RB,),
        in_specs=([own] if base is not None else []) + [row(g.shape[1]) for g in grads] + [wspec(w, c) for w, c in weights],
        out_specs=own,
        out_shape=sds((rows, d), BF16),
        cost_estimate=cost(2 * rows * d * width, 6 * rows * d + 2 * rows * width + 2 * d * width),
        name="in_grad",
    )


class Grid:
    axes = ("dp", "mp")

    def __init__(self):
        i = lax.axis_index("dp")
        self.y = lax.axis_index("mp")
        self.z, self.x, self.c = i // 4, (i // 2) % 2, i % 2
        self.all = [(z, x, c, y) for z in range(4) for x in range(2) for c in range(2) for y in range(2)]

    def permute(self, a, move):
        num = lambda z, x, c, y: ((z * 2 + x) * 2 + c) * 2 + y
        return lax.ppermute(a, self.axes, [(num(*p), num(*move(*p))) for p in self.all])

    def over_y(self, a):
        return self.permute(a, lambda z, x, c, y: (z, x, c, 1 - y))

    def over_x(self, a):
        return self.permute(a, lambda z, x, c, y: (z, 1 - x, c, y))

    def over_c(self, a):
        return self.permute(a, lambda z, x, c, y: (z, x, 1 - c, y))

    def over_zpair(self, a):
        return self.permute(a, lambda z, x, c, y: (z ^ 1, x, c, y))

    def shift_z(self, a, k):
        return self.permute(a, lambda z, x, c, y: ((z + k) % 4, x, c, y))


def place_kernel(moves, bits_ref, *refs):
    for src, dst in moves(bits_ref, refs):
        dst[...] = src[...]


def place(moves, bits, args, out_shape):
    return call(
        partial(place_kernel, moves),
        args,
        prefetch=(jnp.stack(bits).astype(jnp.int32),),
        grid=(1,),
        in_specs=[whole(a.shape) for a in args],
        out_specs=[whole(o.shape) for o in out_shape],
        out_shape=out_shape,
        cost_estimate=cost(0, 4 * sum(math.prod(o.shape) for o in out_shape)),
        name="place",
    )


def join(pairs, bits):
    n = len(pairs)

    def moves(bits_ref, refs):
        for i in range(n):
            rows = refs[2 * i].shape[0]
            for k in range(2):
                bit = bits_ref[i] if k == 0 else 1 - bits_ref[i]
                yield refs[2 * i + k], refs[2 * n + i].at[pl.ds(pl.multiple_of(bit * rows, rows), rows), :]

    outs = [sds((2 * a.shape[0], a.shape[1]), a.dtype) for a, _ in pairs]
    return place(moves, bits, [a for p in pairs for a in p], outs)


class Fetch:
    def __init__(self, grid, w, x_first, cut):
        self.grid, self.x_first = grid, x_first
        self.zbit = grid.z % 2
        pair = (self.zbit * 2 + grid.x) if x_first else (grid.x * 2 + self.zbit)
        self.cut = lambda *deps: cut(after(w, *deps), grid.c, pair)

    def prepare(self, *deps):
        self.op = self.cut(*deps)
        return self.op

    def send_y(self, *deps):
        self.op = after(self.op, *deps)
        self.got = self.grid.over_y(self.op)
        return self.op

    def send(self, by_x):
        self.bit = self.grid.x if by_x else self.zbit
        self.got = self.grid.over_x(self.op) if by_x else self.grid.over_zpair(self.op)
        return self.op

    def first(self, token):
        self.op = after(self.got, token)
        return self.send(self.x_first)

    @staticmethod
    def joined(fetches, token):
        parts = join([(f.op, after(f.got, token)) for f in fetches], [f.bit for f in fetches])
        for f, part in zip(fetches, parts):
            f.op = part

    @staticmethod
    def second(fetches, token):
        Fetch.joined(fetches, token)
        return [f.send(not f.x_first) for f in fetches]

    @staticmethod
    def third(fetches, token):
        Fetch.joined(fetches, token)
        for f in fetches:
            f.got = f.grid.over_c(f.op)
        return [f.op for f in fetches]

    def last(self, token):
        return after(self.got, token)


def at(a, axis, i):
    return lax.dynamic_index_in_dim(a, i, axis, keepdims=False)


class Reduce:
    def __init__(self, grid, own_a=None, oth_a=None, own_b=None, oth_b=None):
        self.grid, self.waiting = grid, {}
        self.own_a, self.oth_a, self.own_b, self.oth_b = own_a, oth_a, own_b, oth_b

    def view(self, a):
        return a.reshape(4, 2, a.shape[0] // 8, a.shape[1])

    def half(self, a, mine):
        g = self.grid
        return at(self.view(a), 1, g.x if mine else 1 - g.x).astype(F32)

    def cores(self, name, keep, send):
        self.waiting[name] = self.grid.over_c(send)
        setattr(self, "keep_" + "_".join(name), keep)
        return send

    def take(self, token):
        for name, got in self.waiting.items():
            got = [after(a, token) for a in got] if isinstance(got, list) else after(got, token)
            if isinstance(name, tuple):
                if not name[0].startswith("x_"):
                    got = (getattr(self, "keep_" + "_".join(name)).astype(F32) + got.astype(F32)).astype(BF16)
                width = got.shape[-1] // len(name)
                for i, n in enumerate(name):
                    setattr(self, n, got[..., i * width:(i + 1) * width])
            else:
                setattr(self, name, got)
        taken, self.waiting = [getattr(self, n) for name in self.waiting for n in ((name,) if isinstance(name, str) else name)], {}
        return [a for t in taken for a in (t if isinstance(t, list) else [t])]

    def a_over_y(self):
        self.waiting["back_a"] = self.grid.over_y(self.oth_a)
        return self.oth_a

    def a_over_x(self):
        op = (self.half(self.own_a, False) + self.half(self.back_a, False)).astype(BF16)
        self.waiting["x_a"] = self.grid.over_x(op)
        return op

    def b_over_x(self, which):
        op = jnp.concatenate([self.half(getattr(self, n), False).astype(BF16) for n in which], axis=-1)
        self.waiting[tuple("x_" + n for n in which)] = self.grid.over_x(op)
        return op

    def b_over_y(self):
        op = (self.half(self.oth_b, True) + self.x_oth_b.astype(F32)).astype(BF16)
        self.waiting["back_b"] = self.grid.over_y(op)
        return op

    def half_a(self):
        return (self.half(self.own_a, True) + self.half(self.back_a, True) + self.x_a.astype(F32)).astype(BF16)

    def over_z(self, *more):
        g = self.grid
        b = self.half(self.own_b, True) + self.x_own_b.astype(F32) + self.back_b.astype(F32)
        self.kept = jnp.concatenate([self.half_a(), b.astype(BF16), *[m.half_a() for m in more]], axis=2)
        self.kept = lax.optimization_barrier(self.kept)
        ops = [at(self.kept, 0, (g.z + k) % 4) for k in (1, 2, 3)]
        self.waiting["z_got"] = [g.shift_z(op, k) for k, op in zip((1, 2, 3), ops)]
        return ops

    def total(self):
        a, b, c = [p.astype(F32) for p in self.z_got]
        return (at(self.kept, 0, self.grid.z).astype(F32) + a) + (b + c)

    def ends(self):
        self.all = self.total().reshape(2, 64, -1)
        op = at(self.all, 0, 1 - self.grid.c).astype(BF16)
        self.waiting["end"] = self.grid.over_c(op)
        return op

    def result(self):
        mine, got = at(self.all, 0, self.grid.c), self.end.astype(F32)
        c = self.grid.c
        return jnp.concatenate([jnp.where(c == 0, mine, got), jnp.where(c == 0, got, mine)], axis=1)


class Small:
    def __init__(self, grid):
        self.grid = grid

    def send_y(self, oth):
        self.got = self.grid.over_y(oth)
        return oth

    def send_c(self, own, token):
        self.value = own + after(self.got, token)
        self.got = self.grid.over_c(self.value)
        return self.value

    def send_x(self, token):
        self.value = self.value + after(self.got, token)
        self.got = self.grid.over_x(self.value)
        return self.value

    def send_z(self, token):
        self.value = self.value + after(self.got, token)
        self.got = [self.grid.shift_z(self.value, k) for k in (1, 2, 3)]
        return self.value

    def total(self, token):
        z = self.grid.z
        ring = jnp.stack([self.value, *[after(g, token) for g in self.got]])
        terms = [at(ring, 0, (z - s) % 4) for s in range(4)]
        return (terms[0] + terms[1]) + (terms[2] + terms[3])


def time_embed(step, d):
    half = d // 2
    frequency = jnp.exp(-math.log(10000.0) * jnp.arange(half, dtype=F32) / half)
    angles = step.astype(F32) * frequency[None, :]
    return jnp.concatenate([jnp.sin(angles), jnp.cos(angles)], axis=-1)


def block_lists(seg_own, seg_halo, rows):
    q = seg_own.reshape(-1, BQ)
    keys = jnp.concatenate([seg_own, seg_halo]).reshape(-1, BK)
    need = (keys[None, :, 0] <= q[:, None, -1]) & (keys[None, :, -1] >= q[:, None, 0])
    need = need.astype(jnp.int32)
    nkb = keys.shape[0]
    before = jnp.sum(need[:, None, :] * (jnp.arange(nkb)[None, None, :] < jnp.arange(nkb)[None, :, None]), axis=2)
    slot = jnp.arange(nkb)[None, :, None]
    pick = need[:, None, :] * (before[:, None, :] == slot)
    lst = jnp.sum(pick * jnp.arange(nkb)[None, None, :], axis=2)
    return jnp.sum(need, axis=1).astype(jnp.int32), lst.astype(jnp.int32).reshape(-1)


def finish(output, grad_input, grad_qkv, head_bias_sum, grad_out, grad_up, up_bias_sum, grad_down, grad_vectors):
    grad_qkv = grad_qkv.reshape(grad_qkv.shape[0], 3, -1).transpose(1, 0, 2)
    return (
        output,
        grad_input,
        grad_qkv,
        head_bias_sum,
        grad_out.T,
        grad_up,
        up_bias_sum,
        grad_down.T,
        grad_vectors,
    )


def per_device_fast(
    tokens_in,
    timesteps,
    segment_ids,
    padding,
    qkv_weight,
    head_bias,
    out_weight,
    up_weight,
    up_bias,
    down_weight,
    vectors,
    cotangent,
):
    rows, d = tokens_in.shape
    assert timesteps.shape[0] == 1
    LIMITED[0] = True
    grid = Grid()
    me, halo = grid.y, MAXDOC
    core = grid.c.reshape(1).astype(jnp.int32)
    own_start = me * rows
    sub = up_weight.shape[1] // 2
    width = qkv_weight.shape[2]
    by_rows = lambda a, c, q: lax.dynamic_slice_in_dim(a, (c * 4 + q) * (a.shape[0] // 8), a.shape[0] // 8, 0)
    by_cols = lambda a, c, q: lax.dynamic_slice(a, (q * (a.shape[0] // 4), c * sub), (a.shape[0] // 4, sub))
    flat_qkv = qkv_weight.reshape(3 * d, width)

    def outer(a, c, q):
        o = by_rows(out_weight, c, q)
        return jnp.concatenate([by_rows(a, c, q), o[:, :width], o[:, width:]], axis=0)

    def split_outer(mine, theirs):
        n, m = 3 * d // 8, out_weight.shape[0] // 8
        rows = n + 2 * m

        def moves(bits_ref, refs):
            for k in range(2):
                c = bits_ref[0] if k == 0 else 1 - bits_ref[0]
                for i in range(4):
                    at_row = lambda r: pl.ds(pl.multiple_of((c * 4 + i) * r, r), r)
                    yield refs[k].at[i * rows:i * rows + n, :], refs[2].at[at_row(n), :]
                    for j in range(2):
                        o = i * rows + n + j * m
                        yield refs[k].at[o:o + m, :], refs[3].at[at_row(m), j * width:(j + 1) * width]

        qkv, out = place(moves, [grid.c], [mine, theirs], [sds((3 * d, width), BF16), sds(out_weight.shape, BF16)])
        return qkv.reshape(qkv_weight.shape), out

    fq = Fetch(grid, flat_qkv, False, outer)
    fu = Fetch(grid, up_weight, False, by_cols)
    fd = Fetch(grid, down_weight, True, by_rows)
    small_w = jnp.concatenate([head_bias.reshape(-1), up_bias])
    small_o = grid.over_y(small_w)
    fq.prepare()
    begin = [fq.send_y(), small_w]

    emb = time_embed(timesteps[:, None], d)
    seg, pad = segment_ids[0], padding[0]
    seg_own = lax.dynamic_slice_in_dim(seg, own_start, rows)
    pad_own = lax.dynamic_slice_in_dim(pad, own_start, rows)
    halo_start = jnp.where(me == 0, rows, own_start - halo)
    seg_halo = lax.dynamic_slice_in_dim(seg, halo_start, halo)
    pad_halo = lax.dynamic_slice_in_dim(pad, halo_start, halo)
    code = jnp.concatenate([jnp.where(pad_own == 0, seg_own, -1), jnp.where(pad_halo == 0, seg_halo, -1)])
    cnt, lst = block_lists(seg_own, seg_halo, rows)
    nkb = (rows + halo) // BK
    segq_row, code_col = seg_own[None, :], code[:, None]
    nb = head_bias.size

    far_blocks = (rows - halo) // BQ
    far = jnp.where(me == 0, 0, rows // BQ - far_blocks).reshape(1).astype(jnp.int32)
    near = jnp.where(me == 0, far_blocks, 0).reshape(1).astype(jnp.int32)
    zero = jnp.zeros((1,), jnp.int32)
    x_own, q0, k0, v0 = qkv_own(tokens_in, emb, qkv_weight, head_bias, deps=begin)
    small_o = after(small_o, k0)
    ops = [fq.first(k0), small_o]
    edge = jnp.where(me == 0, rows - halo, 0)
    halo_op = lax.dynamic_slice_in_dim(after(tokens_in, ops[0]), edge, halo, 0)
    halo_tok = grid.over_y(halo_op)
    part = attn_fwd(far, far_blocks, cnt, lst, nkb, q0, [k0], [v0], segq_row, code_col, deps=[*ops, halo_op])
    ops = [*Fetch.second([fq], part[1]), fu.prepare(part[1]), fd.prepare(part[1])]
    x_halo, kh0, vh0 = kv_halo(after(halo_tok, part[1]), emb, qkv_weight, head_bias, deps=ops)
    ops = [fu.send_y(kh0), fd.send_y(kh0)]
    kv0 = ([k0, kh0], [v0, vh0], segq_row, code_col)
    part = attn_fwd(near, 1, cnt, lst, nkb, q0, *kv0, into=part, deps=ops)
    ops = Fetch.third([fq], part[1])
    o0, lse0 = attn_fwd(near + 1, rows // BQ - far_blocks - 1, cnt, lst, nkb, q0, *kv0, into=part, deps=ops)
    hb_o, up_b_o = small_o[:nb].reshape(head_bias.shape), small_o[nb:].reshape(1, -1)
    qkv_o, out_o = split_outer(fq.op, fq.last(lse0))
    out_ws = [out_weight, out_o]
    _, q1, k1, v1 = qkv_own(tokens_in, emb, qkv_o, hb_o)
    _, kh1, vh1 = kv_halo(halo_tok, emb, qkv_o, hb_o, deps=[q1])
    ops = [fu.first(kh1), fd.first(kh1)]
    o1, lse1 = attn_fwd(zero, rows // BQ, cnt, lst, nkb, q1, [k1, kh1], [v1, vh1], segq_row, code_col, deps=ops)
    ops = Fetch.second([fu, fd], lse1)
    xhat1, normed, rstd1 = out_norm(tokens_in, emb, vectors, [o0, o1], out_ws, deps=ops)
    up_b = up_bias.reshape(1, -1)
    (a0, b0), (ga0, gb0) = ffn_up(core, normed, [(up_weight, 0, up_b, 0), (up_weight, 1, up_b, 1)], sub)
    ops = Fetch.third([fu, fd], ga0)
    b0_got, normed_got = grid.over_c(b0), grid.over_c(normed)
    (a1,), (ga1,) = ffn_up(core, normed, [(fu.op, None, up_b_o, 0)], sub, deps=ops)
    up_b1, down_b1 = fu.last(ga1), fd.last(ga1)
    (b1,), (gb1,) = ffn_up(core, normed, [(up_b1, None, up_b_o, 1)], sub, deps=[ga1])
    b1_got = grid.over_c(b1)
    output, d_down, sums2 = ffn_down(
        core, normed, cotangent, vectors, [a0, b0, a1, b1], [(down_weight, 0), (down_weight, 1), (fd.op, None), (down_b1, None)]
    )

    d_got = grid.over_c(d_down)
    dn1, (ua1, ub1), us1 = ffn_dup(core, d_down, [(fu.op, None, fd.op, None, ga1), (up_b1, None, down_b1, None, gb1)], sub)
    ub1_got = grid.over_c(ub1)
    gd1, gd0 = wide_grad([d_down, after(d_got, ua1)], [(a1, after(b1_got, d_down)), (a0, after(b0_got, d_down))], deps=[ua1])
    rd = Reduce(grid, gd0[0], gd1[0], gd0[1], gd1[1])
    both = ("own_b", "oth_b")
    ops = [rd.a_over_y(), rd.b_over_x(both)]
    dn0, (ua0, ub0), us0 = ffn_dup(core, d_down, [(up_weight, 0, down_weight, 0, ga0), (up_weight, 1, down_weight, 1, gb0)], sub, deps=ops)
    ub0_got = grid.over_c(ub0)
    got = rd.take(dn0)
    d_attn, sums1, dm0, dm1 = norm_bwd([d_down, dn1, dn0], xhat1, rstd1, vectors, out_ws)
    ops = [rd.a_over_x(), rd.b_over_y(), *got]
    *og, os = grad_tn(core, [d_attn], [o0, o1], deps=[sums1, *ops])
    ro = Reduce(grid)
    ops = [ro.cores(("own_a", "oth_a"), *og)]
    gu1, gu0 = wide_grad([normed, after(normed_got, sums1)], [(ua1, after(ub1_got, sums1)), (ua0, after(ub0_got, sums1))], deps=ops)
    ru = Reduce(grid, gu0[0], gu1[0], gu0[1], gu1[1])
    got = rd.take(gu0[1]) + ro.take(gu0[1])
    ops = [*rd.over_z(), ru.a_over_y(), ru.b_over_x(both), *got]
    *dqkv1, hs1 = attn_bwd(cnt, lst, nkb, q1, [k1, kh1], [v1, vh1], dm1, o1, lse1, segq_row, code_col, deps=ops)
    got = ru.take(dqkv1[0]) + rd.take(dqkv1[0])
    ops = [ru.a_over_x(), ru.b_over_y(), *got]
    rq = Reduce(grid)
    *qg1, gt1 = grad_tn(core, [x_own, x_halo], dqkv1, deps=ops)
    got = []
    rq.cores(("oth_a", "oth_b"), *qg1)
    got += rq.take(gt1)
    vec6 = jnp.concatenate([sums1[:2], sums2[:2], sums1[2:3], sums2[2:3]], axis=0)
    up_sum = lambda us: jnp.where(grid.c == 0, jnp.concatenate(us, axis=0), jnp.concatenate(us[::-1], axis=0))
    head_sum = lambda hs: hs.reshape(1, -1)
    small_sums = lambda us, hs: jnp.concatenate([vec6, up_sum(us), head_sum(hs)], axis=0)
    small = Small(grid)
    ops = [rq.a_over_y(), rq.b_over_x(("oth_b",)), ro.a_over_y(), small.send_y(small_sums(us1, hs1)), *got]
    *dqkv0, hs0 = attn_bwd(cnt, lst, nkb, q0, [k0, kh0], [v0, vh0], dm0, o0, lse0, segq_row, code_col, deps=ops)
    got = rq.take(dqkv0[0]) + ro.take(dqkv0[0]) + ru.take(dqkv0[0])
    ops = [rq.b_over_y(), ro.a_over_x(), *ru.over_z(), small.send_c(small_sums(us0, hs0), hs0), *got]
    *qg0, gt0 = grad_tn(core, [x_own, x_halo], dqkv0, deps=ops)
    got = rq.take(gt0) + ro.take(gt0)
    ops = [rq.cores(("own_a", "own_b"), *qg0), small.send_x(gt0), *got]
    pairs = [(g[c], w, c) for g, w in ((dqkv0, qkv_weight), (dqkv1, qkv_o)) for c in range(3)]
    kv_pairs = [(g, (w, c)) for g, w, c in pairs if c]
    halo_grad = in_grad(None, [g for g, _ in kv_pairs], [w for _, w in kv_pairs], rows, halo, deps=ops)
    got = rq.take(halo_grad) + ru.take(gt0)
    back = grid.over_y(halo_grad)
    ops = [rq.a_over_x(), rq.b_over_x(("own_b",)), small.send_z(halo_grad), halo_grad, *got]
    own_grad = in_grad(d_attn, [g for g, _, _ in pairs], [(w, c) for _, w, c in pairs], 0, rows, deps=ops)
    rq.take(own_grad)
    token = rq.over_z(ro)[0]
    for r in (rd, ru):
        r.z_got = [after(a, token) for a in r.z_got]
        r.ends()
        r.take(token)
    near_rows = (jnp.arange(rows // halo) == 1 - me)[:, None, None]
    own_grad, back = after(own_grad, token), after(back, token).astype(F32)
    grad_input = (own_grad.reshape(rows // halo, halo, d).astype(F32) + jnp.where(near_rows, back[None], 0.0)).astype(BF16).reshape(rows, d)
    small = small.total(token)
    rq.take(token)
    total = rq.total()
    qkv_cols = 3 * width
    return finish(
        output, grad_input, total[:, :qkv_cols], small[8:].reshape(2, -1), total[:, qkv_cols:], ru.result(),
        small[6:8].reshape(-1), rd.result(), small[:6],
    )


def per_device(
    mp_size,
    tokens_in,
    timesteps,
    segment_ids,
    padding,
    qkv_weight,
    head_bias,
    out_weight,
    up_weight,
    up_bias,
    down_weight,
    vectors,
    cotangent,
):
    rows, d = tokens_in.shape
    assert timesteps.shape[0] == 1
    LIMITED[0] = False
    me = lax.axis_index("mp")
    own_start = me * rows
    emb = time_embed(timesteps[:, None], d)
    seg, pad = segment_ids[0], padding[0]
    seg_own = lax.dynamic_slice_in_dim(seg, own_start, rows)
    pad_own = lax.dynamic_slice_in_dim(pad, own_start, rows)
    halo_tok = lax.all_gather(tokens_in, "mp", axis=0, tiled=True)
    place = jnp.arange(SEQ, dtype=jnp.int32)
    pad_halo = jnp.where((place >= own_start) & (place < own_start + rows), 1, pad)
    code = jnp.concatenate([jnp.where(pad_own == 0, seg_own, -1), jnp.where(pad_halo == 0, seg, -1)])
    cnt, lst = block_lists(seg_own, seg, rows)
    nkb = (rows + SEQ) // BK
    segq_row, code_col = seg_own[None, :], code[:, None]
    gather = lambda a, axis: lax.all_gather(a, "mp", axis=axis, tiled=True)
    qkv_w, out_w, up_w, down_w = gather(qkv_weight, 2), gather(out_weight, 0), gather(up_weight, 1), gather(down_weight, 0)
    hb, up_b = gather(head_bias, 1), gather(up_bias, 0).reshape(1, -1)

    x_own, q, k, v = qkv_own(tokens_in, emb, qkv_w, hb)
    x_halo, kh, vh = kv_halo(halo_tok, emb, qkv_w, hb)
    k, v = [k, kh], [v, vh]
    o, lse = attn_fwd(jnp.zeros((1,), jnp.int32), rows // BQ, cnt, lst, nkb, q, k, v, segq_row, code_col)
    xhat1, normed, rstd1 = out_norm(tokens_in, emb, vectors, [o], [out_w])
    core, hidden = jnp.zeros((1,), jnp.int32), up_w.shape[1]
    acts, gps = ffn_up(core, normed, [(up_w, None, up_b, None)], hidden)
    output, d_down, sums2 = ffn_down(core, normed, cotangent, vectors, acts, [(down_w, None)])

    dn, dups, (up_sum,) = ffn_dup(core, d_down, [(up_w, None, down_w, None, gps[0])], hidden)
    grad_up = jnp.concatenate(wide_grad([normed], [dups])[0], axis=1)
    grad_down = jnp.concatenate(wide_grad([d_down], [acts])[0], axis=1)
    d_attn, sums1, d_mixed = norm_bwd([d_down, dn], xhat1, rstd1, vectors, [out_w])
    grad_out, _ = grad_tn(None, [d_attn], [o])
    *d_qkv, head_sum = attn_bwd(cnt, lst, nkb, q, k, v, d_mixed, o, lse, segq_row, code_col)
    grad_qkv, _ = grad_tn(None, [x_own, x_halo], d_qkv)
    halo_grad = in_grad(None, d_qkv[1:], [(qkv_w, 1), (qkv_w, 2)], rows, SEQ)
    own_grad = in_grad(d_attn, d_qkv, [(qkv_w, c) for c in range(3)], 0, rows)
    back = lax.psum_scatter(halo_grad, "mp", scatter_dimension=0, tiled=True)
    grad_input = (own_grad.astype(F32) + back.astype(F32)).astype(BF16)

    packed = [sums1[:2], sums2[:2], sums1[2:3], sums2[2:3], head_sum, up_sum.reshape(-1, d)]
    packed = lax.psum(jnp.concatenate(packed, axis=0), ("dp", "mp"))
    local = head_bias.shape[1]
    head_bias_sum = lax.dynamic_slice_in_dim(packed[6:8], me * local, local, 1)
    local = up_bias.shape[0]
    up_bias_sum = lax.dynamic_slice_in_dim(packed[8:].reshape(-1), me * local, local, 0)

    def scatter(g, groups):
        n = g.shape[1] // groups // mp_size
        g = lax.psum_scatter(g, "dp", scatter_dimension=0, tiled=True)
        g = g.reshape(-1, groups, mp_size, n).transpose(2, 0, 1, 3)
        return lax.psum_scatter(g, "mp", scatter_dimension=0, tiled=False).astype(F32).reshape(-1, groups * n)

    return finish(
        output,
        grad_input,
        scatter(grad_qkv, 3),
        head_bias_sum,
        scatter(grad_out, 1),
        scatter(grad_up, 1),
        up_bias_sum,
        scatter(grad_down, 1),
        packed[:6],
    )


def solution(mesh):
    fast = dict(mesh.shape) == {"dp": 16, "mp": 2}
    return jax.shard_map(
        per_device_fast if fast else partial(per_device, mesh.shape["mp"]),
        mesh=mesh,
        in_specs=(
            P(("dp", "mp"), None),
            P("dp"),
            P("dp", None),
            P("dp", None),
            P(None, None, "mp"),
            P(None, "mp"),
            P("mp", None),
            P(None, "mp"),
            P("mp"),
            P("mp", None),
            P(),
            P(("dp", "mp"), None),
        ),
        out_specs=(
            P(("dp", "mp"), None),
            P(("dp", "mp"), None),
            P(None, "dp", "mp"),
            P(None, "mp"),
            P("mp", "dp"),
            P("dp", "mp"),
            P("mp"),
            P("mp", "dp"),
            P(),
        ),
        check_vma=False,
    )
```

```python
from functools import partial
import math

import jax
import jax.numpy as jnp
from jax import lax
from jax.experimental import pallas as pl
from jax.experimental.pallas import tpu as pltpu
from jax.sharding import PartitionSpec as P

HEAD_DIM = 64
SEQ = 2048
MAXDOC = 512
BQ = 256
BK = 256
RB = 256
HB = 512
SCALE = 300.0
VMEM_MIB = {
    "qkv_own": 12, "kv_halo": 12, "attn_fwd": 12, "out_norm": 14, "ffn_up": 22, "ffn_down": 24,
    "ffn_dup": 25, "wide_grad": 24, "norm_bwd": 14, "grad_tn": 16, "attn_bwd": 18, "in_grad": 14, "place": 18,
}
LIMITED = [True]
GROUP = 512
NEG_FILL = -1e30
F32 = jnp.float32
BF16 = jnp.bfloat16


def nt(a, b):
    return lax.dot_general(a, b, (((1,), (1,)), ((), ())), preferred_element_type=F32)


def nn(a, b):
    return lax.dot_general(a, b, (((1,), (0,)), ((), ())), preferred_element_type=F32)


def tn(a, b):
    return lax.dot_general(a, b, (((0,), (0,)), ((), ())), preferred_element_type=F32)


def cost(flops, nbytes, trans=0):
    return pl.CostEstimate(flops=int(flops * SCALE), bytes_accessed=int(nbytes * SCALE), transcendentals=int(trans * SCALE))


def whole(shape):
    return pl.BlockSpec(shape, lambda *_: (0,) * len(shape))


def sds(shape, dtype):
    return jax.ShapeDtypeStruct(shape, dtype)


def call(kernel, args, *, grid, in_specs, out_specs, out_shape, cost_estimate, name, prefetch=(), deps=(), scratch=(), aliases=None):
    first, skip, offset = len(prefetch) + len(args), len(deps), len(prefetch)

    def body(*refs):
        kernel(*refs[:first], *refs[first + skip:])

    return pl.pallas_call(
        body,
        grid_spec=pltpu.PrefetchScalarGridSpec(
            num_scalar_prefetch=offset,
            grid=grid,
            in_specs=list(in_specs) + [pl.BlockSpec(memory_space=pl.ANY)] * skip,
            out_specs=out_specs,
            scratch_shapes=list(scratch),
        ),
        out_shape=out_shape,
        input_output_aliases={k + offset: v for k, v in (aliases or {}).items()},
        cost_estimate=cost_estimate,
        compiler_params=pltpu.CompilerParams(vmem_limit_bytes=VMEM_MIB[name] << 20) if LIMITED[0] else None,
        name=name,
    )(*prefetch, *args, *deps)


def after(x, *deps):
    return lax.optimization_barrier((x, *deps))[0] if deps else x


def qkv_own_kernel(tok_ref, emb_ref, w_ref, hb_ref, x_ref, q_ref, k_ref, v_ref):
    x = (tok_ref[...].astype(F32) + emb_ref[...]).astype(BF16)
    x_ref[...] = x
    q_ref[...] = (nn(x, w_ref[0]) + hb_ref[0:1]).astype(BF16)
    k_ref[...] = nn(x, w_ref[1]).astype(BF16)
    v_ref[...] = (nn(x, w_ref[2]) + hb_ref[1:2]).astype(BF16)


def qkv_own(tok, emb, w, hb, deps=()):
    rows, d = tok.shape
    width = w.shape[2]
    row = lambda n: pl.BlockSpec((RB, n), lambda i, *_: (i, 0))
    return call(
        qkv_own_kernel,
        (tok, emb, w, hb),
        deps=deps,
        grid=(rows // RB,),
        in_specs=[row(d), whole((1, d)), whole(w.shape), whole(hb.shape)],
        out_specs=[row(d), row(width), row(width), row(width)],
        out_shape=[sds((rows, d), BF16)] + [sds((rows, width), BF16)] * 3,
        cost_estimate=cost(6 * rows * d * width, 2 * (2 * rows * d + 3 * rows * width + 3 * d * width)),
        name="qkv_own",
    )


def kv_halo_kernel(tok_ref, emb_ref, w_ref, hb_ref, x_ref, k_ref, v_ref):
    x = (tok_ref[...].astype(F32) + emb_ref[...]).astype(BF16)
    x_ref[...] = x
    k_ref[...] = nn(x, w_ref[1]).astype(BF16)
    v_ref[...] = (nn(x, w_ref[2]) + hb_ref[1:2]).astype(BF16)


def kv_halo(tok, emb, w, hb, deps=()):
    rows, d = tok.shape
    width = w.shape[2]
    row = lambda n: pl.BlockSpec((RB, n), lambda i, *_: (i, 0))
    return call(
        kv_halo_kernel,
        (tok, emb, w, hb),
        deps=deps,
        grid=(rows // RB,),
        in_specs=[row(d), whole((1, d)), whole(w.shape), whole(hb.shape)],
        out_specs=[row(d), row(width), row(width)],
        out_shape=[sds((rows, d), BF16)] + [sds((rows, width), BF16)] * 2,
        cost_estimate=cost(4 * rows * d * width, 2 * (2 * rows * d + 2 * rows * width + 3 * d * width)),
        name="kv_halo",
    )


def pair_stack(x2):
    lane = lax.broadcasted_iota(jnp.int32, (1, 128), 1)
    first = (lane < HEAD_DIM).astype(F32).astype(BF16)
    second = (lane >= HEAD_DIM).astype(F32).astype(BF16)
    return jnp.concatenate([x2 * first, x2 * second], axis=0)


def pair_merge(x):
    half = x.shape[0] // 2
    lane = lax.broadcasted_iota(jnp.int32, (half, 128), 1)
    return jnp.where(lane < HEAD_DIM, x[:half], x[half:])


def load_keys(srcs, dsts, sem, group):
    copies = []
    for pieces, dst in zip(srcs, dsts):
        off = 0
        for src in pieces:
            cols = pl.ds(pl.multiple_of(group * GROUP, GROUP), GROUP)
            copies.append(pltpu.make_async_copy(src.at[:, cols], dst.at[off:off + src.shape[0], :], sem.at[len(copies)]))
            off += src.shape[0]
    for c in copies:
        c.start()
    for c in copies:
        c.wait()


def attn_fwd_kernel(pieces, nkb, pairs, filled, base_ref, cnt_ref, list_ref, q_ref, segq_ref, codek_ref, *refs):
    k_srcs, v_srcs, refs = refs[:pieces], refs[pieces:2 * pieces], refs[2 * pieces + 2 * filled:]
    o_ref, lse_ref, k_ref, v_ref, qs_scr, m_scr, l_scr, acc_scr, sem = refs

    @pl.when(pl.program_id(1) == 0)
    def _():
        load_keys((k_srcs, v_srcs), (k_ref, v_ref), sem, pl.program_id(0))

    qb = pl.program_id(1) + base_ref[0]
    count = cnt_ref[qb]
    for p in range(pairs):
        qs_scr[p] = pair_stack(q_ref[:, 128 * p:128 * (p + 1)] * jnp.asarray(0.125, BF16))
    m_scr[...] = jnp.full(m_scr.shape, -3e38, F32)
    l_scr[...] = jnp.zeros(l_scr.shape, F32)
    acc_scr[...] = jnp.zeros(acc_scr.shape, F32)

    def step(s, carry):
        kb = list_ref[qb * nkb + s]
        off = pl.multiple_of(kb * BK, BK)
        kpos = kb * BK + lax.broadcasted_iota(jnp.int32, (BK, BQ), 0)
        qpos = qb * BQ + lax.broadcasted_iota(jnp.int32, (BK, BQ), 1)
        live = (codek_ref[pl.ds(off, BK), :] == segq_ref[...]) | (qpos == kpos)
        bias = jnp.where(live, 0.0, NEG_FILL).astype(F32)
        bias = jnp.concatenate([bias, bias], axis=1)
        scs = [nt(k_ref[pl.ds(off, BK), 128 * p:128 * (p + 1)], qs_scr[p]) for p in range(pairs)]
        es = []
        for p in range(pairs):
            sc = scs[p] + bias
            old = m_scr[p:p + 1]
            new = jnp.maximum(old, jnp.max(sc, axis=0, keepdims=True))
            e = jnp.exp(sc - new)
            fade = jnp.exp(old - new)
            m_scr[p:p + 1] = new
            l_scr[p:p + 1] = l_scr[p:p + 1] * fade + jnp.sum(e, axis=0, keepdims=True)
            es.append((e.astype(BF16), fade))
        for p in range(pairs):
            acc_scr[p] = acc_scr[p] * es[p][1] + tn(v_ref[pl.ds(off, BK), 128 * p:128 * (p + 1)], es[p][0])
        return carry

    lax.fori_loop(0, count, step, 0)
    lse = m_scr[...] + jnp.log(l_scr[...])
    for p in range(pairs):
        o = acc_scr[p] / l_scr[p:p + 1]
        o = jnp.concatenate([o[:HEAD_DIM, :BQ], o[HEAD_DIM:, BQ:]], axis=0)
        o_ref[:, 128 * p:128 * (p + 1)] = jnp.transpose(o).astype(BF16)
        lse_ref[2 * p:2 * p + 1, :] = lse[p:p + 1, :BQ]
        lse_ref[2 * p + 1:2 * p + 2, :] = lse[p:p + 1, BQ:]


def attn_fwd(base, nqb, cnt, lst, nkb, q, k, v, segq, codek, into=(), deps=()):
    rows, width = q.shape
    pieces, keys = len(k), sum(a.shape[0] for a in k)
    groups, pairs = width // GROUP, GROUP // 128
    est = nqb * BQ * 2 * BK * width
    qspec = lambda n: pl.BlockSpec((BQ, n), lambda g, i, b, *_: (i + b[0], g))
    lspec = pl.BlockSpec((2 * pairs, BQ), lambda g, i, b, *_: (g, i + b[0]))
    anyspec = pl.BlockSpec(memory_space=pl.ANY)
    args = [q, segq, codek, *k, *v, *into]
    first = 3 + 2 * pieces
    return call(
        partial(attn_fwd_kernel, pieces, nkb, pairs, len(into) // 2),
        args,
        prefetch=(base, cnt, lst),
        deps=deps,
        grid=(groups, nqb),
        in_specs=[qspec(GROUP), pl.BlockSpec((1, BQ), lambda g, i, b, *_: (0, i + b[0])), pl.BlockSpec((codek.shape[0], 1), lambda *_: (0, 0))]
        + [anyspec] * (len(args) - 3),
        out_specs=[qspec(GROUP), lspec],
        out_shape=[sds((rows, width), BF16), sds((2 * pairs * groups, rows), F32)],
        aliases={first: 0, first + 1: 1} if into else None,
        scratch=[
            pltpu.VMEM((keys, GROUP), BF16),
            pltpu.VMEM((keys, GROUP), BF16),
            pltpu.VMEM((pairs, 2 * BQ, 128), BF16),
            pltpu.VMEM((pairs, 2 * BQ), F32),
            pltpu.VMEM((pairs, 2 * BQ), F32),
            pltpu.VMEM((pairs, 128, 2 * BQ), F32),
            pltpu.SemaphoreType.DMA((2 * pieces,)),
        ],
        cost_estimate=cost(4 * est, 8 * rows * width, est // 32),
        name="attn_fwd",
    )


def attn_bwd_kernel(pieces, nkb, pairs, cnt_ref, list_ref, q_ref, do_ref, o_ref, lse_ref, segq_ref, codek_ref, *refs):
    k_srcs, v_srcs, refs = refs[:pieces], refs[pieces:2 * pieces], refs[2 * pieces:]
    dq_ref, dk_ref, dv_ref, sum_ref, k_ref, v_ref, qs_scr, ds_scr, row_scr, dq_scr, dk_scr, dv_scr, sem = refs
    qb = pl.program_id(1)

    @pl.when(qb == 0)
    def _():
        load_keys((k_srcs, v_srcs), (k_ref, v_ref), sem, pl.program_id(0))

    @pl.when(qb == 0)
    def _():
        dk_scr[...] = jnp.zeros(dk_scr.shape, F32)
        dv_scr[...] = jnp.zeros(dv_scr.shape, F32)

    count = cnt_ref[qb]
    lse_t = lse_ref[...]
    for p in range(pairs):
        cols = slice(128 * p, 128 * (p + 1))
        qs_scr[p] = pair_stack(q_ref[:, cols] * jnp.asarray(0.125, BF16))
        ds_scr[p] = pair_stack(do_ref[:, cols])
        prod = jnp.transpose(do_ref[:, cols].astype(F32) * o_ref[:, cols].astype(F32))
        da = jnp.sum(prod[:HEAD_DIM], axis=0, keepdims=True)
        db = jnp.sum(prod[HEAD_DIM:], axis=0, keepdims=True)
        row_scr[p, 0:1] = jnp.concatenate([lse_t[2 * p:2 * p + 1], lse_t[2 * p + 1:2 * p + 2]], axis=1)
        row_scr[p, 1:2] = jnp.concatenate([da, db], axis=1)
    dq_scr[...] = jnp.zeros(dq_scr.shape, F32)

    def step(s, carry):
        kb = list_ref[qb * nkb + s]
        off = pl.multiple_of(kb * BK, BK)
        kpos = kb * BK + lax.broadcasted_iota(jnp.int32, (BK, BQ), 0)
        qpos = qb * BQ + lax.broadcasted_iota(jnp.int32, (BK, BQ), 1)
        live = (codek_ref[pl.ds(off, BK), :] == segq_ref[...]) | (qpos == kpos)
        bias = jnp.where(live, 0.0, NEG_FILL).astype(F32)
        bias = jnp.concatenate([bias, bias], axis=1)
        for p in range(pairs):
            cols = slice(128 * p, 128 * (p + 1))
            k2 = k_ref[pl.ds(off, BK), cols]
            v2 = v_ref[pl.ds(off, BK), cols]
            sc = nt(k2, qs_scr[p]) + bias
            probs = jnp.exp(sc - row_scr[p, 0:1])
            dprobs = nt(v2, ds_scr[p])
            dsc = (probs * (dprobs - row_scr[p, 1:2])).astype(BF16)
            dv_scr[pl.ds(off, BK), cols] += nn(probs.astype(BF16), ds_scr[p])
            dk_scr[pl.ds(off, BK), cols] += nn(dsc, qs_scr[p])
            dq_scr[p] += tn(k2, dsc)
        return carry

    lax.fori_loop(0, count, step, 0)
    for p in range(pairs):
        dq = dq_scr[p] * 0.125
        dq = jnp.concatenate([dq[:HEAD_DIM, :BQ], dq[HEAD_DIM:, BQ:]], axis=0)
        dq = jnp.transpose(dq).astype(BF16)
        cols = slice(128 * p, 128 * (p + 1))
        dq_ref[:, cols] = dq
        so_far = jnp.where(qb == 0, 0.0, sum_ref[0:1, cols])
        sum_ref[0:1, cols] = so_far + jnp.sum(dq.astype(F32), axis=0, keepdims=True)

    @pl.when(qb == pl.num_programs(1) - 1)
    def _():
        dk_ref[...] = dk_scr[...].astype(BF16)
        dv_ref[...] = dv_scr[...].astype(BF16)
        sum_ref[1:2, :] = jnp.sum(dv_scr[...], axis=0, keepdims=True)


def attn_bwd(cnt, lst, nkb, q, k, v, do, o, lse, segq, codek, deps=()):
    rows, width = q.shape
    pieces, keys = len(k), sum(a.shape[0] for a in k)
    groups, pairs = width // GROUP, GROUP // 128
    est = rows * 2 * BK * width
    qspec = pl.BlockSpec((BQ, GROUP), lambda g, i, *_: (i, g))
    kspec = pl.BlockSpec((keys, GROUP), lambda g, i, *_: (0, g))
    return call(
        partial(attn_bwd_kernel, pieces, nkb, pairs),
        (q, do, o, lse, segq, codek, *k, *v),
        prefetch=(cnt, lst),
        deps=deps,
        grid=(groups, rows // BQ),
        in_specs=[
            qspec, qspec, qspec,
            pl.BlockSpec((2 * pairs, BQ), lambda g, i, *_: (g, i)),
            pl.BlockSpec((1, BQ), lambda g, i, *_: (0, i)),
            pl.BlockSpec((keys, 1), lambda g, i, *_: (0, 0)),
        ] + [pl.BlockSpec(memory_space=pl.ANY)] * (2 * pieces),
        out_specs=[qspec, kspec, kspec, pl.BlockSpec((2, GROUP), lambda g, i, *_: (0, g))],
        scratch=[
            pltpu.VMEM((keys, GROUP), BF16),
            pltpu.VMEM((keys, GROUP), BF16),
            pltpu.VMEM((pairs, 2 * BQ, 128), BF16),
            pltpu.VMEM((pairs, 2 * BQ, 128), BF16),
            pltpu.VMEM((pairs, 8, 2 * BQ), F32),
            pltpu.VMEM((pairs, 128, 2 * BQ), F32),
            pltpu.VMEM((keys, GROUP), F32),
            pltpu.VMEM((keys, GROUP), F32),
            pltpu.SemaphoreType.DMA((2 * pieces,)),
        ],
        out_shape=[sds((rows, width), BF16), sds((keys, width), BF16), sds((keys, width), BF16), sds((2, width), F32)],
        cost_estimate=cost(10 * est, 16 * rows * width, est // 32),
        name="attn_bwd",
    )


def row_mean(x):
    return jnp.mean(x, axis=-1, keepdims=True)


def out_norm_kernel(parts, tok_ref, emb_ref, vec_ref, *refs):
    mixed, weights = refs[:parts], refs[parts:2 * parts]
    xhat_ref, low_ref, rstd_ref = refs[2 * parts:]
    acc = tok_ref[...].astype(F32) + emb_ref[...] + vec_ref[4:5]
    for m, w in zip(mixed, weights):
        acc = acc + nn(m[...], w[...])
    centered = acc - row_mean(acc)
    rstd = lax.rsqrt(row_mean(centered * centered) + 1e-05)
    xhat = centered * rstd
    xhat_ref[...] = xhat.astype(BF16)
    rstd_ref[...] = jnp.broadcast_to(rstd, rstd_ref.shape)
    low_ref[...] = (xhat * vec_ref[0:1] + vec_ref[1:2]).astype(BF16)


def out_norm(tok, emb, vec, mixed, weights, deps=()):
    rows, d = tok.shape
    parts = len(mixed)
    row = lambda n: pl.BlockSpec((RB, n), lambda i, *_: (i, 0))
    return call(
        partial(out_norm_kernel, parts),
        (tok, emb, vec, *mixed, *weights),
        deps=deps,
        grid=(rows // RB,),
        in_specs=[row(d), whole((1, d)), whole(vec.shape)]
        + [row(m.shape[1]) for m in mixed]
        + [whole(w.shape) for w in weights],
        out_specs=[row(d), row(d), row(128)],
        out_shape=[sds((rows, d), BF16), sds((rows, d), BF16), sds((rows, 128), F32)],
        cost_estimate=cost(2 * rows * d * d, 8 * rows * d + 2 * d * d),
        name="out_norm",
    )


def gelu_pair(h):
    mag = jnp.abs(h)
    t = 1.0 / (1.0 + (0.3275911 * 0.7071067811865476) * mag)
    e = jnp.exp2((-0.5 * 1.4426950408889634) * (h * h))
    poly = t * (0.127414796 + t * (-0.142248368 + t * (0.7107068705 + t * (-0.7265760135 + t * 0.5307027145))))
    tail = poly * e
    phi = jnp.where(h < 0.0, tail, 1.0 - tail)
    return h * phi, phi + h * (e * 0.3989422804014327)


def pick(sel, per):
    if sel is None:
        return lambda j, core: j
    return lambda j, core: j + per * (core[0] if sel == 0 else 1 - core[0])


def ffn_up_kernel(n, core_ref, x_ref, *refs):
    ws, bs, acts, gps = refs[:n], refs[n:2 * n], refs[2 * n:3 * n], refs[3 * n:]
    rows = min(x_ref.shape[0], 1024)

    def chunk(i, carry):
        at_rows = pl.ds(pl.multiple_of(i * rows, rows), rows)
        for w, b, a, g in zip(ws, bs, acts, gps):
            h = nn(x_ref[at_rows, :], w[...]) + b[...]
            act, gp = gelu_pair(h)
            a[at_rows, :] = act.astype(BF16)
            g[at_rows, :] = gp.astype(BF16)
        return carry

    lax.fori_loop(0, x_ref.shape[0] // rows, chunk, 0)


def ffn_up(core, x, items, hidden, deps=()):
    rows, d = x.shape
    n, per = len(items), hidden // HB
    col = lambda r, sel: pl.BlockSpec((r, HB), lambda j, c: (0, pick(sel, per)(j, c)))
    out = call(
        partial(ffn_up_kernel, n),
        (x, *[i[0] for i in items], *[i[2] for i in items]),
        prefetch=(core,),
        deps=deps,
        grid=(per,),
        in_specs=[whole((rows, d))] + [col(d, i[1]) for i in items] + [col(1, i[3]) for i in items],
        out_specs=[col(rows, None)] * (2 * n),
        out_shape=[sds((rows, hidden), BF16)] * (2 * n),
        cost_estimate=cost(2 * rows * d * hidden * n, 2 * (rows * d + n * (d + 2 * rows) * hidden), rows * hidden * n),
        name="ffn_up",
    )
    return out[:n], out[n:]


def ffn_down_kernel(parts, core_ref, norm_ref, cot_ref, vec_ref, *refs):
    acts, weights = refs[:parts], refs[parts:2 * parts]
    out_ref, dlow_ref, sums_ref = refs[2 * parts:]
    acc = norm_ref[...].astype(F32) + vec_ref[5:6]
    for a, w in zip(acts, weights):
        acc = acc + nn(a[...], w[...])
    centered = acc - row_mean(acc)
    rstd = lax.rsqrt(row_mean(centered * centered) + 1e-05)
    xhat = centered * rstd
    out_ref[...] = (xhat * vec_ref[2:3] + vec_ref[3:4]).astype(BF16)
    cot = cot_ref[...].astype(F32)
    gg = cot * vec_ref[2:3]
    dres = rstd * (gg - row_mean(gg) - xhat * row_mean(gg * xhat))
    low = dres.astype(BF16)
    dlow_ref[...] = low

    @pl.when(pl.program_id(0) == 0)
    def _():
        sums_ref[...] = jnp.zeros(sums_ref.shape, F32)

    sums_ref[0:1] += jnp.sum(cot * xhat, axis=0, keepdims=True)
    sums_ref[1:2] += jnp.sum(cot, axis=0, keepdims=True)
    sums_ref[2:3] += jnp.sum(low.astype(F32), axis=0, keepdims=True)


def ffn_down(core, normed, cot, vec, acts, weights, deps=()):
    rows, d = normed.shape
    parts = len(acts)
    hidden = sum(a.shape[1] for a in acts)
    row = lambda n: pl.BlockSpec((RB, n), lambda i, *_: (i, 0))
    wspec = lambda a, sel: pl.BlockSpec((a.shape[1], d), lambda i, c: (pick(sel, 1)(0, c), 0))
    return call(
        partial(ffn_down_kernel, parts),
        (normed, cot, vec, *acts, *[w for w, _ in weights]),
        prefetch=(core,),
        deps=deps,
        grid=(rows // RB,),
        in_specs=[row(d), row(d), whole(vec.shape)]
        + [row(a.shape[1]) for a in acts]
        + [wspec(a, sel) for a, (_, sel) in zip(acts, weights)],
        out_specs=[row(d), row(d), whole((8, d))],
        out_shape=[sds((rows, d), BF16), sds((rows, d), BF16), sds((8, d), F32)],
        cost_estimate=cost(2 * rows * d * hidden, 8 * rows * d + 2 * d * hidden + 2 * rows * hidden),
        name="ffn_down",
    )


def ffn_dup_kernel(n, core_ref, d_ref, *refs):
    ups, downs, gps, refs = refs[:n], refs[n:2 * n], refs[2 * n:3 * n], refs[3 * n:]
    dn_ref, dups, sums, acc_ref = refs[0], refs[1:n + 1], refs[n + 1:2 * n + 1], refs[2 * n + 1]
    rows = min(d_ref.shape[0], 512)
    first = pl.program_id(0) == 0
    last = pl.program_id(0) == pl.num_programs(0) - 1

    for s in sums:
        s[...] = jnp.zeros(s.shape, F32)

    def chunk(i, carry):
        at_rows = pl.ds(pl.multiple_of(i * rows, rows), rows)
        total = None
        for up, down, gp, dup_ref, s in zip(ups, downs, gps, dups, sums):
            dup = (nt(d_ref[at_rows, :], down[...]) * gp[at_rows, :].astype(F32)).astype(BF16)
            dup_ref[at_rows, :] = dup
            s[...] += jnp.sum(dup.astype(F32), axis=0, keepdims=True)
            term = nt(dup, up[...])
            total = term if total is None else total + term
        acc_ref[at_rows, :] = jnp.where(first, total, acc_ref[at_rows, :] + total)
        return carry

    lax.fori_loop(0, d_ref.shape[0] // rows, chunk, 0)

    @pl.when(last)
    def _():
        dn_ref[...] = acc_ref[...].astype(BF16)


def ffn_dup(core, dlow, items, hidden, deps=()):
    rows, d = dlow.shape
    n, per = len(items), hidden // HB
    col = lambda r, sel: pl.BlockSpec((r, HB), lambda j, c: (0, pick(sel, per)(j, c)))
    down = lambda sel: pl.BlockSpec((HB, d), lambda j, c: (pick(sel, per)(j, c), 0))
    out = call(
        partial(ffn_dup_kernel, n),
        (dlow, *[i[0] for i in items], *[i[2] for i in items], *[i[4] for i in items]),
        prefetch=(core,),
        deps=deps,
        grid=(per,),
        in_specs=[whole((rows, d))] + [col(d, i[1]) for i in items] + [down(i[3]) for i in items] + [col(rows, None)] * n,
        out_specs=[whole((rows, d))] + [col(rows, None)] * n + [col(1, None)] * n,
        scratch=[pltpu.VMEM((rows, d), F32)],
        out_shape=[sds((rows, d), BF16)] + [sds((rows, hidden), BF16)] * n + [sds((1, hidden), F32)] * n,
        cost_estimate=cost(4 * rows * d * hidden * n, 2 * n * (2 * d + 2 * rows) * hidden + 4 * rows * d),
        name="ffn_dup",
    )
    return out[0], out[1:n + 1], out[n + 1:]


def put_transposed(dst, tmp, src, core):
    if core is None:
        dst[...] = jnp.transpose(src)
        return
    tmp[...] = jnp.transpose(src)
    d = tmp.shape[0]
    for g in range(d // 128):
        mine = pl.multiple_of(g * 128 + core * 64, 64)
        other = pl.multiple_of(g * 128 + (1 - core) * 64, 64)
        dst[g * 64:(g + 1) * 64, :] = tmp[pl.ds(mine, 64), :]
        dst[d // 2 + g * 64:d // 2 + (g + 1) * 64, :] = tmp[pl.ds(other, 64), :]


def put_grad(keep_ref, send_ref, lt, right):
    d = lt.shape[0]
    if send_ref is None:
        for j in range(d // RB):
            keep_ref[j * RB:(j + 1) * RB, :] = nn(lt[j * RB:(j + 1) * RB, :], right).astype(BF16)
        return
    half = d // 2
    keep_ref[...] = nn(lt[:half, :], right).astype(BF16)
    send_ref[...] = nn(lt[half:, :], right).astype(BF16)


def wide_grad_kernel(n, count, steps, *refs):
    lefts, rights, refs = refs[:n], refs[n:n + n * count], refs[n + n * count:]
    outs, lt = refs[:count * steps], refs[count * steps]
    step = pl.program_id(0)
    cols, off = [], 0
    for left in lefts:
        cols.append(slice(off, off + left.shape[0]))
        off += left.shape[0]

    @pl.when(step == 0)
    def _():
        for c, left in zip(cols, lefts):
            lt[:, c] = jnp.transpose(left[...])

    d = lt.shape[0]
    for p in range(count):
        mine = rights[p * n:(p + 1) * n]
        for s in range(steps):
            @pl.when(step == s)
            def _(s=s, p=p, mine=mine):
                out = outs[p * steps + s]

                def chunk(i, carry):
                    r = pl.ds(pl.multiple_of(i * 1024, 1024), 1024)
                    acc = nn(lt[r, cols[0]], mine[0][...])
                    for c, right in zip(cols[1:], mine[1:]):
                        acc = acc + nn(lt[r, c], right[...])
                    out[r, :] = acc.astype(BF16)
                    return carry

                lax.fori_loop(0, d // 1024, chunk, 0)


def wide_grad(lefts, items, deps=()):
    d, hidden = lefts[0].shape[1], items[0][0].shape[1]
    n, count, steps = len(lefts), len(items), hidden // HB
    rows = sum(a.shape[0] for a in lefts)
    flat = [a for i in items for a in i]
    out = call(
        partial(wide_grad_kernel, n, count, steps),
        (*lefts, *flat),
        deps=deps,
        grid=(steps,),
        in_specs=[whole(a.shape) for a in lefts] + [pl.BlockSpec((a.shape[0], HB), lambda j: (0, j)) for a in flat],
        out_specs=[whole((d, HB))] * (count * steps),
        scratch=[pltpu.VMEM((d, rows), BF16)],
        out_shape=[sds((d, HB), BF16)] * (count * steps),
        cost_estimate=cost(2 * rows * d * hidden * count, 2 * (rows * d + count * (rows + d) * hidden)),
        name="wide_grad",
    )
    return [out[p * steps:(p + 1) * steps] for p in range(count)]


def norm_bwd_kernel(parts, terms, xhat_ref, rstd_ref, vec_ref, *refs):
    weights, dns, refs = refs[:parts], refs[parts:parts + terms], refs[parts + terms:]
    dlow_ref, sums_ref, mixes = refs[0], refs[1], refs[2:]
    dn = dns[0][...].astype(F32)
    for t in dns[1:]:
        dn = dn + t[...].astype(F32)
    xhat = xhat_ref[...].astype(F32)
    gg = dn * vec_ref[0:1]
    low = (rstd_ref[:, :1] * (gg - row_mean(gg) - xhat * row_mean(gg * xhat))).astype(BF16)
    dlow_ref[...] = low

    @pl.when(pl.program_id(0) == 0)
    def _():
        sums_ref[...] = jnp.zeros(sums_ref.shape, F32)

    sums_ref[0:1] += jnp.sum(dn * xhat, axis=0, keepdims=True)
    sums_ref[1:2] += jnp.sum(dn, axis=0, keepdims=True)
    sums_ref[2:3] += jnp.sum(low.astype(F32), axis=0, keepdims=True)
    for w, m in zip(weights, mixes):
        m[...] = nt(low, w[...]).astype(BF16)


def norm_bwd(dns, xhat, rstd, vec, weights, deps=()):
    rows, d = xhat.shape
    parts, terms = len(weights), len(dns)
    row = lambda n: pl.BlockSpec((RB, n), lambda i, *_: (i, 0))
    return call(
        partial(norm_bwd_kernel, parts, terms),
        (xhat, rstd, vec, *weights, *dns),
        deps=deps,
        grid=(rows // RB,),
        in_specs=[row(d), row(128), whole(vec.shape)] + [whole(w.shape) for w in weights] + [row(d)] * terms,
        out_specs=[row(d), whole((8, d))] + [row(w.shape[0]) for w in weights],
        out_shape=[sds((rows, d), BF16), sds((8, d), F32)] + [sds((rows, w.shape[0]), BF16) for w in weights],
        cost_estimate=cost(2 * rows * d * d, 14 * rows * d + 2 * d * d),
        name="norm_bwd",
    )


def grad_tn_kernel(split, lefts, count, core_ref, *refs):
    left_refs, rights, refs = refs[:lefts], refs[lefts:lefts + count], refs[lefts + count:]
    if split:
        keep_ref, send_ref, done_ref, lt_scr, tmp_scr = refs
    else:
        keep_ref, done_ref, lt_scr, tmp_scr = refs
        send_ref = None
    off = 0
    for left in left_refs:
        cols = slice(off, off + left.shape[0])
        put_transposed(lt_scr.at[:, cols], tmp_scr.at[:, cols], left[...], core_ref[0] if split else None)
        off += left.shape[0]
    done_ref[...] = jnp.zeros(done_ref.shape, F32)
    width = rights[0].shape[1]
    for c, right in enumerate(rights):
        cols = slice(c * width, (c + 1) * width)
        put_grad(keep_ref.at[:, cols], None if send_ref is None else send_ref.at[:, cols], lt_scr.at[:, :right.shape[0]], right[...])


def grad_tn(core, lefts, rights, deps=()):
    rows, d = sum(a.shape[0] for a in lefts), lefts[0].shape[1]
    width = rights[0].shape[1]
    n = width * len(rights)
    split = core is not None
    gshape = [sds((d // 2, n), BF16)] * 2 if split else [sds((d, n), BF16)]
    return call(
        partial(grad_tn_kernel, split, len(lefts), len(rights)),
        (*lefts, *rights),
        prefetch=(core if split else jnp.zeros((1,), jnp.int32),),
        deps=deps,
        grid=(1,),
        in_specs=[whole(a.shape) for a in (*lefts, *rights)],
        out_specs=[whole(a.shape) for a in gshape] + [whole((8, 128))],
        scratch=[pltpu.VMEM((d, rows), BF16), pltpu.VMEM((d, rows), BF16)],
        out_shape=gshape + [sds((8, 128), F32)],
        cost_estimate=cost(2 * rows * d * n, 2 * (rows * d + rows * n + d * n)),
        name="grad_tn",
    )


def in_grad_kernel(n, has_base, *refs):
    if has_base:
        base_ref, refs = refs[0], refs[1:]
    grads, weights, out_ref = refs[:n], refs[n:2 * n], refs[2 * n]
    acc = base_ref[...].astype(F32) if has_base else jnp.zeros(out_ref.shape, F32)
    for g, w in zip(grads, weights):
        acc = acc + nt(g[...], w[...])
    out_ref[...] = acc.astype(out_ref.dtype)


def in_grad(base, grads, weights, start, rows, deps=()):
    d = weights[0][0].shape[1]
    n = len(grads)
    first = start // RB
    row = lambda m: pl.BlockSpec((RB, m), lambda i, *_: (i + first, 0))
    wspec = lambda w, c: pl.BlockSpec((None, d, w.shape[2]), lambda i, *_: (c, 0, 0))
    own = pl.BlockSpec((RB, d), lambda i, *_: (i, 0))
    width = sum(g.shape[1] for g in grads)
    return call(
        partial(in_grad_kernel, n, base is not None),
        (*([base] if base is not None else []), *grads, *[w for w, _ in weights]),
        deps=deps,
        grid=(rows // RB,),
        in_specs=([own] if base is not None else []) + [row(g.shape[1]) for g in grads] + [wspec(w, c) for w, c in weights],
        out_specs=own,
        out_shape=sds((rows, d), BF16),
        cost_estimate=cost(2 * rows * d * width, 6 * rows * d + 2 * rows * width + 2 * d * width),
        name="in_grad",
    )


class Grid:
    axes = ("dp", "mp")

    def __init__(self):
        i = lax.axis_index("dp")
        self.y = lax.axis_index("mp")
        self.z, self.x, self.c = i // 4, (i // 2) % 2, i % 2
        self.all = [(z, x, c, y) for z in range(4) for x in range(2) for c in range(2) for y in range(2)]

    def permute(self, a, move):
        num = lambda z, x, c, y: ((z * 2 + x) * 2 + c) * 2 + y
        return lax.ppermute(a, self.axes, [(num(*p), num(*move(*p))) for p in self.all])

    def over_y(self, a):
        return self.permute(a, lambda z, x, c, y: (z, x, c, 1 - y))

    def over_x(self, a):
        return self.permute(a, lambda z, x, c, y: (z, 1 - x, c, y))

    def over_c(self, a):
        return self.permute(a, lambda z, x, c, y: (z, x, 1 - c, y))

    def over_zpair(self, a):
        return self.permute(a, lambda z, x, c, y: (z ^ 1, x, c, y))

    def shift_z(self, a, k):
        return self.permute(a, lambda z, x, c, y: ((z + k) % 4, x, c, y))


def place_kernel(moves, bits_ref, *refs):
    for src, dst in moves(bits_ref, refs):
        dst[...] = src[...]


def place(moves, bits, args, out_shape):
    return call(
        partial(place_kernel, moves),
        args,
        prefetch=(jnp.stack(bits).astype(jnp.int32),),
        grid=(1,),
        in_specs=[whole(a.shape) for a in args],
        out_specs=[whole(o.shape) for o in out_shape],
        out_shape=out_shape,
        cost_estimate=cost(0, 4 * sum(math.prod(o.shape) for o in out_shape)),
        name="place",
    )


def join(pairs, bits):
    n = len(pairs)

    def moves(bits_ref, refs):
        for i in range(n):
            rows = refs[2 * i].shape[0]
            for k in range(2):
                bit = bits_ref[i] if k == 0 else 1 - bits_ref[i]
                yield refs[2 * i + k], refs[2 * n + i].at[pl.ds(pl.multiple_of(bit * rows, rows), rows), :]

    outs = [sds((2 * a.shape[0], a.shape[1]), a.dtype) for a, _ in pairs]
    return place(moves, bits, [a for p in pairs for a in p], outs)


class Fetch:
    def __init__(self, grid, w, x_first, cut):
        self.grid, self.x_first = grid, x_first
        self.zbit = grid.z % 2
        pair = (self.zbit * 2 + grid.x) if x_first else (grid.x * 2 + self.zbit)
        self.cut = lambda *deps: cut(after(w, *deps), grid.c, pair)

    def prepare(self, *deps):
        self.op = self.cut(*deps)
        return self.op

    def send_y(self, *deps):
        self.op = after(self.op, *deps)
        self.got = self.grid.over_y(self.op)
        return self.op

    def send(self, by_x):
        self.bit = self.grid.x if by_x else self.zbit
        self.got = self.grid.over_x(self.op) if by_x else self.grid.over_zpair(self.op)
        return self.op

    def first(self, token):
        self.op = after(self.got, token)
        return self.send(self.x_first)

    @staticmethod
    def joined(fetches, token):
        parts = join([(f.op, after(f.got, token)) for f in fetches], [f.bit for f in fetches])
        for f, part in zip(fetches, parts):
            f.op = part

    @staticmethod
    def second(fetches, token):
        Fetch.joined(fetches, token)
        return [f.send(not f.x_first) for f in fetches]

    @staticmethod
    def third(fetches, token):
        Fetch.joined(fetches, token)
        for f in fetches:
            f.got = f.grid.over_c(f.op)
        return [f.op for f in fetches]

    def last(self, token):
        return after(self.got, token)


def at(a, axis, i):
    return lax.dynamic_index_in_dim(a, i, axis, keepdims=False)


class Reduce:
    def __init__(self, grid, own_a=None, oth_a=None, own_b=None, oth_b=None):
        self.grid, self.waiting = grid, {}
        self.own_a, self.oth_a, self.own_b, self.oth_b = own_a, oth_a, own_b, oth_b

    def view(self, a):
        return a.reshape(4, 2, a.shape[0] // 8, a.shape[1])

    def half(self, a, mine):
        g = self.grid
        return at(self.view(a), 1, g.x if mine else 1 - g.x).astype(F32)

    def cores(self, name, keep, send):
        self.waiting[name] = self.grid.over_c(send)
        setattr(self, "keep_" + "_".join(name), keep)
        return send

    def take(self, token):
        for name, got in self.waiting.items():
            got = [after(a, token) for a in got] if isinstance(got, list) else after(got, token)
            if isinstance(name, tuple):
                if not name[0].startswith("x_"):
                    got = (getattr(self, "keep_" + "_".join(name)).astype(F32) + got.astype(F32)).astype(BF16)
                width = got.shape[-1] // len(name)
                for i, n in enumerate(name):
                    setattr(self, n, got[..., i * width:(i + 1) * width])
            else:
                setattr(self, name, got)
        taken, self.waiting = [getattr(self, n) for name in self.waiting for n in ((name,) if isinstance(name, str) else name)], {}
        return [a for t in taken for a in (t if isinstance(t, list) else [t])]

    def a_over_y(self):
        self.waiting["back_a"] = self.grid.over_y(self.oth_a)
        return self.oth_a

    def a_over_x(self):
        op = (self.half(self.own_a, False) + self.half(self.back_a, False)).astype(BF16)
        self.waiting["x_a"] = self.grid.over_x(op)
        return op

    def b_over_x(self, which):
        op = jnp.concatenate([self.half(getattr(self, n), False).astype(BF16) for n in which], axis=-1)
        self.waiting[tuple("x_" + n for n in which)] = self.grid.over_x(op)
        return op

    def b_over_y(self):
        op = (self.half(self.oth_b, True) + self.x_oth_b.astype(F32)).astype(BF16)
        self.waiting["back_b"] = self.grid.over_y(op)
        return op

    def half_a(self):
        return (self.half(self.own_a, True) + self.half(self.back_a, True) + self.x_a.astype(F32)).astype(BF16)

    def over_z(self, *more):
        g = self.grid
        b = self.half(self.own_b, True) + self.x_own_b.astype(F32) + self.back_b.astype(F32)
        self.kept = jnp.concatenate([self.half_a(), b.astype(BF16), *[m.half_a() for m in more]], axis=2)
        self.kept = lax.optimization_barrier(self.kept)
        ops = [at(self.kept, 0, (g.z + k) % 4) for k in (1, 2, 3)]
        self.waiting["z_got"] = [g.shift_z(op, k) for k, op in zip((1, 2, 3), ops)]
        return ops

    def total(self):
        a, b, c = [p.astype(F32) for p in self.z_got]
        return (at(self.kept, 0, self.grid.z).astype(F32) + a) + (b + c)

    def ends(self):
        self.all = self.total().reshape(2, 64, -1)
        op = at(self.all, 0, 1 - self.grid.c).astype(BF16)
        self.waiting["end"] = self.grid.over_c(op)
        return op

    def result(self):
        mine, got = at(self.all, 0, self.grid.c), self.end.astype(F32)
        c = self.grid.c
        return jnp.concatenate([jnp.where(c == 0, mine, got), jnp.where(c == 0, got, mine)], axis=1)


class Small:
    def __init__(self, grid):
        self.grid = grid

    def send_y(self, oth):
        self.got = self.grid.over_y(oth)
        return oth

    def send_c(self, own, token):
        self.value = own + after(self.got, token)
        self.got = self.grid.over_c(self.value)
        return self.value

    def send_x(self, token):
        self.value = self.value + after(self.got, token)
        self.got = self.grid.over_x(self.value)
        return self.value

    def send_z(self, token):
        self.value = self.value + after(self.got, token)
        self.got = [self.grid.shift_z(self.value, k) for k in (1, 2, 3)]
        return self.value

    def total(self, token):
        z = self.grid.z
        ring = jnp.stack([self.value, *[after(g, token) for g in self.got]])
        terms = [at(ring, 0, (z - s) % 4) for s in range(4)]
        return (terms[0] + terms[1]) + (terms[2] + terms[3])


def time_embed(step, d):
    half = d // 2
    frequency = jnp.exp(-math.log(10000.0) * jnp.arange(half, dtype=F32) / half)
    angles = step.astype(F32) * frequency[None, :]
    return jnp.concatenate([jnp.sin(angles), jnp.cos(angles)], axis=-1)


def block_lists(seg_own, seg_halo, rows):
    q = seg_own.reshape(-1, BQ)
    keys = jnp.concatenate([seg_own, seg_halo]).reshape(-1, BK)
    need = (keys[None, :, 0] <= q[:, None, -1]) & (keys[None, :, -1] >= q[:, None, 0])
    need = need.astype(jnp.int32)
    nkb = keys.shape[0]
    before = jnp.sum(need[:, None, :] * (jnp.arange(nkb)[None, None, :] < jnp.arange(nkb)[None, :, None]), axis=2)
    slot = jnp.arange(nkb)[None, :, None]
    pick = need[:, None, :] * (before[:, None, :] == slot)
    lst = jnp.sum(pick * jnp.arange(nkb)[None, None, :], axis=2)
    return jnp.sum(need, axis=1).astype(jnp.int32), lst.astype(jnp.int32).reshape(-1)


def finish(output, grad_input, grad_qkv, head_bias_sum, grad_out, grad_up, up_bias_sum, grad_down, grad_vectors):
    grad_qkv = grad_qkv.reshape(grad_qkv.shape[0], 3, -1).transpose(1, 0, 2)
    return (
        output,
        grad_input,
        grad_qkv,
        head_bias_sum,
        grad_out.T,
        grad_up,
        up_bias_sum,
        grad_down.T,
        grad_vectors,
    )


def per_device_fast(
    tokens_in,
    timesteps,
    segment_ids,
    padding,
    qkv_weight,
    head_bias,
    out_weight,
    up_weight,
    up_bias,
    down_weight,
    vectors,
    cotangent,
):
    rows, d = tokens_in.shape
    assert timesteps.shape[0] == 1
    LIMITED[0] = True
    grid = Grid()
    me, halo = grid.y, MAXDOC
    core = grid.c.reshape(1).astype(jnp.int32)
    own_start = me * rows
    sub = up_weight.shape[1] // 2
    width = qkv_weight.shape[2]
    by_rows = lambda a, c, q: lax.dynamic_slice_in_dim(a, (c * 4 + q) * (a.shape[0] // 8), a.shape[0] // 8, 0)
    by_cols = lambda a, c, q: lax.dynamic_slice(a, (q * (a.shape[0] // 4), c * sub), (a.shape[0] // 4, sub))
    flat_qkv = qkv_weight.reshape(3 * d, width)

    def outer(a, c, q):
        o = by_rows(out_weight, c, q)
        return jnp.concatenate([by_rows(a, c, q), o[:, :width], o[:, width:]], axis=0)

    def split_outer(mine, theirs):
        n, m = 3 * d // 8, out_weight.shape[0] // 8
        rows = n + 2 * m

        def moves(bits_ref, refs):
            for k in range(2):
                c = bits_ref[0] if k == 0 else 1 - bits_ref[0]
                for i in range(4):
                    at_row = lambda r: pl.ds(pl.multiple_of((c * 4 + i) * r, r), r)
                    yield refs[k].at[i * rows:i * rows + n, :], refs[2].at[at_row(n), :]
                    for j in range(2):
                        o = i * rows + n + j * m
                        yield refs[k].at[o:o + m, :], refs[3].at[at_row(m), j * width:(j + 1) * width]

        qkv, out = place(moves, [grid.c], [mine, theirs], [sds((3 * d, width), BF16), sds(out_weight.shape, BF16)])
        return qkv.reshape(qkv_weight.shape), out

    fq = Fetch(grid, flat_qkv, False, outer)
    fu = Fetch(grid, up_weight, False, by_cols)
    fd = Fetch(grid, down_weight, True, by_rows)
    small_w = jnp.concatenate([head_bias.reshape(-1), up_bias])
    small_o = grid.over_y(small_w)
    fq.prepare()
    begin = [fq.send_y(), small_w]

    emb = time_embed(timesteps[:, None], d)
    seg, pad = segment_ids[0], padding[0]
    seg_own = lax.dynamic_slice_in_dim(seg, own_start, rows)
    pad_own = lax.dynamic_slice_in_dim(pad, own_start, rows)
    halo_start = jnp.where(me == 0, rows, own_start - halo)
    seg_halo = lax.dynamic_slice_in_dim(seg, halo_start, halo)
    pad_halo = lax.dynamic_slice_in_dim(pad, halo_start, halo)
    code = jnp.concatenate([jnp.where(pad_own == 0, seg_own, -1), jnp.where(pad_halo == 0, seg_halo, -1)])
    cnt, lst = block_lists(seg_own, seg_halo, rows)
    nkb = (rows + halo) // BK
    segq_row, code_col = seg_own[None, :], code[:, None]
    nb = head_bias.size

    far_blocks = (rows - halo) // BQ
    far = jnp.where(me == 0, 0, rows // BQ - far_blocks).reshape(1).astype(jnp.int32)
    near = jnp.where(me == 0, far_blocks, 0).reshape(1).astype(jnp.int32)
    zero = jnp.zeros((1,), jnp.int32)
    x_own, q0, k0, v0 = qkv_own(tokens_in, emb, qkv_weight, head_bias, deps=begin)
    small_o = after(small_o, k0)
    ops = [fq.first(k0), small_o]
    edge = jnp.where(me == 0, rows - halo, 0)
    halo_op = lax.dynamic_slice_in_dim(after(tokens_in, ops[0]), edge, halo, 0)
    halo_tok = grid.over_y(halo_op)
    part = attn_fwd(far, far_blocks, cnt, lst, nkb, q0, [k0], [v0], segq_row, code_col, deps=[*ops, halo_op])
    ops = [*Fetch.second([fq], part[1]), fu.prepare(part[1]), fd.prepare(part[1])]
    x_halo, kh0, vh0 = kv_halo(after(halo_tok, part[1]), emb, qkv_weight, head_bias, deps=ops)
    ops = [fu.send_y(kh0), fd.send_y(kh0)]
    kv0 = ([k0, kh0], [v0, vh0], segq_row, code_col)
    part = attn_fwd(near, 1, cnt, lst, nkb, q0, *kv0, into=part, deps=ops)
    ops = Fetch.third([fq], part[1])
    o0, lse0 = attn_fwd(near + 1, rows // BQ - far_blocks - 1, cnt, lst, nkb, q0, *kv0, into=part, deps=ops)
    hb_o, up_b_o = small_o[:nb].reshape(head_bias.shape), small_o[nb:].reshape(1, -1)
    qkv_o, out_o = split_outer(fq.op, fq.last(lse0))
    out_ws = [out_weight, out_o]
    _, q1, k1, v1 = qkv_own(tokens_in, emb, qkv_o, hb_o)
    _, kh1, vh1 = kv_halo(halo_tok, emb, qkv_o, hb_o, deps=[q1])
    ops = [fu.first(kh1), fd.first(kh1)]
    o1, lse1 = attn_fwd(zero, rows // BQ, cnt, lst, nkb, q1, [k1, kh1], [v1, vh1], segq_row, code_col, deps=ops)
    ops = Fetch.second([fu, fd], lse1)
    xhat1, normed, rstd1 = out_norm(tokens_in, emb, vectors, [o0, o1], out_ws, deps=ops)
    up_b = up_bias.reshape(1, -1)
    (a0, b0), (ga0, gb0) = ffn_up(core, normed, [(up_weight, 0, up_b, 0), (up_weight, 1, up_b, 1)], sub)
    ops = Fetch.third([fu, fd], ga0)
    b0_got, normed_got = grid.over_c(b0), grid.over_c(normed)
    (a1,), (ga1,) = ffn_up(core, normed, [(fu.op, None, up_b_o, 0)], sub, deps=ops)
    up_b1, down_b1 = fu.last(ga1), fd.last(ga1)
    (b1,), (gb1,) = ffn_up(core, normed, [(up_b1, None, up_b_o, 1)], sub, deps=[ga1])
    b1_got = grid.over_c(b1)
    output, d_down, sums2 = ffn_down(
        core, normed, cotangent, vectors, [a0, b0, a1, b1], [(down_weight, 0), (down_weight, 1), (fd.op, None), (down_b1, None)]
    )

    d_got = grid.over_c(d_down)
    dn1, (ua1, ub1), us1 = ffn_dup(core, d_down, [(fu.op, None, fd.op, None, ga1), (up_b1, None, down_b1, None, gb1)], sub)
    ub1_got = grid.over_c(ub1)
    gd1, gd0 = wide_grad([d_down, after(d_got, ua1)], [(a1, after(b1_got, d_down)), (a0, after(b0_got, d_down))], deps=[ua1])
    rd = Reduce(grid, gd0[0], gd1[0], gd0[1], gd1[1])
    both = ("own_b", "oth_b")
    ops = [rd.a_over_y(), rd.b_over_x(both)]
    dn0, (ua0, ub0), us0 = ffn_dup(core, d_down, [(up_weight, 0, down_weight, 0, ga0), (up_weight, 1, down_weight, 1, gb0)], sub, deps=ops)
    ub0_got = grid.over_c(ub0)
    got = rd.take(dn0)
    d_attn, sums1, dm0, dm1 = norm_bwd([d_down, dn1, dn0], xhat1, rstd1, vectors, out_ws)
    ops = [rd.a_over_x(), rd.b_over_y(), *got]
    *og, os = grad_tn(core, [d_attn], [o0, o1], deps=[sums1, *ops])
    ro = Reduce(grid)
    ops = [ro.cores(("own_a", "oth_a"), *og)]
    gu1, gu0 = wide_grad([normed, after(normed_got, sums1)], [(ua1, after(ub1_got, sums1)), (ua0, after(ub0_got, sums1))], deps=ops)
    ru = Reduce(grid, gu0[0], gu1[0], gu0[1], gu1[1])
    got = rd.take(gu0[1]) + ro.take(gu0[1])
    ops = [*rd.over_z(), ru.a_over_y(), ru.b_over_x(both), *got]
    *dqkv1, hs1 = attn_bwd(cnt, lst, nkb, q1, [k1, kh1], [v1, vh1], dm1, o1, lse1, segq_row, code_col, deps=ops)
    got = ru.take(dqkv1[0]) + rd.take(dqkv1[0])
    ops = [ru.a_over_x(), ru.b_over_y(), *got]
    rq = Reduce(grid)
    *qg1, gt1 = grad_tn(core, [x_own, x_halo], dqkv1, deps=ops)
    got = []
    rq.cores(("oth_a", "oth_b"), *qg1)
    got += rq.take(gt1)
    vec6 = jnp.concatenate([sums1[:2], sums2[:2], sums1[2:3], sums2[2:3]], axis=0)
    up_sum = lambda us: jnp.where(grid.c == 0, jnp.concatenate(us, axis=0), jnp.concatenate(us[::-1], axis=0))
    head_sum = lambda hs: hs.reshape(1, -1)
    small_sums = lambda us, hs: jnp.concatenate([vec6, up_sum(us), head_sum(hs)], axis=0)
    small = Small(grid)
    ops = [rq.a_over_y(), rq.b_over_x(("oth_b",)), ro.a_over_y(), small.send_y(small_sums(us1, hs1)), *got]
    *dqkv0, hs0 = attn_bwd(cnt, lst, nkb, q0, [k0, kh0], [v0, vh0], dm0, o0, lse0, segq_row, code_col, deps=ops)
    got = rq.take(dqkv0[0]) + ro.take(dqkv0[0]) + ru.take(dqkv0[0])
    ops = [rq.b_over_y(), ro.a_over_x(), *ru.over_z(), small.send_c(small_sums(us0, hs0), hs0), *got]
    *qg0, gt0 = grad_tn(core, [x_own, x_halo], dqkv0, deps=ops)
    got = rq.take(gt0) + ro.take(gt0)
    ops = [rq.cores(("own_a", "own_b"), *qg0), small.send_x(gt0), *got]
    pairs = [(g[c], w, c) for g, w in ((dqkv0, qkv_weight), (dqkv1, qkv_o)) for c in range(3)]
    kv_pairs = [(g, (w, c)) for g, w, c in pairs if c]
    halo_grad = in_grad(None, [g for g, _ in kv_pairs], [w for _, w in kv_pairs], rows, halo, deps=ops)
    got = rq.take(halo_grad) + ru.take(gt0)
    back = grid.over_y(halo_grad)
    ops = [rq.a_over_x(), rq.b_over_x(("own_b",)), small.send_z(halo_grad), halo_grad, *got]
    own_grad = in_grad(d_attn, [g for g, _, _ in pairs], [(w, c) for _, w, c in pairs], 0, rows, deps=ops)
    rq.take(own_grad)
    token = rq.over_z(ro)[0]
    for r in (rd, ru):
        r.z_got = [after(a, token) for a in r.z_got]
        r.ends()
        r.take(token)
    near_rows = (jnp.arange(rows // halo) == 1 - me)[:, None, None]
    own_grad, back = after(own_grad, token), after(back, token).astype(F32)
    grad_input = (own_grad.reshape(rows // halo, halo, d).astype(F32) + jnp.where(near_rows, back[None], 0.0)).astype(BF16).reshape(rows, d)
    small = small.total(token)
    rq.take(token)
    total = rq.total()
    qkv_cols = 3 * width
    return finish(
        output, grad_input, total[:, :qkv_cols], small[8:].reshape(2, -1), total[:, qkv_cols:], ru.result(),
        small[6:8].reshape(-1), rd.result(), small[:6],
    )


def per_device(
    mp_size,
    tokens_in,
    timesteps,
    segment_ids,
    padding,
    qkv_weight,
    head_bias,
    out_weight,
    up_weight,
    up_bias,
    down_weight,
    vectors,
    cotangent,
):
    rows, d = tokens_in.shape
    assert timesteps.shape[0] == 1
    LIMITED[0] = False
    me = lax.axis_index("mp")
    own_start = me * rows
    emb = time_embed(timesteps[:, None], d)
    seg, pad = segment_ids[0], padding[0]
    seg_own = lax.dynamic_slice_in_dim(seg, own_start, rows)
    pad_own = lax.dynamic_slice_in_dim(pad, own_start, rows)
    halo_tok = lax.all_gather(tokens_in, "mp", axis=0, tiled=True)
    place = jnp.arange(SEQ, dtype=jnp.int32)
    pad_halo = jnp.where((place >= own_start) & (place < own_start + rows), 1, pad)
    code = jnp.concatenate([jnp.where(pad_own == 0, seg_own, -1), jnp.where(pad_halo == 0, seg, -1)])
    cnt, lst = block_lists(seg_own, seg, rows)
    nkb = (rows + SEQ) // BK
    segq_row, code_col = seg_own[None, :], code[:, None]
    gather = lambda a, axis: lax.all_gather(a, "mp", axis=axis, tiled=True)
    qkv_w, out_w, up_w, down_w = gather(qkv_weight, 2), gather(out_weight, 0), gather(up_weight, 1), gather(down_weight, 0)
    hb, up_b = gather(head_bias, 1), gather(up_bias, 0).reshape(1, -1)

    x_own, q, k, v = qkv_own(tokens_in, emb, qkv_w, hb)
    x_halo, kh, vh = kv_halo(halo_tok, emb, qkv_w, hb)
    k, v = [k, kh], [v, vh]
    o, lse = attn_fwd(jnp.zeros((1,), jnp.int32), rows // BQ, cnt, lst, nkb, q, k, v, segq_row, code_col)
    xhat1, normed, rstd1 = out_norm(tokens_in, emb, vectors, [o], [out_w])
    core, hidden = jnp.zeros((1,), jnp.int32), up_w.shape[1]
    acts, gps = ffn_up(core, normed, [(up_w, None, up_b, None)], hidden)
    output, d_down, sums2 = ffn_down(core, normed, cotangent, vectors, acts, [(down_w, None)])

    dn, dups, (up_sum,) = ffn_dup(core, d_down, [(up_w, None, down_w, None, gps[0])], hidden)
    grad_up = jnp.concatenate(wide_grad([normed], [dups])[0], axis=1)
    grad_down = jnp.concatenate(wide_grad([d_down], [acts])[0], axis=1)
    d_attn, sums1, d_mixed = norm_bwd([d_down, dn], xhat1, rstd1, vectors, [out_w])
    grad_out, _ = grad_tn(None, [d_attn], [o])
    *d_qkv, head_sum = attn_bwd(cnt, lst, nkb, q, k, v, d_mixed, o, lse, segq_row, code_col)
    grad_qkv, _ = grad_tn(None, [x_own, x_halo], d_qkv)
    halo_grad = in_grad(None, d_qkv[1:], [(qkv_w, 1), (qkv_w, 2)], rows, SEQ)
    own_grad = in_grad(d_attn, d_qkv, [(qkv_w, c) for c in range(3)], 0, rows)
    back = lax.psum_scatter(halo_grad, "mp", scatter_dimension=0, tiled=True)
    grad_input = (own_grad.astype(F32) + back.astype(F32)).astype(BF16)

    packed = [sums1[:2], sums2[:2], sums1[2:3], sums2[2:3], head_sum, up_sum.reshape(-1, d)]
    packed = lax.psum(jnp.concatenate(packed, axis=0), ("dp", "mp"))
    local = head_bias.shape[1]
    head_bias_sum = lax.dynamic_slice_in_dim(packed[6:8], me * local, local, 1)
    local = up_bias.shape[0]
    up_bias_sum = lax.dynamic_slice_in_dim(packed[8:].reshape(-1), me * local, local, 0)

    def scatter(g, groups):
        n = g.shape[1] // groups // mp_size
        g = lax.psum_scatter(g, "dp", scatter_dimension=0, tiled=True)
        g = g.reshape(-1, groups, mp_size, n).transpose(2, 0, 1, 3)
        return lax.psum_scatter(g, "mp", scatter_dimension=0, tiled=False).astype(F32).reshape(-1, groups * n)

    return finish(
        output,
        grad_input,
        scatter(grad_qkv, 3),
        head_bias_sum,
        scatter(grad_out, 1),
        scatter(grad_up, 1),
        up_bias_sum,
        scatter(grad_down, 1),
        packed[:6],
    )


def solution(mesh):
    fast = dict(mesh.shape) == {"dp": 16, "mp": 2}
    return jax.shard_map(
        per_device_fast if fast else partial(per_device, mesh.shape["mp"]),
        mesh=mesh,
        in_specs=(
            P(("dp", "mp"), None),
            P("dp"),
            P("dp", None),
            P("dp", None),
            P(None, None, "mp"),
            P(None, "mp"),
            P("mp", None),
            P(None, "mp"),
            P("mp"),
            P("mp", None),
            P(),
            P(("dp", "mp"), None),
        ),
        out_specs=(
            P(("dp", "mp"), None),
            P(("dp", "mp"), None),
            P(None, "dp", "mp"),
            P(None, "mp"),
            P("mp", "dp"),
            P("dp", "mp"),
            P("mp"),
            P("mp", "dp"),
            P(),
        ),
        check_vma=False,
    )
```

```python
from functools import partial
import math

import jax
import jax.numpy as jnp
from jax import lax
from jax.experimental import pallas as pl
from jax.experimental.pallas import tpu as pltpu
from jax.sharding import PartitionSpec as P

HEAD_DIM = 64
SEQ = 2048
MAXDOC = 512
BQ = 256
BK = 256
RB = 256
HB = 512
SCALE = 300.0
VMEM_MIB = {
    "qkv_own": 12, "kv_halo": 12, "attn_fwd": 12, "out_norm": 14, "ffn_up": 22, "ffn_down": 24,
    "ffn_dup": 25, "wide_grad": 24, "norm_bwd": 14, "grad_tn": 16, "attn_bwd": 18, "in_grad": 14, "place": 18,
}
LIMITED = [True]
GROUP = 512
NEG_FILL = -1e30
F32 = jnp.float32
BF16 = jnp.bfloat16


def nt(a, b):
    return lax.dot_general(a, b, (((1,), (1,)), ((), ())), preferred_element_type=F32)


def nn(a, b):
    return lax.dot_general(a, b, (((1,), (0,)), ((), ())), preferred_element_type=F32)


def tn(a, b):
    return lax.dot_general(a, b, (((0,), (0,)), ((), ())), preferred_element_type=F32)


def cost(flops, nbytes, trans=0):
    return pl.CostEstimate(flops=int(flops * SCALE), bytes_accessed=int(nbytes * SCALE), transcendentals=int(trans * SCALE))


def whole(shape):
    return pl.BlockSpec(shape, lambda *_: (0,) * len(shape))


def sds(shape, dtype):
    return jax.ShapeDtypeStruct(shape, dtype)


def call(kernel, args, *, grid, in_specs, out_specs, out_shape, cost_estimate, name, prefetch=(), deps=(), scratch=(), aliases=None):
    first, skip, offset = len(prefetch) + len(args), len(deps), len(prefetch)

    def body(*refs):
        kernel(*refs[:first], *refs[first + skip:])

    return pl.pallas_call(
        body,
        grid_spec=pltpu.PrefetchScalarGridSpec(
            num_scalar_prefetch=offset,
            grid=grid,
            in_specs=list(in_specs) + [pl.BlockSpec(memory_space=pl.ANY)] * skip,
            out_specs=out_specs,
            scratch_shapes=list(scratch),
        ),
        out_shape=out_shape,
        input_output_aliases={k + offset: v for k, v in (aliases or {}).items()},
        cost_estimate=cost_estimate,
        compiler_params=pltpu.CompilerParams(vmem_limit_bytes=VMEM_MIB[name] << 20) if LIMITED[0] else None,
        name=name,
    )(*prefetch, *args, *deps)


def after(x, *deps):
    return lax.optimization_barrier((x, *deps))[0] if deps else x


def qkv_own_kernel(tok_ref, emb_ref, w_ref, hb_ref, x_ref, q_ref, k_ref, v_ref):
    x = (tok_ref[...].astype(F32) + emb_ref[...]).astype(BF16)
    x_ref[...] = x
    q_ref[...] = (nn(x, w_ref[0]) + hb_ref[0:1]).astype(BF16)
    k_ref[...] = nn(x, w_ref[1]).astype(BF16)
    v_ref[...] = (nn(x, w_ref[2]) + hb_ref[1:2]).astype(BF16)


def qkv_own(tok, emb, w, hb, deps=()):
    rows, d = tok.shape
    width = w.shape[2]
    row = lambda n: pl.BlockSpec((RB, n), lambda i, *_: (i, 0))
    return call(
        qkv_own_kernel,
        (tok, emb, w, hb),
        deps=deps,
        grid=(rows // RB,),
        in_specs=[row(d), whole((1, d)), whole(w.shape), whole(hb.shape)],
        out_specs=[row(d), row(width), row(width), row(width)],
        out_shape=[sds((rows, d), BF16)] + [sds((rows, width), BF16)] * 3,
        cost_estimate=cost(6 * rows * d * width, 2 * (2 * rows * d + 3 * rows * width + 3 * d * width)),
        name="qkv_own",
    )


def kv_halo_kernel(tok_ref, emb_ref, w_ref, hb_ref, x_ref, k_ref, v_ref):
    x = (tok_ref[...].astype(F32) + emb_ref[...]).astype(BF16)
    x_ref[...] = x
    k_ref[...] = nn(x, w_ref[1]).astype(BF16)
    v_ref[...] = (nn(x, w_ref[2]) + hb_ref[1:2]).astype(BF16)


def kv_halo(tok, emb, w, hb, deps=()):
    rows, d = tok.shape
    width = w.shape[2]
    row = lambda n: pl.BlockSpec((RB, n), lambda i, *_: (i, 0))
    return call(
        kv_halo_kernel,
        (tok, emb, w, hb),
        deps=deps,
        grid=(rows // RB,),
        in_specs=[row(d), whole((1, d)), whole(w.shape), whole(hb.shape)],
        out_specs=[row(d), row(width), row(width)],
        out_shape=[sds((rows, d), BF16)] + [sds((rows, width), BF16)] * 2,
        cost_estimate=cost(4 * rows * d * width, 2 * (2 * rows * d + 2 * rows * width + 3 * d * width)),
        name="kv_halo",
    )


def pair_stack(x2):
    lane = lax.broadcasted_iota(jnp.int32, (1, 128), 1)
    first = (lane < HEAD_DIM).astype(F32).astype(BF16)
    second = (lane >= HEAD_DIM).astype(F32).astype(BF16)
    return jnp.concatenate([x2 * first, x2 * second], axis=0)


def pair_merge(x):
    half = x.shape[0] // 2
    lane = lax.broadcasted_iota(jnp.int32, (half, 128), 1)
    return jnp.where(lane < HEAD_DIM, x[:half], x[half:])


def load_keys(srcs, dsts, sem, group):
    copies = []
    for pieces, dst in zip(srcs, dsts):
        off = 0
        for src in pieces:
            cols = pl.ds(pl.multiple_of(group * GROUP, GROUP), GROUP)
            copies.append(pltpu.make_async_copy(src.at[:, cols], dst.at[off:off + src.shape[0], :], sem.at[len(copies)]))
            off += src.shape[0]
    for c in copies:
        c.start()
    for c in copies:
        c.wait()


def attn_fwd_kernel(pieces, nkb, pairs, filled, base_ref, cnt_ref, list_ref, q_ref, segq_ref, codek_ref, *refs):
    k_srcs, v_srcs, refs = refs[:pieces], refs[pieces:2 * pieces], refs[2 * pieces + 2 * filled:]
    o_ref, lse_ref, k_ref, v_ref, qs_scr, m_scr, l_scr, acc_scr, sem = refs

    @pl.when(pl.program_id(1) == 0)
    def _():
        load_keys((k_srcs, v_srcs), (k_ref, v_ref), sem, pl.program_id(0))

    qb = pl.program_id(1) + base_ref[0]
    count = cnt_ref[qb]
    for p in range(pairs):
        qs_scr[p] = pair_stack(q_ref[:, 128 * p:128 * (p + 1)] * jnp.asarray(0.125, BF16))
    m_scr[...] = jnp.full(m_scr.shape, -3e38, F32)
    l_scr[...] = jnp.zeros(l_scr.shape, F32)
    acc_scr[...] = jnp.zeros(acc_scr.shape, F32)

    def step(s, carry):
        kb = list_ref[qb * nkb + s]
        off = pl.multiple_of(kb * BK, BK)
        kpos = kb * BK + lax.broadcasted_iota(jnp.int32, (BK, BQ), 0)
        qpos = qb * BQ + lax.broadcasted_iota(jnp.int32, (BK, BQ), 1)
        live = (codek_ref[pl.ds(off, BK), :] == segq_ref[...]) | (qpos == kpos)
        bias = jnp.where(live, 0.0, NEG_FILL).astype(F32)
        bias = jnp.concatenate([bias, bias], axis=1)
        scs = [nt(k_ref[pl.ds(off, BK), 128 * p:128 * (p + 1)], qs_scr[p]) for p in range(pairs)]
        es = []
        for p in range(pairs):
            sc = scs[p] + bias
            old = m_scr[p:p + 1]
            new = jnp.maximum(old, jnp.max(sc, axis=0, keepdims=True))
            e = jnp.exp(sc - new)
            fade = jnp.exp(old - new)
            m_scr[p:p + 1] = new
            l_scr[p:p + 1] = l_scr[p:p + 1] * fade + jnp.sum(e, axis=0, keepdims=True)
            es.append((e.astype(BF16), fade))
        for p in range(pairs):
            acc_scr[p] = acc_scr[p] * es[p][1] + tn(v_ref[pl.ds(off, BK), 128 * p:128 * (p + 1)], es[p][0])
        return carry

    lax.fori_loop(0, count, step, 0)
    lse = m_scr[...] + jnp.log(l_scr[...])
    for p in range(pairs):
        o = acc_scr[p] / l_scr[p:p + 1]
        o = jnp.concatenate([o[:HEAD_DIM, :BQ], o[HEAD_DIM:, BQ:]], axis=0)
        o_ref[:, 128 * p:128 * (p + 1)] = jnp.transpose(o).astype(BF16)
        lse_ref[2 * p:2 * p + 1, :] = lse[p:p + 1, :BQ]
        lse_ref[2 * p + 1:2 * p + 2, :] = lse[p:p + 1, BQ:]


def attn_fwd(base, nqb, cnt, lst, nkb, q, k, v, segq, codek, into=(), deps=()):
    rows, width = q.shape
    pieces, keys = len(k), sum(a.shape[0] for a in k)
    groups, pairs = width // GROUP, GROUP // 128
    est = nqb * BQ * 2 * BK * width
    qspec = lambda n: pl.BlockSpec((BQ, n), lambda g, i, b, *_: (i + b[0], g))
    lspec = pl.BlockSpec((2 * pairs, BQ), lambda g, i, b, *_: (g, i + b[0]))
    anyspec = pl.BlockSpec(memory_space=pl.ANY)
    args = [q, segq, codek, *k, *v, *into]
    first = 3 + 2 * pieces
    return call(
        partial(attn_fwd_kernel, pieces, nkb, pairs, len(into) // 2),
        args,
        prefetch=(base, cnt, lst),
        deps=deps,
        grid=(groups, nqb),
        in_specs=[qspec(GROUP), pl.BlockSpec((1, BQ), lambda g, i, b, *_: (0, i + b[0])), pl.BlockSpec((codek.shape[0], 1), lambda *_: (0, 0))]
        + [anyspec] * (len(args) - 3),
        out_specs=[qspec(GROUP), lspec],
        out_shape=[sds((rows, width), BF16), sds((2 * pairs * groups, rows), F32)],
        aliases={first: 0, first + 1: 1} if into else None,
        scratch=[
            pltpu.VMEM((keys, GROUP), BF16),
            pltpu.VMEM((keys, GROUP), BF16),
            pltpu.VMEM((pairs, 2 * BQ, 128), BF16),
            pltpu.VMEM((pairs, 2 * BQ), F32),
            pltpu.VMEM((pairs, 2 * BQ), F32),
            pltpu.VMEM((pairs, 128, 2 * BQ), F32),
            pltpu.SemaphoreType.DMA((2 * pieces,)),
        ],
        cost_estimate=cost(4 * est, 8 * rows * width, est // 32),
        name="attn_fwd",
    )


def attn_bwd_kernel(pieces, nkb, pairs, cnt_ref, list_ref, q_ref, do_ref, o_ref, lse_ref, segq_ref, codek_ref, *refs):
    k_srcs, v_srcs, refs = refs[:pieces], refs[pieces:2 * pieces], refs[2 * pieces:]
    dq_ref, dk_ref, dv_ref, sum_ref, k_ref, v_ref, qs_scr, ds_scr, row_scr, dq_scr, dk_scr, dv_scr, sem = refs
    qb = pl.program_id(1)

    @pl.when(qb == 0)
    def _():
        load_keys((k_srcs, v_srcs), (k_ref, v_ref), sem, pl.program_id(0))

    @pl.when(qb == 0)
    def _():
        dk_scr[...] = jnp.zeros(dk_scr.shape, F32)
        dv_scr[...] = jnp.zeros(dv_scr.shape, F32)

    count = cnt_ref[qb]
    lse_t = lse_ref[...]
    for p in range(pairs):
        cols = slice(128 * p, 128 * (p + 1))
        qs_scr[p] = pair_stack(q_ref[:, cols] * jnp.asarray(0.125, BF16))
        ds_scr[p] = pair_stack(do_ref[:, cols])
        prod = jnp.transpose(do_ref[:, cols].astype(F32) * o_ref[:, cols].astype(F32))
        da = jnp.sum(prod[:HEAD_DIM], axis=0, keepdims=True)
        db = jnp.sum(prod[HEAD_DIM:], axis=0, keepdims=True)
        row_scr[p, 0:1] = jnp.concatenate([lse_t[2 * p:2 * p + 1], lse_t[2 * p + 1:2 * p + 2]], axis=1)
        row_scr[p, 1:2] = jnp.concatenate([da, db], axis=1)
    dq_scr[...] = jnp.zeros(dq_scr.shape, F32)

    def step(s, carry):
        kb = list_ref[qb * nkb + s]
        off = pl.multiple_of(kb * BK, BK)
        kpos = kb * BK + lax.broadcasted_iota(jnp.int32, (BK, BQ), 0)
        qpos = qb * BQ + lax.broadcasted_iota(jnp.int32, (BK, BQ), 1)
        live = (codek_ref[pl.ds(off, BK), :] == segq_ref[...]) | (qpos == kpos)
        bias = jnp.where(live, 0.0, NEG_FILL).astype(F32)
        bias = jnp.concatenate([bias, bias], axis=1)
        for p in range(pairs):
            cols = slice(128 * p, 128 * (p + 1))
            k2 = k_ref[pl.ds(off, BK), cols]
            v2 = v_ref[pl.ds(off, BK), cols]
            sc = nt(k2, qs_scr[p]) + bias
            probs = jnp.exp(sc - row_scr[p, 0:1])
            dprobs = nt(v2, ds_scr[p])
            dsc = (probs * (dprobs - row_scr[p, 1:2])).astype(BF16)
            dv_scr[pl.ds(off, BK), cols] += nn(probs.astype(BF16), ds_scr[p])
            dk_scr[pl.ds(off, BK), cols] += nn(dsc, qs_scr[p])
            dq_scr[p] += tn(k2, dsc)
        return carry

    lax.fori_loop(0, count, step, 0)
    for p in range(pairs):
        dq = dq_scr[p] * 0.125
        dq = jnp.concatenate([dq[:HEAD_DIM, :BQ], dq[HEAD_DIM:, BQ:]], axis=0)
        dq = jnp.transpose(dq).astype(BF16)
        cols = slice(128 * p, 128 * (p + 1))
        dq_ref[:, cols] = dq
        so_far = jnp.where(qb == 0, 0.0, sum_ref[0:1, cols])
        sum_ref[0:1, cols] = so_far + jnp.sum(dq.astype(F32), axis=0, keepdims=True)

    @pl.when(qb == pl.num_programs(1) - 1)
    def _():
        dk_ref[...] = dk_scr[...].astype(BF16)
        dv_ref[...] = dv_scr[...].astype(BF16)
        sum_ref[1:2, :] = jnp.sum(dv_scr[...], axis=0, keepdims=True)


def attn_bwd(cnt, lst, nkb, q, k, v, do, o, lse, segq, codek, deps=()):
    rows, width = q.shape
    pieces, keys = len(k), sum(a.shape[0] for a in k)
    groups, pairs = width // GROUP, GROUP // 128
    est = rows * 2 * BK * width
    qspec = pl.BlockSpec((BQ, GROUP), lambda g, i, *_: (i, g))
    kspec = pl.BlockSpec((keys, GROUP), lambda g, i, *_: (0, g))
    return call(
        partial(attn_bwd_kernel, pieces, nkb, pairs),
        (q, do, o, lse, segq, codek, *k, *v),
        prefetch=(cnt, lst),
        deps=deps,
        grid=(groups, rows // BQ),
        in_specs=[
            qspec, qspec, qspec,
            pl.BlockSpec((2 * pairs, BQ), lambda g, i, *_: (g, i)),
            pl.BlockSpec((1, BQ), lambda g, i, *_: (0, i)),
            pl.BlockSpec((keys, 1), lambda g, i, *_: (0, 0)),
        ] + [pl.BlockSpec(memory_space=pl.ANY)] * (2 * pieces),
        out_specs=[qspec, kspec, kspec, pl.BlockSpec((2, GROUP), lambda g, i, *_: (0, g))],
        scratch=[
            pltpu.VMEM((keys, GROUP), BF16),
            pltpu.VMEM((keys, GROUP), BF16),
            pltpu.VMEM((pairs, 2 * BQ, 128), BF16),
            pltpu.VMEM((pairs, 2 * BQ, 128), BF16),
            pltpu.VMEM((pairs, 8, 2 * BQ), F32),
            pltpu.VMEM((pairs, 128, 2 * BQ), F32),
            pltpu.VMEM((keys, GROUP), F32),
            pltpu.VMEM((keys, GROUP), F32),
            pltpu.SemaphoreType.DMA((2 * pieces,)),
        ],
        out_shape=[sds((rows, width), BF16), sds((keys, width), BF16), sds((keys, width), BF16), sds((2, width), F32)],
        cost_estimate=cost(10 * est, 16 * rows * width, est // 32),
        name="attn_bwd",
    )


def row_mean(x):
    return jnp.mean(x, axis=-1, keepdims=True)


def out_norm_kernel(parts, tok_ref, emb_ref, vec_ref, *refs):
    mixed, weights = refs[:parts], refs[parts:2 * parts]
    xhat_ref, low_ref, rstd_ref = refs[2 * parts:]
    acc = tok_ref[...].astype(F32) + emb_ref[...] + vec_ref[4:5]
    for m, w in zip(mixed, weights):
        acc = acc + nn(m[...], w[...])
    centered = acc - row_mean(acc)
    rstd = lax.rsqrt(row_mean(centered * centered) + 1e-05)
    xhat = centered * rstd
    xhat_ref[...] = xhat.astype(BF16)
    rstd_ref[...] = jnp.broadcast_to(rstd, rstd_ref.shape)
    low_ref[...] = (xhat * vec_ref[0:1] + vec_ref[1:2]).astype(BF16)


def out_norm(tok, emb, vec, mixed, weights, deps=()):
    rows, d = tok.shape
    parts = len(mixed)
    row = lambda n: pl.BlockSpec((RB, n), lambda i, *_: (i, 0))
    return call(
        partial(out_norm_kernel, parts),
        (tok, emb, vec, *mixed, *weights),
        deps=deps,
        grid=(rows // RB,),
        in_specs=[row(d), whole((1, d)), whole(vec.shape)]
        + [row(m.shape[1]) for m in mixed]
        + [whole(w.shape) for w in weights],
        out_specs=[row(d), row(d), row(128)],
        out_shape=[sds((rows, d), BF16), sds((rows, d), BF16), sds((rows, 128), F32)],
        cost_estimate=cost(2 * rows * d * d, 8 * rows * d + 2 * d * d),
        name="out_norm",
    )


def gelu_pair(h):
    mag = jnp.abs(h)
    t = 1.0 / (1.0 + (0.3275911 * 0.7071067811865476) * mag)
    e = jnp.exp2((-0.5 * 1.4426950408889634) * (h * h))
    poly = t * (0.127414796 + t * (-0.142248368 + t * (0.7107068705 + t * (-0.7265760135 + t * 0.5307027145))))
    tail = poly * e
    phi = jnp.where(h < 0.0, tail, 1.0 - tail)
    return h * phi, phi + h * (e * 0.3989422804014327)


def pick(sel, per):
    if sel is None:
        return lambda j, core: j
    return lambda j, core: j + per * (core[0] if sel == 0 else 1 - core[0])


def ffn_up_kernel(n, core_ref, x_ref, *refs):
    ws, bs, acts, gps = refs[:n], refs[n:2 * n], refs[2 * n:3 * n], refs[3 * n:]
    rows = min(x_ref.shape[0], 1024)

    def chunk(i, carry):
        at_rows = pl.ds(pl.multiple_of(i * rows, rows), rows)
        for w, b, a, g in zip(ws, bs, acts, gps):
            h = nn(x_ref[at_rows, :], w[...]) + b[...]
            act, gp = gelu_pair(h)
            a[at_rows, :] = act.astype(BF16)
            g[at_rows, :] = gp.astype(BF16)
        return carry

    lax.fori_loop(0, x_ref.shape[0] // rows, chunk, 0)


def ffn_up(core, x, items, hidden, deps=()):
    rows, d = x.shape
    n, per = len(items), hidden // HB
    col = lambda r, sel: pl.BlockSpec((r, HB), lambda j, c: (0, pick(sel, per)(j, c)))
    out = call(
        partial(ffn_up_kernel, n),
        (x, *[i[0] for i in items], *[i[2] for i in items]),
        prefetch=(core,),
        deps=deps,
        grid=(per,),
        in_specs=[whole((rows, d))] + [col(d, i[1]) for i in items] + [col(1, i[3]) for i in items],
        out_specs=[col(rows, None)] * (2 * n),
        out_shape=[sds((rows, hidden), BF16)] * (2 * n),
        cost_estimate=cost(2 * rows * d * hidden * n, 2 * (rows * d + n * (d + 2 * rows) * hidden), rows * hidden * n),
        name="ffn_up",
    )
    return out[:n], out[n:]


def ffn_down_kernel(parts, core_ref, norm_ref, cot_ref, vec_ref, *refs):
    acts, weights = refs[:parts], refs[parts:2 * parts]
    out_ref, dlow_ref, sums_ref = refs[2 * parts:]
    acc = norm_ref[...].astype(F32) + vec_ref[5:6]
    for a, w in zip(acts, weights):
        acc = acc + nn(a[...], w[...])
    centered = acc - row_mean(acc)
    rstd = lax.rsqrt(row_mean(centered * centered) + 1e-05)
    xhat = centered * rstd
    out_ref[...] = (xhat * vec_ref[2:3] + vec_ref[3:4]).astype(BF16)
    cot = cot_ref[...].astype(F32)
    gg = cot * vec_ref[2:3]
    dres = rstd * (gg - row_mean(gg) - xhat * row_mean(gg * xhat))
    low = dres.astype(BF16)
    dlow_ref[...] = low

    @pl.when(pl.program_id(0) == 0)
    def _():
        sums_ref[...] = jnp.zeros(sums_ref.shape, F32)

    sums_ref[0:1] += jnp.sum(cot * xhat, axis=0, keepdims=True)
    sums_ref[1:2] += jnp.sum(cot, axis=0, keepdims=True)
    sums_ref[2:3] += jnp.sum(low.astype(F32), axis=0, keepdims=True)


def ffn_down(core, normed, cot, vec, acts, weights, deps=()):
    rows, d = normed.shape
    parts = len(acts)
    hidden = sum(a.shape[1] for a in acts)
    row = lambda n: pl.BlockSpec((RB, n), lambda i, *_: (i, 0))
    wspec = lambda a, sel: pl.BlockSpec((a.shape[1], d), lambda i, c: (pick(sel, 1)(0, c), 0))
    return call(
        partial(ffn_down_kernel, parts),
        (normed, cot, vec, *acts, *[w for w, _ in weights]),
        prefetch=(core,),
        deps=deps,
        grid=(rows // RB,),
        in_specs=[row(d), row(d), whole(vec.shape)]
        + [row(a.shape[1]) for a in acts]
        + [wspec(a, sel) for a, (_, sel) in zip(acts, weights)],
        out_specs=[row(d), row(d), whole((8, d))],
        out_shape=[sds((rows, d), BF16), sds((rows, d), BF16), sds((8, d), F32)],
        cost_estimate=cost(2 * rows * d * hidden, 8 * rows * d + 2 * d * hidden + 2 * rows * hidden),
        name="ffn_down",
    )


def ffn_dup_kernel(n, core_ref, d_ref, *refs):
    ups, downs, gps, refs = refs[:n], refs[n:2 * n], refs[2 * n:3 * n], refs[3 * n:]
    dn_ref, dups, sums, acc_ref = refs[0], refs[1:n + 1], refs[n + 1:2 * n + 1], refs[2 * n + 1]
    rows = min(d_ref.shape[0], 512)
    first = pl.program_id(0) == 0
    last = pl.program_id(0) == pl.num_programs(0) - 1

    for s in sums:
        s[...] = jnp.zeros(s.shape, F32)

    def chunk(i, carry):
        at_rows = pl.ds(pl.multiple_of(i * rows, rows), rows)
        total = None
        for up, down, gp, dup_ref, s in zip(ups, downs, gps, dups, sums):
            dup = (nt(d_ref[at_rows, :], down[...]) * gp[at_rows, :].astype(F32)).astype(BF16)
            dup_ref[at_rows, :] = dup
            s[...] += jnp.sum(dup.astype(F32), axis=0, keepdims=True)
            term = nt(dup, up[...])
            total = term if total is None else total + term
        acc_ref[at_rows, :] = jnp.where(first, total, acc_ref[at_rows, :] + total)
        return carry

    lax.fori_loop(0, d_ref.shape[0] // rows, chunk, 0)

    @pl.when(last)
    def _():
        dn_ref[...] = acc_ref[...].astype(BF16)


def ffn_dup(core, dlow, items, hidden, deps=()):
    rows, d = dlow.shape
    n, per = len(items), hidden // HB
    col = lambda r, sel: pl.BlockSpec((r, HB), lambda j, c: (0, pick(sel, per)(j, c)))
    down = lambda sel: pl.BlockSpec((HB, d), lambda j, c: (pick(sel, per)(j, c), 0))
    out = call(
        partial(ffn_dup_kernel, n),
        (dlow, *[i[0] for i in items], *[i[2] for i in items], *[i[4] for i in items]),
        prefetch=(core,),
        deps=deps,
        grid=(per,),
        in_specs=[whole((rows, d))] + [col(d, i[1]) for i in items] + [down(i[3]) for i in items] + [col(rows, None)] * n,
        out_specs=[whole((rows, d))] + [col(rows, None)] * n + [col(1, None)] * n,
        scratch=[pltpu.VMEM((rows, d), F32)],
        out_shape=[sds((rows, d), BF16)] + [sds((rows, hidden), BF16)] * n + [sds((1, hidden), F32)] * n,
        cost_estimate=cost(4 * rows * d * hidden * n, 2 * n * (2 * d + 2 * rows) * hidden + 4 * rows * d),
        name="ffn_dup",
    )
    return out[0], out[1:n + 1], out[n + 1:]


def put_transposed(dst, tmp, src, core):
    if core is None:
        dst[...] = jnp.transpose(src)
        return
    tmp[...] = jnp.transpose(src)
    d = tmp.shape[0]
    for g in range(d // 128):
        mine = pl.multiple_of(g * 128 + core * 64, 64)
        other = pl.multiple_of(g * 128 + (1 - core) * 64, 64)
        dst[g * 64:(g + 1) * 64, :] = tmp[pl.ds(mine, 64), :]
        dst[d // 2 + g * 64:d // 2 + (g + 1) * 64, :] = tmp[pl.ds(other, 64), :]


def put_grad(keep_ref, send_ref, lt, right):
    d = lt.shape[0]
    if send_ref is None:
        for j in range(d // RB):
            keep_ref[j * RB:(j + 1) * RB, :] = nn(lt[j * RB:(j + 1) * RB, :], right).astype(BF16)
        return
    half = d // 2
    keep_ref[...] = nn(lt[:half, :], right).astype(BF16)
    send_ref[...] = nn(lt[half:, :], right).astype(BF16)


def wide_grad_kernel(n, count, steps, *refs):
    lefts, rights, refs = refs[:n], refs[n:n + n * count], refs[n + n * count:]
    outs, lt = refs[:count * steps], refs[count * steps]
    step = pl.program_id(0)
    cols, off = [], 0
    for left in lefts:
        cols.append(slice(off, off + left.shape[0]))
        off += left.shape[0]

    @pl.when(step == 0)
    def _():
        for c, left in zip(cols, lefts):
            lt[:, c] = jnp.transpose(left[...])

    d = lt.shape[0]
    for p in range(count):
        mine = rights[p * n:(p + 1) * n]
        for s in range(steps):
            @pl.when(step == s)
            def _(s=s, p=p, mine=mine):
                out = outs[p * steps + s]

                def chunk(i, carry):
                    r = pl.ds(pl.multiple_of(i * 1024, 1024), 1024)
                    acc = nn(lt[r, cols[0]], mine[0][...])
                    for c, right in zip(cols[1:], mine[1:]):
                        acc = acc + nn(lt[r, c], right[...])
                    out[r, :] = acc.astype(BF16)
                    return carry

                lax.fori_loop(0, d // 1024, chunk, 0)


def wide_grad(lefts, items, deps=()):
    d, hidden = lefts[0].shape[1], items[0][0].shape[1]
    n, count, steps = len(lefts), len(items), hidden // HB
    rows = sum(a.shape[0] for a in lefts)
    flat = [a for i in items for a in i]
    out = call(
        partial(wide_grad_kernel, n, count, steps),
        (*lefts, *flat),
        deps=deps,
        grid=(steps,),
        in_specs=[whole(a.shape) for a in lefts] + [pl.BlockSpec((a.shape[0], HB), lambda j: (0, j)) for a in flat],
        out_specs=[whole((d, HB))] * (count * steps),
        scratch=[pltpu.VMEM((d, rows), BF16)],
        out_shape=[sds((d, HB), BF16)] * (count * steps),
        cost_estimate=cost(2 * rows * d * hidden * count, 2 * (rows * d + count * (rows + d) * hidden)),
        name="wide_grad",
    )
    return [out[p * steps:(p + 1) * steps] for p in range(count)]


def norm_bwd_kernel(parts, terms, xhat_ref, rstd_ref, vec_ref, *refs):
    weights, dns, refs = refs[:parts], refs[parts:parts + terms], refs[parts + terms:]
    dlow_ref, sums_ref, mixes = refs[0], refs[1], refs[2:]
    dn = dns[0][...].astype(F32)
    for t in dns[1:]:
        dn = dn + t[...].astype(F32)
    xhat = xhat_ref[...].astype(F32)
    gg = dn * vec_ref[0:1]
    low = (rstd_ref[:, :1] * (gg - row_mean(gg) - xhat * row_mean(gg * xhat))).astype(BF16)
    dlow_ref[...] = low

    @pl.when(pl.program_id(0) == 0)
    def _():
        sums_ref[...] = jnp.zeros(sums_ref.shape, F32)

    sums_ref[0:1] += jnp.sum(dn * xhat, axis=0, keepdims=True)
    sums_ref[1:2] += jnp.sum(dn, axis=0, keepdims=True)
    sums_ref[2:3] += jnp.sum(low.astype(F32), axis=0, keepdims=True)
    for w, m in zip(weights, mixes):
        m[...] = nt(low, w[...]).astype(BF16)


def norm_bwd(dns, xhat, rstd, vec, weights, deps=()):
    rows, d = xhat.shape
    parts, terms = len(weights), len(dns)
    row = lambda n: pl.BlockSpec((RB, n), lambda i, *_: (i, 0))
    return call(
        partial(norm_bwd_kernel, parts, terms),
        (xhat, rstd, vec, *weights, *dns),
        deps=deps,
        grid=(rows // RB,),
        in_specs=[row(d), row(128), whole(vec.shape)] + [whole(w.shape) for w in weights] + [row(d)] * terms,
        out_specs=[row(d), whole((8, d))] + [row(w.shape[0]) for w in weights],
        out_shape=[sds((rows, d), BF16), sds((8, d), F32)] + [sds((rows, w.shape[0]), BF16) for w in weights],
        cost_estimate=cost(2 * rows * d * d, 14 * rows * d + 2 * d * d),
        name="norm_bwd",
    )


def grad_tn_kernel(split, lefts, count, core_ref, *refs):
    left_refs, rights, refs = refs[:lefts], refs[lefts:lefts + count], refs[lefts + count:]
    if split:
        keep_ref, send_ref, done_ref, lt_scr, tmp_scr = refs
    else:
        keep_ref, done_ref, lt_scr, tmp_scr = refs
        send_ref = None
    off = 0
    for left in left_refs:
        cols = slice(off, off + left.shape[0])
        put_transposed(lt_scr.at[:, cols], tmp_scr.at[:, cols], left[...], core_ref[0] if split else None)
        off += left.shape[0]
    done_ref[...] = jnp.zeros(done_ref.shape, F32)
    width = rights[0].shape[1]
    for c, right in enumerate(rights):
        cols = slice(c * width, (c + 1) * width)
        put_grad(keep_ref.at[:, cols], None if send_ref is None else send_ref.at[:, cols], lt_scr.at[:, :right.shape[0]], right[...])


def grad_tn(core, lefts, rights, deps=()):
    rows, d = sum(a.shape[0] for a in lefts), lefts[0].shape[1]
    width = rights[0].shape[1]
    n = width * len(rights)
    split = core is not None
    gshape = [sds((d // 2, n), BF16)] * 2 if split else [sds((d, n), BF16)]
    return call(
        partial(grad_tn_kernel, split, len(lefts), len(rights)),
        (*lefts, *rights),
        prefetch=(core if split else jnp.zeros((1,), jnp.int32),),
        deps=deps,
        grid=(1,),
        in_specs=[whole(a.shape) for a in (*lefts, *rights)],
        out_specs=[whole(a.shape) for a in gshape] + [whole((8, 128))],
        scratch=[pltpu.VMEM((d, rows), BF16), pltpu.VMEM((d, rows), BF16)],
        out_shape=gshape + [sds((8, 128), F32)],
        cost_estimate=cost(2 * rows * d * n, 2 * (rows * d + rows * n + d * n)),
        name="grad_tn",
    )


def in_grad_kernel(n, has_base, *refs):
    if has_base:
        base_ref, refs = refs[0], refs[1:]
    grads, weights, out_ref = refs[:n], refs[n:2 * n], refs[2 * n]
    acc = base_ref[...].astype(F32) if has_base else jnp.zeros(out_ref.shape, F32)
    for g, w in zip(grads, weights):
        acc = acc + nt(g[...], w[...])
    out_ref[...] = acc.astype(out_ref.dtype)


def in_grad(base, grads, weights, start, rows, deps=()):
    d = weights[0][0].shape[1]
    n = len(grads)
    first = start // RB
    row = lambda m: pl.BlockSpec((RB, m), lambda i, *_: (i + first, 0))
    wspec = lambda w, c: pl.BlockSpec((None, d, w.shape[2]), lambda i, *_: (c, 0, 0))
    own = pl.BlockSpec((RB, d), lambda i, *_: (i, 0))
    width = sum(g.shape[1] for g in grads)
    return call(
        partial(in_grad_kernel, n, base is not None),
        (*([base] if base is not None else []), *grads, *[w for w, _ in weights]),
        deps=deps,
        grid=(rows // RB,),
        in_specs=([own] if base is not None else []) + [row(g.shape[1]) for g in grads] + [wspec(w, c) for w, c in weights],
        out_specs=own,
        out_shape=sds((rows, d), BF16),
        cost_estimate=cost(2 * rows * d * width, 6 * rows * d + 2 * rows * width + 2 * d * width),
        name="in_grad",
    )


class Grid:
    axes = ("dp", "mp")

    def __init__(self):
        i = lax.axis_index("dp")
        self.y = lax.axis_index("mp")
        self.z, self.x, self.c = i // 4, (i // 2) % 2, i % 2
        self.all = [(z, x, c, y) for z in range(4) for x in range(2) for c in range(2) for y in range(2)]

    def permute(self, a, move):
        num = lambda z, x, c, y: ((z * 2 + x) * 2 + c) * 2 + y
        return lax.ppermute(a, self.axes, [(num(*p), num(*move(*p))) for p in self.all])

    def over_y(self, a):
        return self.permute(a, lambda z, x, c, y: (z, x, c, 1 - y))

    def over_x(self, a):
        return self.permute(a, lambda z, x, c, y: (z, 1 - x, c, y))

    def over_c(self, a):
        return self.permute(a, lambda z, x, c, y: (z, x, 1 - c, y))

    def over_zpair(self, a):
        return self.permute(a, lambda z, x, c, y: (z ^ 1, x, c, y))

    def shift_z(self, a, k):
        return self.permute(a, lambda z, x, c, y: ((z + k) % 4, x, c, y))


def place_kernel(moves, bits_ref, *refs):
    for src, dst in moves(bits_ref, refs):
        dst[...] = src[...]


def place(moves, bits, args, out_shape):
    return call(
        partial(place_kernel, moves),
        args,
        prefetch=(jnp.stack(bits).astype(jnp.int32),),
        grid=(1,),
        in_specs=[whole(a.shape) for a in args],
        out_specs=[whole(o.shape) for o in out_shape],
        out_shape=out_shape,
        cost_estimate=cost(0, 4 * sum(math.prod(o.shape) for o in out_shape)),
        name="place",
    )


def join(pairs, bits):
    n = len(pairs)

    def moves(bits_ref, refs):
        for i in range(n):
            rows = refs[2 * i].shape[0]
            for k in range(2):
                bit = bits_ref[i] if k == 0 else 1 - bits_ref[i]
                yield refs[2 * i + k], refs[2 * n + i].at[pl.ds(pl.multiple_of(bit * rows, rows), rows), :]

    outs = [sds((2 * a.shape[0], a.shape[1]), a.dtype) for a, _ in pairs]
    return place(moves, bits, [a for p in pairs for a in p], outs)


class Fetch:
    def __init__(self, grid, w, x_first, cut):
        self.grid, self.x_first = grid, x_first
        self.zbit = grid.z % 2
        pair = (self.zbit * 2 + grid.x) if x_first else (grid.x * 2 + self.zbit)
        self.cut = lambda *deps: cut(after(w, *deps), grid.c, pair)

    def prepare(self, *deps):
        self.op = self.cut(*deps)
        return self.op

    def send_y(self, *deps):
        self.op = after(self.op, *deps)
        self.got = self.grid.over_y(self.op)
        return self.op

    def send(self, by_x):
        self.bit = self.grid.x if by_x else self.zbit
        self.got = self.grid.over_x(self.op) if by_x else self.grid.over_zpair(self.op)
        return self.op

    def first(self, token):
        self.op = after(self.got, token)
        return self.send(self.x_first)

    @staticmethod
    def joined(fetches, token):
        parts = join([(f.op, after(f.got, token)) for f in fetches], [f.bit for f in fetches])
        for f, part in zip(fetches, parts):
            f.op = part

    @staticmethod
    def second(fetches, token):
        Fetch.joined(fetches, token)
        return [f.send(not f.x_first) for f in fetches]

    @staticmethod
    def third(fetches, token):
        Fetch.joined(fetches, token)
        for f in fetches:
            f.got = f.grid.over_c(f.op)
        return [f.op for f in fetches]

    def last(self, token):
        return after(self.got, token)


def at(a, axis, i):
    return lax.dynamic_index_in_dim(a, i, axis, keepdims=False)


class Reduce:
    def __init__(self, grid, own_a=None, oth_a=None, own_b=None, oth_b=None):
        self.grid, self.waiting = grid, {}
        self.own_a, self.oth_a, self.own_b, self.oth_b = own_a, oth_a, own_b, oth_b

    def view(self, a):
        return a.reshape(4, 2, a.shape[0] // 8, a.shape[1])

    def half(self, a, mine):
        g = self.grid
        return at(self.view(a), 1, g.x if mine else 1 - g.x).astype(F32)

    def cores(self, name, keep, send):
        self.waiting[name] = self.grid.over_c(send)
        setattr(self, "keep_" + "_".join(name), keep)
        return send

    def take(self, token):
        for name, got in self.waiting.items():
            got = [after(a, token) for a in got] if isinstance(got, list) else after(got, token)
            if isinstance(name, tuple):
                if not name[0].startswith("x_"):
                    got = (getattr(self, "keep_" + "_".join(name)).astype(F32) + got.astype(F32)).astype(BF16)
                width = got.shape[-1] // len(name)
                for i, n in enumerate(name):
                    setattr(self, n, got[..., i * width:(i + 1) * width])
            else:
                setattr(self, name, got)
        taken, self.waiting = [getattr(self, n) for name in self.waiting for n in ((name,) if isinstance(name, str) else name)], {}
        return [a for t in taken for a in (t if isinstance(t, list) else [t])]

    def a_over_y(self):
        self.waiting["back_a"] = self.grid.over_y(self.oth_a)
        return self.oth_a

    def a_over_x(self):
        op = (self.half(self.own_a, False) + self.half(self.back_a, False)).astype(BF16)
        self.waiting["x_a"] = self.grid.over_x(op)
        return op

    def b_over_x(self, which):
        op = jnp.concatenate([self.half(getattr(self, n), False).astype(BF16) for n in which], axis=-1)
        self.waiting[tuple("x_" + n for n in which)] = self.grid.over_x(op)
        return op

    def b_over_y(self):
        op = (self.half(self.oth_b, True) + self.x_oth_b.astype(F32)).astype(BF16)
        self.waiting["back_b"] = self.grid.over_y(op)
        return op

    def half_a(self):
        return (self.half(self.own_a, True) + self.half(self.back_a, True) + self.x_a.astype(F32)).astype(BF16)

    def over_z(self, *more):
        g = self.grid
        b = self.half(self.own_b, True) + self.x_own_b.astype(F32) + self.back_b.astype(F32)
        self.kept = jnp.concatenate([self.half_a(), b.astype(BF16), *[m.half_a() for m in more]], axis=2)
        self.kept = lax.optimization_barrier(self.kept)
        ops = [at(self.kept, 0, (g.z + k) % 4) for k in (1, 2, 3)]
        self.waiting["z_got"] = [g.shift_z(op, k) for k, op in zip((1, 2, 3), ops)]
        return ops

    def total(self):
        a, b, c = [p.astype(F32) for p in self.z_got]
        return (at(self.kept, 0, self.grid.z).astype(F32) + a) + (b + c)

    def ends(self):
        self.all = self.total().reshape(2, 64, -1)
        op = at(self.all, 0, 1 - self.grid.c).astype(BF16)
        self.waiting["end"] = self.grid.over_c(op)
        return op

    def result(self):
        mine, got = at(self.all, 0, self.grid.c), self.end.astype(F32)
        c = self.grid.c
        return jnp.concatenate([jnp.where(c == 0, mine, got), jnp.where(c == 0, got, mine)], axis=1)


class Small:
    def __init__(self, grid):
        self.grid = grid

    def send_y(self, oth):
        self.got = self.grid.over_y(oth)
        return oth

    def send_c(self, own, token):
        self.value = own + after(self.got, token)
        self.got = self.grid.over_c(self.value)
        return self.value

    def send_x(self, token):
        self.value = self.value + after(self.got, token)
        self.got = self.grid.over_x(self.value)
        return self.value

    def send_z(self, token):
        self.value = self.value + after(self.got, token)
        self.got = [self.grid.shift_z(self.value, k) for k in (1, 2, 3)]
        return self.value

    def total(self, token):
        z = self.grid.z
        ring = jnp.stack([self.value, *[after(g, token) for g in self.got]])
        terms = [at(ring, 0, (z - s) % 4) for s in range(4)]
        return (terms[0] + terms[1]) + (terms[2] + terms[3])


def time_embed(step, d):
    half = d // 2
    frequency = jnp.exp(-math.log(10000.0) * jnp.arange(half, dtype=F32) / half)
    angles = step.astype(F32) * frequency[None, :]
    return jnp.concatenate([jnp.sin(angles), jnp.cos(angles)], axis=-1)


def block_lists(seg_own, seg_halo, rows):
    q = seg_own.reshape(-1, BQ)
    keys = jnp.concatenate([seg_own, seg_halo]).reshape(-1, BK)
    need = (keys[None, :, 0] <= q[:, None, -1]) & (keys[None, :, -1] >= q[:, None, 0])
    need = need.astype(jnp.int32)
    nkb = keys.shape[0]
    before = jnp.sum(need[:, None, :] * (jnp.arange(nkb)[None, None, :] < jnp.arange(nkb)[None, :, None]), axis=2)
    slot = jnp.arange(nkb)[None, :, None]
    pick = need[:, None, :] * (before[:, None, :] == slot)
    lst = jnp.sum(pick * jnp.arange(nkb)[None, None, :], axis=2)
    return jnp.sum(need, axis=1).astype(jnp.int32), lst.astype(jnp.int32).reshape(-1)


def finish(output, grad_input, grad_qkv, head_bias_sum, grad_out, grad_up, up_bias_sum, grad_down, grad_vectors):
    grad_qkv = grad_qkv.reshape(grad_qkv.shape[0], 3, -1).transpose(1, 0, 2)
    return (
        output,
        grad_input,
        grad_qkv,
        head_bias_sum,
        grad_out.T,
        grad_up,
        up_bias_sum,
        grad_down.T,
        grad_vectors,
    )


def per_device_fast(
    tokens_in,
    timesteps,
    segment_ids,
    padding,
    qkv_weight,
    head_bias,
    out_weight,
    up_weight,
    up_bias,
    down_weight,
    vectors,
    cotangent,
):
    rows, d = tokens_in.shape
    assert timesteps.shape[0] == 1
    LIMITED[0] = True
    grid = Grid()
    me, halo = grid.y, MAXDOC
    core = grid.c.reshape(1).astype(jnp.int32)
    own_start = me * rows
    sub = up_weight.shape[1] // 2
    width = qkv_weight.shape[2]
    by_rows = lambda a, c, q: lax.dynamic_slice_in_dim(a, (c * 4 + q) * (a.shape[0] // 8), a.shape[0] // 8, 0)
    by_cols = lambda a, c, q: lax.dynamic_slice(a, (q * (a.shape[0] // 4), c * sub), (a.shape[0] // 4, sub))
    flat_qkv = qkv_weight.reshape(3 * d, width)

    def outer(a, c, q):
        o = by_rows(out_weight, c, q)
        return jnp.concatenate([by_rows(a, c, q), o[:, :width], o[:, width:]], axis=0)

    def split_outer(mine, theirs):
        n, m = 3 * d // 8, out_weight.shape[0] // 8
        rows = n + 2 * m

        def moves(bits_ref, refs):
            for k in range(2):
                c = bits_ref[0] if k == 0 else 1 - bits_ref[0]
                for i in range(4):
                    at_row = lambda r: pl.ds(pl.multiple_of((c * 4 + i) * r, r), r)
                    yield refs[k].at[i * rows:i * rows + n, :], refs[2].at[at_row(n), :]
                    for j in range(2):
                        o = i * rows + n + j * m
                        yield refs[k].at[o:o + m, :], refs[3].at[at_row(m), j * width:(j + 1) * width]

        qkv, out = place(moves, [grid.c], [mine, theirs], [sds((3 * d, width), BF16), sds(out_weight.shape, BF16)])
        return qkv.reshape(qkv_weight.shape), out

    fq = Fetch(grid, flat_qkv, False, outer)
    fu = Fetch(grid, up_weight, False, by_cols)
    fd = Fetch(grid, down_weight, True, by_rows)
    small_w = jnp.concatenate([head_bias.reshape(-1), up_bias])
    small_o = grid.over_y(small_w)
    fq.prepare()
    begin = [fq.send_y(), small_w]

    emb = time_embed(timesteps[:, None], d)
    seg, pad = segment_ids[0], padding[0]
    seg_own = lax.dynamic_slice_in_dim(seg, own_start, rows)
    pad_own = lax.dynamic_slice_in_dim(pad, own_start, rows)
    halo_start = jnp.where(me == 0, rows, own_start - halo)
    seg_halo = lax.dynamic_slice_in_dim(seg, halo_start, halo)
    pad_halo = lax.dynamic_slice_in_dim(pad, halo_start, halo)
    code = jnp.concatenate([jnp.where(pad_own == 0, seg_own, -1), jnp.where(pad_halo == 0, seg_halo, -1)])
    cnt, lst = block_lists(seg_own, seg_halo, rows)
    nkb = (rows + halo) // BK
    segq_row, code_col = seg_own[None, :], code[:, None]
    nb = head_bias.size

    far_blocks = (rows - halo) // BQ
    far = jnp.where(me == 0, 0, rows // BQ - far_blocks).reshape(1).astype(jnp.int32)
    near = jnp.where(me == 0, far_blocks, 0).reshape(1).astype(jnp.int32)
    zero = jnp.zeros((1,), jnp.int32)
    x_own, q0, k0, v0 = qkv_own(tokens_in, emb, qkv_weight, head_bias, deps=begin)
    small_o = after(small_o, k0)
    ops = [fq.first(k0), small_o]
    edge = jnp.where(me == 0, rows - halo, 0)
    halo_op = lax.dynamic_slice_in_dim(after(tokens_in, ops[0]), edge, halo, 0)
    halo_tok = grid.over_y(halo_op)
    part = attn_fwd(far, far_blocks, cnt, lst, nkb, q0, [k0], [v0], segq_row, code_col, deps=[*ops, halo_op])
    ops = [*Fetch.second([fq], part[1]), fu.prepare(part[1]), fd.prepare(part[1])]
    x_halo, kh0, vh0 = kv_halo(after(halo_tok, part[1]), emb, qkv_weight, head_bias, deps=ops)
    ops = [fu.send_y(kh0), fd.send_y(kh0)]
    kv0 = ([k0, kh0], [v0, vh0], segq_row, code_col)
    part = attn_fwd(near, 1, cnt, lst, nkb, q0, *kv0, into=part, deps=ops)
    ops = Fetch.third([fq], part[1])
    o0, lse0 = attn_fwd(near + 1, rows // BQ - far_blocks - 1, cnt, lst, nkb, q0, *kv0, into=part, deps=ops)
    hb_o, up_b_o = small_o[:nb].reshape(head_bias.shape), small_o[nb:].reshape(1, -1)
    qkv_o, out_o = split_outer(fq.op, fq.last(lse0))
    out_ws = [out_weight, out_o]
    _, q1, k1, v1 = qkv_own(tokens_in, emb, qkv_o, hb_o)
    _, kh1, vh1 = kv_halo(halo_tok, emb, qkv_o, hb_o, deps=[q1])
    ops = [fu.first(kh1), fd.first(kh1)]
    o1, lse1 = attn_fwd(zero, rows // BQ, cnt, lst, nkb, q1, [k1, kh1], [v1, vh1], segq_row, code_col, deps=ops)
    ops = Fetch.second([fu, fd], lse1)
    xhat1, normed, rstd1 = out_norm(tokens_in, emb, vectors, [o0, o1], out_ws, deps=ops)
    up_b = up_bias.reshape(1, -1)
    (a0, b0), (ga0, gb0) = ffn_up(core, normed, [(up_weight, 0, up_b, 0), (up_weight, 1, up_b, 1)], sub)
    ops = Fetch.third([fu, fd], ga0)
    b0_got, normed_got = grid.over_c(b0), grid.over_c(normed)
    (a1,), (ga1,) = ffn_up(core, normed, [(fu.op, None, up_b_o, 0)], sub, deps=ops)
    up_b1, down_b1 = fu.last(ga1), fd.last(ga1)
    (b1,), (gb1,) = ffn_up(core, normed, [(up_b1, None, up_b_o, 1)], sub, deps=[ga1])
    b1_got = grid.over_c(b1)
    output, d_down, sums2 = ffn_down(
        core, normed, cotangent, vectors, [a0, b0, a1, b1], [(down_weight, 0), (down_weight, 1), (fd.op, None), (down_b1, None)]
    )

    d_got = grid.over_c(d_down)
    dn1, (ua1, ub1), us1 = ffn_dup(core, d_down, [(fu.op, None, fd.op, None, ga1), (up_b1, None, down_b1, None, gb1)], sub)
    ub1_got = grid.over_c(ub1)
    gd1, gd0 = wide_grad([d_down, after(d_got, ua1)], [(a1, after(b1_got, d_down)), (a0, after(b0_got, d_down))], deps=[ua1])
    rd = Reduce(grid, gd0[0], gd1[0], gd0[1], gd1[1])
    both = ("own_b", "oth_b")
    ops = [rd.a_over_y(), rd.b_over_x(both)]
    dn0, (ua0, ub0), us0 = ffn_dup(core, d_down, [(up_weight, 0, down_weight, 0, ga0), (up_weight, 1, down_weight, 1, gb0)], sub, deps=ops)
    ub0_got = grid.over_c(ub0)
    got = rd.take(dn0)
    d_attn, sums1, dm0, dm1 = norm_bwd([d_down, dn1, dn0], xhat1, rstd1, vectors, out_ws)
    ops = [rd.a_over_x(), rd.b_over_y(), *got]
    *og, os = grad_tn(core, [d_attn], [o0, o1], deps=[sums1, *ops])
    ro = Reduce(grid)
    ops = [ro.cores(("own_a", "oth_a"), *og)]
    gu1, gu0 = wide_grad([normed, after(normed_got, sums1)], [(ua1, after(ub1_got, sums1)), (ua0, after(ub0_got, sums1))], deps=ops)
    ru = Reduce(grid, gu0[0], gu1[0], gu0[1], gu1[1])
    got = rd.take(gu0[1]) + ro.take(gu0[1])
    ops = [*rd.over_z(), ru.a_over_y(), ru.b_over_x(both), *got]
    *dqkv1, hs1 = attn_bwd(cnt, lst, nkb, q1, [k1, kh1], [v1, vh1], dm1, o1, lse1, segq_row, code_col, deps=ops)
    got = ru.take(dqkv1[0]) + rd.take(dqkv1[0])
    ops = [ru.a_over_x(), ru.b_over_y(), *got]
    rq = Reduce(grid)
    *qg1, gt1 = grad_tn(core, [x_own, x_halo], dqkv1, deps=ops)
    got = []
    rq.cores(("oth_a", "oth_b"), *qg1)
    got += rq.take(gt1)
    vec6 = jnp.concatenate([sums1[:2], sums2[:2], sums1[2:3], sums2[2:3]], axis=0)
    up_sum = lambda us: jnp.where(grid.c == 0, jnp.concatenate(us, axis=0), jnp.concatenate(us[::-1], axis=0))
    head_sum = lambda hs: hs.reshape(1, -1)
    small_sums = lambda us, hs: jnp.concatenate([vec6, up_sum(us), head_sum(hs)], axis=0)
    small = Small(grid)
    ops = [rq.a_over_y(), rq.b_over_x(("oth_b",)), ro.a_over_y(), small.send_y(small_sums(us1, hs1)), *got]
    *dqkv0, hs0 = attn_bwd(cnt, lst, nkb, q0, [k0, kh0], [v0, vh0], dm0, o0, lse0, segq_row, code_col, deps=ops)
    got = rq.take(dqkv0[0]) + ro.take(dqkv0[0]) + ru.take(dqkv0[0])
    ops = [rq.b_over_y(), ro.a_over_x(), *ru.over_z(), small.send_c(small_sums(us0, hs0), hs0), *got]
    *qg0, gt0 = grad_tn(core, [x_own, x_halo], dqkv0, deps=ops)
    got = rq.take(gt0) + ro.take(gt0)
    ops = [rq.cores(("own_a", "own_b"), *qg0), small.send_x(gt0), *got]
    pairs = [(g[c], w, c) for g, w in ((dqkv0, qkv_weight), (dqkv1, qkv_o)) for c in range(3)]
    kv_pairs = [(g, (w, c)) for g, w, c in pairs if c]
    halo_grad = in_grad(None, [g for g, _ in kv_pairs], [w for _, w in kv_pairs], rows, halo, deps=ops)
    got = rq.take(halo_grad) + ru.take(gt0)
    back = grid.over_y(halo_grad)
    ops = [rq.a_over_x(), rq.b_over_x(("own_b",)), small.send_z(halo_grad), halo_grad, *got]
    own_grad = in_grad(d_attn, [g for g, _, _ in pairs], [(w, c) for _, w, c in pairs], 0, rows, deps=ops)
    rq.take(own_grad)
    z_ops = rq.over_z(ro)
    token = z_ops[0]
    for r in (rd, ru):
        r.z_got = [after(a, token) for a in r.z_got]
        r.ends()
        r.take(token)
    near_rows = (jnp.arange(rows // halo) == 1 - me)[:, None, None]
    own_grad, back = after(own_grad, *z_ops), after(back, *z_ops).astype(F32)
    grad_input = (own_grad.reshape(rows // halo, halo, d).astype(F32) + jnp.where(near_rows, back[None], 0.0)).astype(BF16).reshape(rows, d)
    small = small.total(token)
    rq.take(token)
    total = rq.total()
    qkv_cols = 3 * width
    return finish(
        output, grad_input, total[:, :qkv_cols], small[8:].reshape(2, -1), total[:, qkv_cols:], ru.result(),
        small[6:8].reshape(-1), rd.result(), small[:6],
    )


def per_device(
    mp_size,
    tokens_in,
    timesteps,
    segment_ids,
    padding,
    qkv_weight,
    head_bias,
    out_weight,
    up_weight,
    up_bias,
    down_weight,
    vectors,
    cotangent,
):
    rows, d = tokens_in.shape
    assert timesteps.shape[0] == 1
    LIMITED[0] = False
    me = lax.axis_index("mp")
    own_start = me * rows
    emb = time_embed(timesteps[:, None], d)
    seg, pad = segment_ids[0], padding[0]
    seg_own = lax.dynamic_slice_in_dim(seg, own_start, rows)
    pad_own = lax.dynamic_slice_in_dim(pad, own_start, rows)
    halo_tok = lax.all_gather(tokens_in, "mp", axis=0, tiled=True)
    place = jnp.arange(SEQ, dtype=jnp.int32)
    pad_halo = jnp.where((place >= own_start) & (place < own_start + rows), 1, pad)
    code = jnp.concatenate([jnp.where(pad_own == 0, seg_own, -1), jnp.where(pad_halo == 0, seg, -1)])
    cnt, lst = block_lists(seg_own, seg, rows)
    nkb = (rows + SEQ) // BK
    segq_row, code_col = seg_own[None, :], code[:, None]
    gather = lambda a, axis: lax.all_gather(a, "mp", axis=axis, tiled=True)
    qkv_w, out_w, up_w, down_w = gather(qkv_weight, 2), gather(out_weight, 0), gather(up_weight, 1), gather(down_weight, 0)
    hb, up_b = gather(head_bias, 1), gather(up_bias, 0).reshape(1, -1)

    x_own, q, k, v = qkv_own(tokens_in, emb, qkv_w, hb)
    x_halo, kh, vh = kv_halo(halo_tok, emb, qkv_w, hb)
    k, v = [k, kh], [v, vh]
    o, lse = attn_fwd(jnp.zeros((1,), jnp.int32), rows // BQ, cnt, lst, nkb, q, k, v, segq_row, code_col)
    xhat1, normed, rstd1 = out_norm(tokens_in, emb, vectors, [o], [out_w])
    core, hidden = jnp.zeros((1,), jnp.int32), up_w.shape[1]
    acts, gps = ffn_up(core, normed, [(up_w, None, up_b, None)], hidden)
    output, d_down, sums2 = ffn_down(core, normed, cotangent, vectors, acts, [(down_w, None)])

    dn, dups, (up_sum,) = ffn_dup(core, d_down, [(up_w, None, down_w, None, gps[0])], hidden)
    grad_up = jnp.concatenate(wide_grad([normed], [dups])[0], axis=1)
    grad_down = jnp.concatenate(wide_grad([d_down], [acts])[0], axis=1)
    d_attn, sums1, d_mixed = norm_bwd([d_down, dn], xhat1, rstd1, vectors, [out_w])
    grad_out, _ = grad_tn(None, [d_attn], [o])
    *d_qkv, head_sum = attn_bwd(cnt, lst, nkb, q, k, v, d_mixed, o, lse, segq_row, code_col)
    grad_qkv, _ = grad_tn(None, [x_own, x_halo], d_qkv)
    halo_grad = in_grad(None, d_qkv[1:], [(qkv_w, 1), (qkv_w, 2)], rows, SEQ)
    own_grad = in_grad(d_attn, d_qkv, [(qkv_w, c) for c in range(3)], 0, rows)
    back = lax.psum_scatter(halo_grad, "mp", scatter_dimension=0, tiled=True)
    grad_input = (own_grad.astype(F32) + back.astype(F32)).astype(BF16)

    packed = [sums1[:2], sums2[:2], sums1[2:3], sums2[2:3], head_sum, up_sum.reshape(-1, d)]
    packed = lax.psum(jnp.concatenate(packed, axis=0), ("dp", "mp"))
    local = head_bias.shape[1]
    head_bias_sum = lax.dynamic_slice_in_dim(packed[6:8], me * local, local, 1)
    local = up_bias.shape[0]
    up_bias_sum = lax.dynamic_slice_in_dim(packed[8:].reshape(-1), me * local, local, 0)

    def scatter(g, groups):
        n = g.shape[1] // groups // mp_size
        g = lax.psum_scatter(g, "dp", scatter_dimension=0, tiled=True)
        g = g.reshape(-1, groups, mp_size, n).transpose(2, 0, 1, 3)
        return lax.psum_scatter(g, "mp", scatter_dimension=0, tiled=False).astype(F32).reshape(-1, groups * n)

    return finish(
        output,
        grad_input,
        scatter(grad_qkv, 3),
        head_bias_sum,
        scatter(grad_out, 1),
        scatter(grad_up, 1),
        up_bias_sum,
        scatter(grad_down, 1),
        packed[:6],
    )


def solution(mesh):
    fast = dict(mesh.shape) == {"dp": 16, "mp": 2}
    return jax.shard_map(
        per_device_fast if fast else partial(per_device, mesh.shape["mp"]),
        mesh=mesh,
        in_specs=(
            P(("dp", "mp"), None),
            P("dp"),
            P("dp", None),
            P("dp", None),
            P(None, None, "mp"),
            P(None, "mp"),
            P("mp", None),
            P(None, "mp"),
            P("mp"),
            P("mp", None),
            P(),
            P(("dp", "mp"), None),
        ),
        out_specs=(
            P(("dp", "mp"), None),
            P(("dp", "mp"), None),
            P(None, "dp", "mp"),
            P(None, "mp"),
            P("mp", "dp"),
            P("dp", "mp"),
            P("mp"),
            P("mp", "dp"),
            P(),
        ),
        check_vma=False,
    )
```
